128 devices in a mesh: ctx: 32 (over y_lo, z, x), ch: 4 (over y_hi, core).
Axes of the slice: x: 4, y: 4 (y_hi: 2, y_lo: 2; y = y_hi * 2 + y_lo), z: 4, core: 2. Of those that a mesh axis runs over, the one named last changes fastest.
Arguments:
- query_gate: bfloat16 [8192, 4096], P('ctx', 'ch'), may hold values from -6 to 6
- gated_value: bfloat16 [8192, 4096], P('ctx', 'ch'), may hold values from -6 to 6
- long_filter: bfloat16 [8192, 4096], P(None, 'ch'), may hold values from -0.0625 to 0.0625
- out_weight: bfloat16 [4096, 4096], P('ch'), may hold values from -0.125 to 0.125
Outputs:
- output: bfloat16 [8192, 4096], P('ctx', 'ch')
The draws below stay inside these ranges and needn't reach their ends.
All inputs are finite; a program needn't handle non-finite values.
Results may differ from the reference program's by a relative error of at most 0.019.
Values may be sent and summed in bfloat16 or wider, within the bound.
No kernel may reach another device: no remote copies, remote signals or barrier semaphores. Data moves between devices by JAX's collectives and lax.ppermute only.
A program may use at most 128 MiB of HBM per device.

```python
import jax
import jax.numpy as jnp
import numpy as np
from jax import lax

WIDTH = 4096
SPAN = 128
SEQUENCE = 8192
N_CTX = 32


def with_spikes(values, own_key, source, target, blocks, factor):
    def block_of(dim):
        return (jnp.arange(values.shape[dim]) // (values.shape[dim] // blocks)).reshape((-1,) + (1,) * (values.ndim - 1 - dim))

    near = jax.random.permutation(own_key, blocks)[block_of(target)]
    second = (block_of(target) + blocks // 2) % blocks
    return jnp.where((block_of(source) == near) | (block_of(source) == second), factor * values, values)


def shard_levels(rng, shape, shards, least, largest):
    factor_of = 1.0
    for dim, shards_of in shards:
        draws = jax.random.uniform(jax.random.fold_in(jax.random.fold_in(rng, 6), dim), (shards_of,), jnp.float32, least / len(shards), largest / len(shards))
        factor_of = factor_of * jnp.repeat(jnp.exp(draws), shape[dim] // shards_of).reshape((-1,) + (1,) * (len(shape) - 1 - dim))
    return factor_of


def noise(own_key, extent, scale, reach, shards=(), dtype=jnp.bfloat16):
    result = scale * jax.random.normal(own_key, extent, jnp.float32)
    if shards:
        result = result * shard_levels(own_key, extent, shards, -0.22, 0.18)
    return jnp.clip(result, -reach, reach).astype(dtype)


def noise_with(stream_key, shape, deviation, most, split, heavy, held_as=jnp.bfloat16):
    entries = deviation * jax.random.normal(stream_key, shape, jnp.float32)
    if split:
        entries = entries * shard_levels(stream_key, shape, split, -0.22, 0.18)
    return jnp.clip(with_spikes(entries, jax.random.fold_in(stream_key, 3), *heavy), -most, most).astype(held_as)


def setup_inputs(seed: int = 0) -> dict:
    arg_keys = jax.random.split(jax.random.key(seed), 5)
    query_gate = noise(arg_keys[0], (SEQUENCE, WIDTH), 1.0, 6.0, ((0, 32), (1, 4)))
    gated_value = noise(arg_keys[1], (SEQUENCE, WIDTH), 1.0, 6.0, ((0, 32), (1, 4)))
    long_filter = noise(arg_keys[2], (SEQUENCE, WIDTH), SEQUENCE ** -0.5, 0.0625, ((1, 4),))
    out_weight = noise_with(arg_keys[3], (WIDTH, WIDTH), WIDTH ** -0.5, 0.125, ((0, 4),), (0, 1, 4, 2.0))
    return {"query_gate": query_gate, "gated_value": gated_value, "long_filter": long_filter, "out_weight": out_weight}


def stored_blocks(count):
    order = []
    for index in range(count):
        order.append(index)
        order.append(2 * count - 1 - index)
    return np.array(order)


def group_convolve(operands):
    values, taps = operands
    length = 2 * SEQUENCE
    spectrum = jnp.fft.rfft(values, n=length, axis=0) * jnp.fft.rfft(taps, n=length, axis=0)
    return jnp.fft.irfft(spectrum, n=length, axis=0)[:SEQUENCE]


def reference(query_gate, gated_value, long_filter, out_weight):
    order = stored_blocks(N_CTX)
    inverse = np.argsort(order)
    blocks = gated_value.astype(jnp.float32).reshape(2 * N_CTX, SPAN, WIDTH)
    sequence_values = blocks[inverse].reshape(SEQUENCE, WIDTH)
    groups = WIDTH // 64
    values = sequence_values.reshape(SEQUENCE, groups, 64).transpose(1, 0, 2)
    taps = long_filter.astype(jnp.float32).reshape(SEQUENCE, groups, 64).transpose(1, 0, 2)
    convolved = lax.map(group_convolve, (values, taps))
    convolved = convolved.astype(jnp.float32).transpose(1, 0, 2).reshape(SEQUENCE, WIDTH)
    convolved = convolved.reshape(2 * N_CTX, SPAN, WIDTH)[order].reshape(SEQUENCE, WIDTH)
    gated_mix = (query_gate.astype(jnp.float32) * convolved).astype(jnp.bfloat16)
    return jnp.dot(gated_mix, out_weight, preferred_element_type=jnp.float32).astype(jnp.bfloat16)
```

```python
import functools

import jax
import jax.numpy as jnp
import numpy as np
from jax import lax
from jax.experimental import pallas as pl
from jax.experimental.pallas import tpu as pltpu
from jax.sharding import PartitionSpec as P

SPAN = 128
BLOCKS = 64
HALF = BLOCKS // 2
LENGTH = SPAN * BLOCKS
GROUP = 32
SUB = 16
F32 = jnp.float32
BF16 = jnp.bfloat16


def tables():
    first = np.arange(BLOCKS)[:, None] + 0.25
    natural = np.arange(BLOCKS)[None, :]
    stored = np.concatenate([np.arange(HALF), BLOCKS - 1 - np.arange(HALF)])[None, :]

    def stage_a(order):
        angle = 2 * np.pi * first * order / BLOCKS
        return np.concatenate([np.cos(angle), -np.sin(angle)], 0)

    def stage_a_back(order):
        angle = (2 * np.pi * first * order / BLOCKS).T
        return np.concatenate([np.cos(angle), -np.sin(angle)], 1) / LENGTH

    twist = 2 * np.pi * first * np.arange(SPAN)[None, :] / LENGTH
    angle = 2 * np.pi * np.arange(SPAN)[:, None] * np.arange(SPAN)[None, :] / SPAN
    cos, sin = np.cos(angle), np.sin(angle)
    forth = np.block([[cos, -sin], [sin, cos]])
    back = np.block([[cos, sin], [-sin, cos]])
    rows = np.arange(HALF * SUB)
    swap = np.zeros((HALF * SUB, HALF * SUB))
    swap[(rows % SUB) * HALF + rows // SUB, rows] = 1.0
    bf = lambda a: jnp.asarray(a.astype(np.float32)).astype(BF16)
    return dict(
        a_filter=bf(stage_a(natural)),
        a_value=bf(stage_a(stored)),
        a_back=bf(stage_a_back(stored)),
        twist=jnp.asarray(np.concatenate([np.cos(twist), -np.sin(twist)], 1).astype(np.float32)),
        forth=bf(forth),
        back=bf(back),
        swap=bf(swap),
        unswap=bf(swap.T),
    )


def dot(left, right):
    return jnp.dot(left, right, preferred_element_type=F32)


def stage_a_rows(swapped, a_table, twist, mid_ref):
    t_re = jnp.concatenate([twist[:, :SPAN]] * 2, 1)
    t_im = jnp.concatenate([twist[:, SPAN:]] * 2, 1)
    for c in range(SUB):
        block = swapped[c * HALF : (c + 1) * HALF, :]
        rows = jnp.concatenate([block[:, : 2 * SPAN], block[:, 2 * SPAN :]], 0)
        spec = dot(a_table, rows)
        re, im = spec[:BLOCKS], spec[BLOCKS:]
        out_re = (re * t_re - im * t_im).astype(BF16)
        out_im = (re * t_im + im * t_re).astype(BF16)
        for g in range(2):
            at = (g * SUB + c) * BLOCKS
            mid_ref[at : at + BLOCKS, :SPAN] = out_re[:, g * SPAN : (g + 1) * SPAN]
            mid_ref[at : at + BLOCKS, SPAN:] = out_im[:, g * SPAN : (g + 1) * SPAN]


CHUNK = 512


def filter_kernel(which, h_ref, a_ref, twist_ref, forth_ref, swap_ref, out_ref, gather_ref, mid_ref):
    offset = (which[0] % 4) * GROUP
    rows = lax.broadcasted_iota(jnp.int32, (GROUP, SPAN), 0)
    lanes = lax.broadcasted_iota(jnp.int32, (GROUP, SPAN), 1)
    pick = jnp.where(lanes == rows + offset, 1.0, 0.0).astype(BF16)
    for a in range(HALF):
        for half in range(2):
            at = (half * HALF + a) * SPAN
            turned = lax.dot_general(
                pick, h_ref[at : at + SPAN, :], (((1,), (1,)), ((), ())), preferred_element_type=F32
            ).astype(BF16)
            for g in range(2):
                lane = (half * 2 + g) * SPAN
                gather_ref[a * SUB : (a + 1) * SUB, lane : lane + SPAN] = turned[g * SUB : (g + 1) * SUB]
    swapped = dot(swap_ref[...], gather_ref[...]).astype(BF16)
    stage_a_rows(swapped, a_ref[...], twist_ref[...], mid_ref)
    for k in range(GROUP * BLOCKS // CHUNK):
        part = slice(k * CHUNK, (k + 1) * CHUNK)
        out_ref[part, :] = dot(mid_ref[part, :], forth_ref[...]).astype(out_ref.dtype)


def conv_kernel(
    x_ref, spec_ref, a_ref, a_back_ref, twist_ref, forth_ref, back_ref, swap_ref, unswap_ref, out_ref, mid_ref, turn_ref
):
    pieces = []
    for half in range(2):
        for g in range(2):
            piece = x_ref[:, g * SUB : (g + 1) * SUB, half * SPAN : (half + 1) * SPAN]
            pieces.append(piece.reshape(HALF * SUB, SPAN))
    swapped = dot(swap_ref[...], jnp.concatenate(pieces, 1)).astype(BF16)
    twist = twist_ref[...]
    stage_a_rows(swapped, a_ref[...], twist, mid_ref)
    t_re = jnp.concatenate([twist[:, :SPAN]] * (CHUNK // BLOCKS), 0)
    t_im = jnp.concatenate([twist[:, SPAN:]] * (CHUNK // BLOCKS), 0)
    for k in range(GROUP * BLOCKS // CHUNK):
        part = slice(k * CHUNK, (k + 1) * CHUNK)
        spec = dot(mid_ref[part, :], forth_ref[...])
        x_re, x_im = spec[:, :SPAN], spec[:, SPAN:]
        h = spec_ref[part, :].astype(F32)
        h_re, h_im = h[:, :SPAN], h[:, SPAN:]
        prod = jnp.concatenate([x_re * h_re - x_im * h_im, x_re * h_im + x_im * h_re], 1).astype(BF16)
        turn = dot(prod, back_ref[...])
        re, im = turn[:, :SPAN], turn[:, SPAN:]
        mid_ref[part, :SPAN] = (re * t_re + im * t_im).astype(BF16)
        mid_ref[part, SPAN:] = (im * t_re - re * t_im).astype(BF16)
    for c in range(SUB):
        sides = []
        for g in range(2):
            at = (g * SUB + c) * BLOCKS
            sides.append(
                jnp.concatenate([mid_ref[at : at + BLOCKS, :SPAN], mid_ref[at : at + BLOCKS, SPAN:]], 0)
            )
        y = dot(a_back_ref[...], jnp.concatenate(sides, 1)).astype(BF16)
        turn_ref[c * HALF : (c + 1) * HALF, : 2 * SPAN] = y[:HALF]
        turn_ref[c * HALF : (c + 1) * HALF, 2 * SPAN :] = y[HALF:]
    result = dot(unswap_ref[...], turn_ref[...]).astype(BF16)
    for half in range(2):
        for g in range(2):
            lane = (half * 2 + g) * SPAN
            out_ref[:, g * SUB : (g + 1) * SUB, half * SPAN : (half + 1) * SPAN] = result[:, lane : lane + SPAN].reshape(
                HALF, SUB, SPAN
            )


def full(shape):
    return pl.BlockSpec(shape, lambda *_: (0,) * len(shape))


def filter_spectrum(which, long_filter, t):
    return pl.pallas_call(
        filter_kernel,
        out_shape=jax.ShapeDtypeStruct((GROUP * BLOCKS, 2 * SPAN), BF16),
        grid_spec=pltpu.PrefetchScalarGridSpec(
            num_scalar_prefetch=1,
            grid=(1,),
            in_specs=[
                pl.BlockSpec((LENGTH, SPAN), lambda i, w: (0, w[0] // 4)),
                full((2 * BLOCKS, BLOCKS)),
                full((BLOCKS, 2 * SPAN)),
                full((2 * SPAN, 2 * SPAN)),
                full((HALF * SUB, HALF * SUB)),
            ],
            out_specs=full((GROUP * BLOCKS, 2 * SPAN)),
            scratch_shapes=[
                pltpu.VMEM((HALF * SUB, 4 * SPAN), BF16),
                pltpu.VMEM((GROUP * BLOCKS, 2 * SPAN), BF16),
            ],
        ),
        compiler_params=pltpu.CompilerParams(vmem_limit_bytes=32 << 20),
        name="filter_spectrum",
    )(which, long_filter, t["a_filter"], t["twist"], t["forth"], t["swap"])


def convolve(x, spec, t):
    return pl.pallas_call(
        conv_kernel,
        out_shape=jax.ShapeDtypeStruct((HALF, GROUP, 2 * SPAN), BF16),
        scratch_shapes=[
            pltpu.VMEM((GROUP * BLOCKS, 2 * SPAN), BF16),
            pltpu.VMEM((HALF * SUB, 4 * SPAN), BF16),
        ],
        compiler_params=pltpu.CompilerParams(vmem_limit_bytes=32 << 20),
        name="convolve",
    )(x, spec, t["a_value"], t["a_back"], t["twist"], t["forth"], t["back"], t["swap"], t["unswap"])


def gate_kernel(y_ref, gate_ref, out_ref):
    turned = jnp.transpose(y_ref[...], (1, 0))
    out_ref[...] = (gate_ref[...].astype(F32) * turned.astype(F32)).astype(BF16)


def gate_mix(y, gate):
    return pl.pallas_call(
        gate_kernel,
        out_shape=jax.ShapeDtypeStruct(gate.shape, BF16),
        compiler_params=pltpu.CompilerParams(vmem_limit_bytes=32 << 20),
        name="gate_mix",
    )(y, gate)


def project_kernel(order, mix_ref, w_ref, out_ref):
    out_ref[0] = dot(mix_ref[...], w_ref[...]).astype(BF16)


def project(order, mix, weight):
    tokens, inner = mix.shape
    chunks = order.shape[0]
    cols = weight.shape[1] // 4
    return pl.pallas_call(
        project_kernel,
        out_shape=jax.ShapeDtypeStruct((chunks, tokens, cols), BF16),
        grid_spec=pltpu.PrefetchScalarGridSpec(
            num_scalar_prefetch=1,
            grid=(chunks,),
            in_specs=[
                pl.BlockSpec((tokens, inner), lambda j, o: (0, 0)),
                pl.BlockSpec((inner, cols), lambda j, o: (0, o[j])),
            ],
            out_specs=pl.BlockSpec((1, tokens, cols), lambda j, o: (j, 0, 0)),
        ),
        compiler_params=pltpu.CompilerParams(vmem_limit_bytes=32 << 20),
        name="project",
    )(order, mix, weight)


CORE_PAIR = [(0, 1), (1, 0), (2, 3), (3, 2)]
CHIP_PAIR = [(0, 2), (2, 0), (1, 3), (3, 1)]


def per_device(query_gate, gated_value, long_filter, out_weight):
    t = tables()
    me = lax.axis_index("ctx")
    mine = lax.axis_index("ch")
    tokens, width = gated_value.shape
    turned = gated_value.T.reshape(HALF, GROUP, tokens)
    x = lax.all_to_all(turned, "ctx", 0, 0, tiled=True)
    spec = filter_spectrum(me.reshape(1), long_filter, t)
    y = convolve(x, spec, t)
    y = lax.all_to_all(y, "ctx", 0, 0, tiled=True).reshape(width, tokens)
    mix = gate_mix(y, query_gate)
    away = project(jnp.stack([mine ^ 3, mine ^ 2]), mix, out_weight)
    home = project(jnp.stack([mine ^ 1, mine]), mix, out_weight)
    away_in = lax.ppermute(away[0], "ch", CORE_PAIR)
    away_sum = (away[1].astype(F32) + away_in.astype(F32)).astype(BF16)
    far = lax.ppermute(away_sum, "ch", CHIP_PAIR)
    near = lax.ppermute(home[0], "ch", CORE_PAIR)
    return (home[1].astype(F32) + near.astype(F32) + far.astype(F32)).astype(BF16)


def solution(mesh):
    placed = (P("ctx", "ch"), P("ctx", "ch"), P(None, "ch"), P("ch", None))
    return jax.shard_map(
        per_device, mesh=mesh, in_specs=placed, out_specs=P("ctx", "ch"), check_vma=False
    )
```

```python
import functools

import jax
import jax.numpy as jnp
import numpy as np
from jax import lax
from jax.experimental import pallas as pl
from jax.experimental.pallas import tpu as pltpu
from jax.sharding import PartitionSpec as P

SPAN = 128
BLOCKS = 64
HALF = BLOCKS // 2
LENGTH = SPAN * BLOCKS
GROUP = 32
SUB = 16
F32 = jnp.float32
BF16 = jnp.bfloat16


def tables():
    first = np.arange(BLOCKS)[:, None] + 0.25
    natural = np.arange(BLOCKS)[None, :]
    stored = np.concatenate([np.arange(HALF), BLOCKS - 1 - np.arange(HALF)])[None, :]

    def stage_a(order):
        angle = 2 * np.pi * first * order / BLOCKS
        return np.concatenate([np.cos(angle), -np.sin(angle)], 0)

    def stage_a_back(order):
        angle = (2 * np.pi * first * order / BLOCKS).T
        return np.concatenate([np.cos(angle), -np.sin(angle)], 1) / LENGTH

    twist = 2 * np.pi * first * np.arange(SPAN)[None, :] / LENGTH
    angle = 2 * np.pi * np.arange(SPAN)[:, None] * np.arange(SPAN)[None, :] / SPAN
    cos, sin = np.cos(angle), np.sin(angle)
    forth = np.block([[cos, -sin], [sin, cos]])
    back = np.block([[cos, sin], [-sin, cos]])
    rows = np.arange(HALF * SUB)
    swap = np.zeros((HALF * SUB, HALF * SUB))
    swap[(rows % SUB) * HALF + rows // SUB, rows] = 1.0
    bf = lambda a: jnp.asarray(a.astype(np.float32)).astype(BF16)
    return dict(
        a_filter=bf(stage_a(natural)),
        a_value=bf(stage_a(stored)),
        a_back=bf(stage_a_back(stored)),
        twist=jnp.asarray(np.concatenate([np.cos(twist), -np.sin(twist)], 1).astype(np.float32)),
        forth=bf(forth),
        back=bf(back),
        swap=bf(swap),
        unswap=bf(swap.T),
    )


def dot(left, right):
    return jnp.dot(left, right, preferred_element_type=F32)


def stage_a_rows(swapped, a_table, twist, mid_ref):
    t_re = jnp.concatenate([twist[:, :SPAN]] * 2, 1)
    t_im = jnp.concatenate([twist[:, SPAN:]] * 2, 1)
    for c in range(SUB):
        block = swapped[c * HALF : (c + 1) * HALF, :]
        rows = jnp.concatenate([block[:, : 2 * SPAN], block[:, 2 * SPAN :]], 0)
        spec = dot(a_table, rows)
        re, im = spec[:BLOCKS], spec[BLOCKS:]
        out_re = (re * t_re - im * t_im).astype(BF16)
        out_im = (re * t_im + im * t_re).astype(BF16)
        for g in range(2):
            at = (g * SUB + c) * BLOCKS
            mid_ref[at : at + BLOCKS, :SPAN] = out_re[:, g * SPAN : (g + 1) * SPAN]
            mid_ref[at : at + BLOCKS, SPAN:] = out_im[:, g * SPAN : (g + 1) * SPAN]


CHUNK = 512


SLABS = 8


def filter_kernel(
    which, h_hbm, a_hbm, twist_hbm, forth_hbm, swap_hbm, out_ref,
    slab_ref, a_ref, twist_ref, forth_ref, swap_ref, gather_ref, mid_ref, slab_sem, table_sem,
):
    lane_block = pl.multiple_of((which[0] // 4) * SPAN, SPAN)
    piece = LENGTH // SLABS
    slabs = [
        pltpu.make_async_copy(
            h_hbm.at[pl.ds(k * piece, piece), pl.ds(lane_block, SPAN)],
            slab_ref.at[pl.ds(k * piece, piece), :],
            slab_sem.at[k],
        )
        for k in range(SLABS)
    ]
    pairs = [(a_hbm, a_ref), (twist_hbm, twist_ref), (forth_hbm, forth_ref), (swap_hbm, swap_ref)]
    loads = [pltpu.make_async_copy(s, d, table_sem.at[k]) for k, (s, d) in enumerate(pairs)]
    for copy in slabs + loads:
        copy.start()
    offset = (which[0] % 4) * GROUP
    rows = lax.broadcasted_iota(jnp.int32, (GROUP, SPAN), 0)
    lanes = lax.broadcasted_iota(jnp.int32, (GROUP, SPAN), 1)
    pick = jnp.where(lanes == rows + offset, 1.0, 0.0).astype(BF16)
    for block in range(BLOCKS):
        if block % (BLOCKS // SLABS) == 0:
            slabs[block // (BLOCKS // SLABS)].wait()
        half, a = divmod(block, HALF)
        turned = lax.dot_general(
            pick, slab_ref[block * SPAN : (block + 1) * SPAN, :], (((1,), (1,)), ((), ())), preferred_element_type=F32
        ).astype(BF16)
        for g in range(2):
            lane = (half * 2 + g) * SPAN
            gather_ref[a * SUB : (a + 1) * SUB, lane : lane + SPAN] = turned[g * SUB : (g + 1) * SUB]
    for copy in loads:
        copy.wait()
    swapped = dot(swap_ref[...], gather_ref[...]).astype(BF16)
    stage_a_rows(swapped, a_ref[...], twist_ref[...], mid_ref)
    for k in range(GROUP * BLOCKS // CHUNK):
        part = slice(k * CHUNK, (k + 1) * CHUNK)
        out_ref[part, :] = dot(mid_ref[part, :], forth_ref[...]).astype(out_ref.dtype)


def conv_kernel(
    x_ref, spec_ref, a_ref, a_back_ref, twist_ref, forth_ref, back_ref, swap_ref, unswap_ref, out_ref, mid_ref, turn_ref
):
    pieces = []
    for half in range(2):
        for g in range(2):
            piece = x_ref[:, g * SUB : (g + 1) * SUB, half * SPAN : (half + 1) * SPAN]
            pieces.append(piece.reshape(HALF * SUB, SPAN))
    swapped = dot(swap_ref[...], jnp.concatenate(pieces, 1)).astype(BF16)
    twist = twist_ref[...]
    stage_a_rows(swapped, a_ref[...], twist, mid_ref)
    t_re = jnp.concatenate([twist[:, :SPAN]] * (CHUNK // BLOCKS), 0)
    t_im = jnp.concatenate([twist[:, SPAN:]] * (CHUNK // BLOCKS), 0)
    for k in range(GROUP * BLOCKS // CHUNK):
        part = slice(k * CHUNK, (k + 1) * CHUNK)
        spec = dot(mid_ref[part, :], forth_ref[...])
        x_re, x_im = spec[:, :SPAN], spec[:, SPAN:]
        h = spec_ref[part, :].astype(F32)
        h_re, h_im = h[:, :SPAN], h[:, SPAN:]
        prod = jnp.concatenate([x_re * h_re - x_im * h_im, x_re * h_im + x_im * h_re], 1).astype(BF16)
        turn = dot(prod, back_ref[...])
        re, im = turn[:, :SPAN], turn[:, SPAN:]
        mid_ref[part, :SPAN] = (re * t_re + im * t_im).astype(BF16)
        mid_ref[part, SPAN:] = (im * t_re - re * t_im).astype(BF16)
    for c in range(SUB):
        sides = []
        for g in range(2):
            at = (g * SUB + c) * BLOCKS
            sides.append(
                jnp.concatenate([mid_ref[at : at + BLOCKS, :SPAN], mid_ref[at : at + BLOCKS, SPAN:]], 0)
            )
        y = dot(a_back_ref[...], jnp.concatenate(sides, 1)).astype(BF16)
        turn_ref[c * HALF : (c + 1) * HALF, : 2 * SPAN] = y[:HALF]
        turn_ref[c * HALF : (c + 1) * HALF, 2 * SPAN :] = y[HALF:]
    result = dot(unswap_ref[...], turn_ref[...]).astype(BF16)
    for half in range(2):
        for g in range(2):
            lane = (half * 2 + g) * SPAN
            out_ref[:, g * SUB : (g + 1) * SUB, half * SPAN : (half + 1) * SPAN] = result[:, lane : lane + SPAN].reshape(
                HALF, SUB, SPAN
            )


def in_hbm(*arrays):
    return tuple(pltpu.with_memory_space_constraint(a, pltpu.HBM) for a in arrays)


def filter_spectrum(which, long_filter, t):
    return pl.pallas_call(
        filter_kernel,
        out_shape=jax.ShapeDtypeStruct((GROUP * BLOCKS, 2 * SPAN), BF16),
        in_specs=[pl.BlockSpec(memory_space=pltpu.SMEM)] + [pl.BlockSpec(memory_space=pltpu.HBM)] * 5,
        out_specs=pl.BlockSpec(memory_space=pltpu.VMEM),
        scratch_shapes=[
            pltpu.VMEM((LENGTH, SPAN), BF16),
            pltpu.VMEM((2 * BLOCKS, BLOCKS), BF16),
            pltpu.VMEM((BLOCKS, 2 * SPAN), F32),
            pltpu.VMEM((2 * SPAN, 2 * SPAN), BF16),
            pltpu.VMEM((HALF * SUB, HALF * SUB), BF16),
            pltpu.VMEM((HALF * SUB, 4 * SPAN), BF16),
            pltpu.VMEM((GROUP * BLOCKS, 2 * SPAN), BF16),
            pltpu.SemaphoreType.DMA((SLABS,)),
            pltpu.SemaphoreType.DMA((4,)),
        ],
        compiler_params=pltpu.CompilerParams(vmem_limit_bytes=32 << 20),
        name="filter_spectrum",
    )(which, *in_hbm(long_filter, t["a_filter"], t["twist"], t["forth"], t["swap"]))


def convolve(x, spec, t):
    return pl.pallas_call(
        conv_kernel,
        out_shape=jax.ShapeDtypeStruct((HALF, GROUP, 2 * SPAN), BF16),
        scratch_shapes=[
            pltpu.VMEM((GROUP * BLOCKS, 2 * SPAN), BF16),
            pltpu.VMEM((HALF * SUB, 4 * SPAN), BF16),
        ],
        compiler_params=pltpu.CompilerParams(vmem_limit_bytes=32 << 20),
        name="convolve",
    )(x, spec, t["a_value"], t["a_back"], t["twist"], t["forth"], t["back"], t["swap"], t["unswap"])


def turn_kernel(v_hbm, out_ref, in_ref, sem):
    width = v_hbm.shape[1] // 4
    copies = [
        pltpu.make_async_copy(v_hbm.at[:, pl.ds(k * width, width)], in_ref.at[k], sem.at[k]) for k in range(4)
    ]
    for copy in copies:
        copy.start()
    for k in range(4):
        copies[k].wait()
        out_ref[k * width : (k + 1) * width, :] = jnp.transpose(in_ref[k], (1, 0))


def turn(v):
    tokens, width = v.shape
    return pl.pallas_call(
        turn_kernel,
        out_shape=jax.ShapeDtypeStruct((width, tokens), BF16),
        in_specs=[pl.BlockSpec(memory_space=pltpu.HBM)],
        out_specs=pl.BlockSpec(memory_space=pltpu.VMEM),
        scratch_shapes=[pltpu.VMEM((4, tokens, width // 4), BF16), pltpu.SemaphoreType.DMA((4,))],
        compiler_params=pltpu.CompilerParams(vmem_limit_bytes=16 << 20),
        name="turn",
    )(*in_hbm(v))


PARTS = 4


def weight_copies(chunk, w_hbm, w_ref, sem):
    inner, cols = w_ref.shape
    rows = inner // PARTS
    start = pl.multiple_of(chunk * cols, cols)
    return [
        pltpu.make_async_copy(
            w_hbm.at[pl.ds(k * rows, rows), pl.ds(start, cols)], w_ref.at[pl.ds(k * rows, rows), :], sem.at[k]
        )
        for k in range(PARTS)
    ]


def product(mix_ref, w_ref, copies):
    rows = w_ref.shape[0] // PARTS
    total = None
    for k in range(PARTS):
        copies[k].wait()
        part = dot(mix_ref[:, k * rows : (k + 1) * rows], w_ref[k * rows : (k + 1) * rows, :])
        total = part if total is None else total + part
    return total


def gate_kernel(chunks, y_ref, gate_ref, w_hbm, mix_ref, out_ref, w_ref, sem):
    copies = weight_copies(chunks[0], w_hbm, w_ref, sem)
    for copy in copies:
        copy.start()
    turned = jnp.transpose(y_ref[...], (1, 0))
    mix_ref[...] = (gate_ref[...].astype(F32) * turned.astype(F32)).astype(BF16)
    out_ref[...] = product(mix_ref, w_ref, copies).astype(BF16)


def gate_project(chunks, y, gate, w):
    tokens, inner, cols = gate.shape[0], w.shape[0], w.shape[1] // 4
    vmem = pl.BlockSpec(memory_space=pltpu.VMEM)
    return pl.pallas_call(
        gate_kernel,
        out_shape=(jax.ShapeDtypeStruct(gate.shape, BF16), jax.ShapeDtypeStruct((tokens, cols), BF16)),
        in_specs=[pl.BlockSpec(memory_space=pltpu.SMEM), vmem, vmem, pl.BlockSpec(memory_space=pltpu.HBM)],
        out_specs=(vmem, vmem),
        scratch_shapes=[pltpu.VMEM((inner, cols), BF16), pltpu.SemaphoreType.DMA((PARTS,))],
        compiler_params=pltpu.CompilerParams(vmem_limit_bytes=32 << 20),
        name="gate_project",
    )(chunks, y, gate, *in_hbm(w))


def project(chunks, mix, w, dtypes):
    tokens, inner, cols = mix.shape[0], w.shape[0], w.shape[1] // 4
    count = len(dtypes)
    vmem = pl.BlockSpec(memory_space=pltpu.VMEM)

    def kernel(chunks, mix_ref, w_hbm, *refs):
        out_refs, (w_ref, sem) = refs[:count], refs[count:]
        copies = [weight_copies(chunks[j], w_hbm, w_ref.at[j], sem.at[j]) for j in range(count)]
        for copy in sum(copies, []):
            copy.start()
        for j in range(count):
            out_refs[j][...] = product(mix_ref, w_ref.at[j], copies[j]).astype(dtypes[j])

    return pl.pallas_call(
        kernel,
        out_shape=tuple(jax.ShapeDtypeStruct((tokens, cols), d) for d in dtypes),
        in_specs=[pl.BlockSpec(memory_space=pltpu.SMEM), vmem, pl.BlockSpec(memory_space=pltpu.HBM)],
        out_specs=(vmem,) * count,
        scratch_shapes=[pltpu.VMEM((count, inner, cols), BF16), pltpu.SemaphoreType.DMA((count, PARTS))],
        compiler_params=pltpu.CompilerParams(vmem_limit_bytes=32 << 20),
        name="project",
    )(chunks, mix, *in_hbm(w))


CORE_PAIR = [(0, 1), (1, 0), (2, 3), (3, 2)]
CHIP_PAIR = [(0, 2), (2, 0), (1, 3), (3, 1)]


def per_device(query_gate, gated_value, long_filter, out_weight):
    t = tables()
    me = lax.axis_index("ctx")
    mine = lax.axis_index("ch")
    tokens, width = gated_value.shape
    turned = turn(gated_value).reshape(HALF, GROUP, tokens)
    x = lax.all_to_all(turned, "ctx", 0, 0, tiled=True)
    spec = filter_spectrum(me.reshape(1), long_filter, t)
    y = convolve(x, spec, t)
    y = lax.all_to_all(y, "ctx", 0, 0, tiled=True).reshape(width, tokens)
    order = jnp.arange(3, -1, -1, dtype=jnp.int32) ^ mine
    mix, away_pair = gate_project(order[:1], y, query_gate, out_weight)
    away_in = lax.ppermute(away_pair, "ch", CORE_PAIR)
    (away_own,) = project(order[1:2], mix, out_weight, (F32,))
    away_sum = (away_own + away_in.astype(F32)).astype(BF16)
    far = lax.ppermute(away_sum, "ch", CHIP_PAIR)
    home_pair, home_own = project(order[2:], mix, out_weight, (BF16, F32))
    near = lax.ppermute(home_pair, "ch", CORE_PAIR)
    return (home_own + near.astype(F32) + far.astype(F32)).astype(BF16)


def solution(mesh):
    placed = (P("ctx", "ch"), P("ctx", "ch"), P(None, "ch"), P("ch", None))
    return jax.shard_map(
        per_device, mesh=mesh, in_specs=placed, out_specs=P("ctx", "ch"), check_vma=False
    )
```

```python
import functools

import jax
import jax.numpy as jnp
import numpy as np
from jax import lax
from jax.experimental import pallas as pl
from jax.experimental.pallas import tpu as pltpu
from jax.sharding import PartitionSpec as P

SPAN = 128
BLOCKS = 64
HALF = BLOCKS // 2
LENGTH = SPAN * BLOCKS
GROUP = 32
SUB = 16
F32 = jnp.float32
BF16 = jnp.bfloat16


def tables():
    first = np.arange(BLOCKS)[:, None] + 0.25
    natural = np.arange(BLOCKS)[None, :]
    stored = np.concatenate([np.arange(HALF), BLOCKS - 1 - np.arange(HALF)])[None, :]

    def stage_a(order):
        angle = 2 * np.pi * first * order / BLOCKS
        return np.concatenate([np.cos(angle), -np.sin(angle)], 0)

    def stage_a_back(order):
        angle = (2 * np.pi * first * order / BLOCKS).T
        return np.concatenate([np.cos(angle), -np.sin(angle)], 1) / LENGTH

    twist = 2 * np.pi * first * np.arange(SPAN)[None, :] / LENGTH
    angle = 2 * np.pi * np.arange(SPAN)[:, None] * np.arange(SPAN)[None, :] / SPAN
    cos, sin = np.cos(angle), np.sin(angle)
    forth = np.block([[cos, -sin], [sin, cos]])
    back = np.block([[cos, sin], [-sin, cos]])
    rows = np.arange(HALF * SUB)
    swap = np.zeros((HALF * SUB, HALF * SUB))
    swap[(rows % SUB) * HALF + rows // SUB, rows] = 1.0
    bf = lambda a: jnp.asarray(a.astype(np.float32)).astype(BF16)
    return dict(
        a_filter=bf(stage_a(natural)),
        a_value=bf(stage_a(stored)),
        a_back=bf(stage_a_back(stored)),
        twist=jnp.asarray(np.concatenate([np.cos(twist), -np.sin(twist)], 1).astype(np.float32)),
        forth=bf(forth),
        back=bf(back),
        swap=bf(swap),
        unswap=bf(swap.T),
    )


def dot(left, right):
    return jnp.dot(left, right, preferred_element_type=F32)


def stage_a_rows(swapped, a_table, twist, mid_ref):
    t_re = jnp.concatenate([twist[:, :SPAN]] * 2, 1)
    t_im = jnp.concatenate([twist[:, SPAN:]] * 2, 1)
    for c in range(SUB):
        block = swapped[c * HALF : (c + 1) * HALF, :]
        rows = jnp.concatenate([block[:, : 2 * SPAN], block[:, 2 * SPAN :]], 0)
        spec = dot(a_table, rows)
        re, im = spec[:BLOCKS], spec[BLOCKS:]
        out_re = (re * t_re - im * t_im).astype(BF16)
        out_im = (re * t_im + im * t_re).astype(BF16)
        for g in range(2):
            at = (g * SUB + c) * BLOCKS
            mid_ref[at : at + BLOCKS, :SPAN] = out_re[:, g * SPAN : (g + 1) * SPAN]
            mid_ref[at : at + BLOCKS, SPAN:] = out_im[:, g * SPAN : (g + 1) * SPAN]


CHUNK = 512


SLABS = 8


def filter_kernel(
    which, h_hbm, a_hbm, twist_hbm, forth_hbm, swap_hbm, out_ref,
    slab_ref, a_ref, twist_ref, forth_ref, swap_ref, gather_ref, mid_ref, slab_sem, table_sem,
):
    lane_block = pl.multiple_of((which[0] // 4) * SPAN, SPAN)
    piece = LENGTH // SLABS
    slabs = [
        pltpu.make_async_copy(
            h_hbm.at[pl.ds(k * piece, piece), pl.ds(lane_block, SPAN)],
            slab_ref.at[pl.ds(k * piece, piece), :],
            slab_sem.at[k],
        )
        for k in range(SLABS)
    ]
    pairs = [(a_hbm, a_ref), (twist_hbm, twist_ref), (forth_hbm, forth_ref), (swap_hbm, swap_ref)]
    loads = [pltpu.make_async_copy(s, d, table_sem.at[k]) for k, (s, d) in enumerate(pairs)]
    for copy in slabs + loads:
        copy.start()
    offset = (which[0] % 4) * GROUP
    rows = lax.broadcasted_iota(jnp.int32, (GROUP, SPAN), 0)
    lanes = lax.broadcasted_iota(jnp.int32, (GROUP, SPAN), 1)
    pick = jnp.where(lanes == rows + offset, 1.0, 0.0).astype(BF16)
    for block in range(BLOCKS):
        if block % (BLOCKS // SLABS) == 0:
            slabs[block // (BLOCKS // SLABS)].wait()
        half, a = divmod(block, HALF)
        turned = lax.dot_general(
            pick, slab_ref[block * SPAN : (block + 1) * SPAN, :], (((1,), (1,)), ((), ())), preferred_element_type=F32
        ).astype(BF16)
        for g in range(2):
            lane = (half * 2 + g) * SPAN
            gather_ref[a * SUB : (a + 1) * SUB, lane : lane + SPAN] = turned[g * SUB : (g + 1) * SUB]
    for copy in loads:
        copy.wait()
    swapped = dot(swap_ref[...], gather_ref[...]).astype(BF16)
    stage_a_rows(swapped, a_ref[...], twist_ref[...], mid_ref)
    for k in range(GROUP * BLOCKS // CHUNK):
        part = slice(k * CHUNK, (k + 1) * CHUNK)
        out_ref[part, :] = dot(mid_ref[part, :], forth_ref[...]).astype(out_ref.dtype)


def conv_kernel(
    chunks, x_ref, spec_ref, a_ref, a_back_ref, twist_ref, forth_ref, back_ref, swap_ref, unswap_ref, w_hbm,
    out_ref, w_ref, mid_ref, turn_ref, sem,
):
    copies = weight_copies(chunks[0], w_hbm, w_ref, sem)
    for copy in copies:
        copy.start()
    pieces = []
    for half in range(2):
        for g in range(2):
            piece = x_ref[:, g * SUB : (g + 1) * SUB, half * SPAN : (half + 1) * SPAN]
            pieces.append(piece.reshape(HALF * SUB, SPAN))
    swapped = dot(swap_ref[...], jnp.concatenate(pieces, 1)).astype(BF16)
    twist = twist_ref[...]
    stage_a_rows(swapped, a_ref[...], twist, mid_ref)
    t_re = jnp.concatenate([twist[:, :SPAN]] * (CHUNK // BLOCKS), 0)
    t_im = jnp.concatenate([twist[:, SPAN:]] * (CHUNK // BLOCKS), 0)
    for k in range(GROUP * BLOCKS // CHUNK):
        part = slice(k * CHUNK, (k + 1) * CHUNK)
        spec = dot(mid_ref[part, :], forth_ref[...])
        x_re, x_im = spec[:, :SPAN], spec[:, SPAN:]
        h = spec_ref[part, :].astype(F32)
        h_re, h_im = h[:, :SPAN], h[:, SPAN:]
        prod = jnp.concatenate([x_re * h_re - x_im * h_im, x_re * h_im + x_im * h_re], 1).astype(BF16)
        turn = dot(prod, back_ref[...])
        re, im = turn[:, :SPAN], turn[:, SPAN:]
        mid_ref[part, :SPAN] = (re * t_re + im * t_im).astype(BF16)
        mid_ref[part, SPAN:] = (im * t_re - re * t_im).astype(BF16)
    for c in range(SUB):
        sides = []
        for g in range(2):
            at = (g * SUB + c) * BLOCKS
            sides.append(
                jnp.concatenate([mid_ref[at : at + BLOCKS, :SPAN], mid_ref[at : at + BLOCKS, SPAN:]], 0)
            )
        y = dot(a_back_ref[...], jnp.concatenate(sides, 1)).astype(BF16)
        turn_ref[c * HALF : (c + 1) * HALF, : 2 * SPAN] = y[:HALF]
        turn_ref[c * HALF : (c + 1) * HALF, 2 * SPAN :] = y[HALF:]
    result = dot(unswap_ref[...], turn_ref[...]).astype(BF16)
    for half in range(2):
        for g in range(2):
            lane = (half * 2 + g) * SPAN
            out_ref[:, g * SUB : (g + 1) * SUB, half * SPAN : (half + 1) * SPAN] = result[:, lane : lane + SPAN].reshape(
                HALF, SUB, SPAN
            )
    for copy in copies:
        copy.wait()


def in_hbm(*arrays):
    return tuple(pltpu.with_memory_space_constraint(a, pltpu.HBM) for a in arrays)


def filter_spectrum(which, long_filter, t):
    return pl.pallas_call(
        filter_kernel,
        out_shape=jax.ShapeDtypeStruct((GROUP * BLOCKS, 2 * SPAN), BF16),
        in_specs=[pl.BlockSpec(memory_space=pltpu.SMEM)] + [pl.BlockSpec(memory_space=pltpu.HBM)] * 5,
        out_specs=pl.BlockSpec(memory_space=pltpu.VMEM),
        scratch_shapes=[
            pltpu.VMEM((LENGTH, SPAN), BF16),
            pltpu.VMEM((2 * BLOCKS, BLOCKS), BF16),
            pltpu.VMEM((BLOCKS, 2 * SPAN), F32),
            pltpu.VMEM((2 * SPAN, 2 * SPAN), BF16),
            pltpu.VMEM((HALF * SUB, HALF * SUB), BF16),
            pltpu.VMEM((HALF * SUB, 4 * SPAN), BF16),
            pltpu.VMEM((GROUP * BLOCKS, 2 * SPAN), BF16),
            pltpu.SemaphoreType.DMA((SLABS,)),
            pltpu.SemaphoreType.DMA((4,)),
        ],
        compiler_params=pltpu.CompilerParams(vmem_limit_bytes=32 << 20),
        name="filter_spectrum",
    )(which, *in_hbm(long_filter, t["a_filter"], t["twist"], t["forth"], t["swap"]))


def convolve(chunks, x, spec, w, t):
    inner, cols = w.shape[0], w.shape[1] // 4
    vmem = pl.BlockSpec(memory_space=pltpu.VMEM)
    return pl.pallas_call(
        conv_kernel,
        out_shape=(pltpu.VMEM((HALF, GROUP, 2 * SPAN), BF16), pltpu.VMEM((inner, cols), BF16)),
        in_specs=[pl.BlockSpec(memory_space=pltpu.SMEM)] + [vmem] * 9 + [pl.BlockSpec(memory_space=pltpu.HBM)],
        out_specs=(vmem, vmem),
        scratch_shapes=[
            pltpu.VMEM((GROUP * BLOCKS, 2 * SPAN), BF16),
            pltpu.VMEM((HALF * SUB, 4 * SPAN), BF16),
            pltpu.SemaphoreType.DMA((PARTS,)),
        ],
        compiler_params=pltpu.CompilerParams(vmem_limit_bytes=32 << 20),
        name="convolve",
    )(
        chunks, x, spec, t["a_value"], t["a_back"], t["twist"], t["forth"], t["back"], t["swap"], t["unswap"], *in_hbm(w)
    )


def turn_kernel(v_hbm, out_ref, in_ref, sem):
    width = v_hbm.shape[1] // 4
    copies = [
        pltpu.make_async_copy(v_hbm.at[:, pl.ds(k * width, width)], in_ref.at[k], sem.at[k]) for k in range(4)
    ]
    for copy in copies:
        copy.start()
    for k in range(4):
        copies[k].wait()
        out_ref[k * width : (k + 1) * width, :] = jnp.transpose(in_ref[k], (1, 0))


def turn(v):
    tokens, width = v.shape
    return pl.pallas_call(
        turn_kernel,
        out_shape=pltpu.VMEM((width, tokens), BF16),
        in_specs=[pl.BlockSpec(memory_space=pltpu.HBM)],
        out_specs=pl.BlockSpec(memory_space=pltpu.VMEM),
        scratch_shapes=[pltpu.VMEM((4, tokens, width // 4), BF16), pltpu.SemaphoreType.DMA((4,))],
        compiler_params=pltpu.CompilerParams(vmem_limit_bytes=16 << 20),
        name="turn",
    )(*in_hbm(v))


PARTS = 4


def weight_copies(chunk, w_hbm, w_ref, sem):
    inner, cols = w_ref.shape
    rows = inner // PARTS
    start = pl.multiple_of(chunk * cols, cols)
    return [
        pltpu.make_async_copy(
            w_hbm.at[pl.ds(k * rows, rows), pl.ds(start, cols)], w_ref.at[pl.ds(k * rows, rows), :], sem.at[k]
        )
        for k in range(PARTS)
    ]


def product(mix_ref, w_ref, copies):
    rows = w_ref.shape[0] // PARTS
    total = None
    for k in range(PARTS):
        copies[k].wait()
        part = dot(mix_ref[:, k * rows : (k + 1) * rows], w_ref[k * rows : (k + 1) * rows, :])
        total = part if total is None else total + part
    return total


def gate_kernel(y_ref, gate_ref, w_ref, mix_ref, out_ref):
    turned = jnp.transpose(y_ref[...], (1, 0))
    mix = (gate_ref[...].astype(F32) * turned.astype(F32)).astype(BF16)
    mix_ref[...] = mix
    out_ref[...] = dot(mix, w_ref[...]).astype(BF16)


def gate_project(y, gate, w):
    tokens, cols = gate.shape[0], w.shape[1]
    return pl.pallas_call(
        gate_kernel,
        out_shape=(jax.ShapeDtypeStruct(gate.shape, BF16), jax.ShapeDtypeStruct((tokens, cols), BF16)),
        compiler_params=pltpu.CompilerParams(vmem_limit_bytes=32 << 20),
        name="gate_project",
    )(y, gate, w)


def project(chunks, mix, w, dtypes):
    tokens, inner, cols = mix.shape[0], w.shape[0], w.shape[1] // 4
    count = len(dtypes)
    vmem = pl.BlockSpec(memory_space=pltpu.VMEM)

    def kernel(chunks, mix_ref, w_hbm, *refs):
        out_refs, (w_ref, sem) = refs[:count], refs[count:]
        copies = [weight_copies(chunks[j], w_hbm, w_ref.at[j], sem.at[j]) for j in range(count)]
        for copy in sum(copies, []):
            copy.start()
        for j in range(count):
            out_refs[j][...] = product(mix_ref, w_ref.at[j], copies[j]).astype(dtypes[j])

    return pl.pallas_call(
        kernel,
        out_shape=tuple(jax.ShapeDtypeStruct((tokens, cols), d) for d in dtypes),
        in_specs=[pl.BlockSpec(memory_space=pltpu.SMEM), vmem, pl.BlockSpec(memory_space=pltpu.HBM)],
        out_specs=(vmem,) * count,
        scratch_shapes=[pltpu.VMEM((count, inner, cols), BF16), pltpu.SemaphoreType.DMA((count, PARTS))],
        compiler_params=pltpu.CompilerParams(vmem_limit_bytes=32 << 20),
        name="project",
    )(chunks, mix, *in_hbm(w))


CORE_PAIR = [(0, 1), (1, 0), (2, 3), (3, 2)]
CHIP_PAIR = [(0, 2), (2, 0), (1, 3), (3, 1)]


def per_device(query_gate, gated_value, long_filter, out_weight):
    t = tables()
    me = lax.axis_index("ctx")
    mine = lax.axis_index("ch")
    tokens, width = gated_value.shape
    turned = turn(gated_value).reshape(HALF, GROUP, tokens)
    x = lax.all_to_all(turned, "ctx", 0, 0, tiled=True)
    spec = filter_spectrum(me.reshape(1), long_filter, t)
    order = jnp.arange(3, -1, -1, dtype=jnp.int32) ^ mine
    y, w_first = convolve(order[:1], x, spec, out_weight, t)
    y = lax.all_to_all(y, "ctx", 0, 0, tiled=True).reshape(width, tokens)
    mix, away_pair = gate_project(y, query_gate, w_first)
    away_in = lax.ppermute(away_pair, "ch", CORE_PAIR)
    (away_own,) = project(order[1:2], mix, out_weight, (F32,))
    away_sum = (away_own + away_in.astype(F32)).astype(BF16)
    mix, away_sum = lax.optimization_barrier((mix, away_sum))
    far = lax.ppermute(away_sum, "ch", CHIP_PAIR)
    home_pair, home_own = project(order[2:], mix, out_weight, (BF16, F32))
    near = lax.ppermute(home_pair, "ch", CORE_PAIR)
    return (home_own + near.astype(F32) + far.astype(F32)).astype(BF16)


def solution(mesh):
    placed = (P("ctx", "ch"), P("ctx", "ch"), P(None, "ch"), P("ch", None))
    return jax.shard_map(
        per_device, mesh=mesh, in_specs=placed, out_specs=P("ctx", "ch"), check_vma=False
    )
```

```python
import functools

import jax
import jax.numpy as jnp
import numpy as np
from jax import lax
from jax.experimental import pallas as pl
from jax.experimental.pallas import tpu as pltpu
from jax.sharding import PartitionSpec as P

SPAN = 128
BLOCKS = 64
HALF = BLOCKS // 2
LENGTH = SPAN * BLOCKS
GROUP = 32
SUB = 16
F32 = jnp.float32
BF16 = jnp.bfloat16


def tables():
    first = np.arange(BLOCKS)[:, None] + 0.25
    natural = np.arange(BLOCKS)[None, :]
    stored = np.concatenate([np.arange(HALF), BLOCKS - 1 - np.arange(HALF)])[None, :]

    def stage_a(order):
        angle = 2 * np.pi * first * order / BLOCKS
        return np.concatenate([np.cos(angle), -np.sin(angle)], 0)

    def stage_a_back(order):
        angle = (2 * np.pi * first * order / BLOCKS).T
        return np.concatenate([np.cos(angle), -np.sin(angle)], 1) / LENGTH

    twist = 2 * np.pi * first * np.arange(SPAN)[None, :] / LENGTH
    angle = 2 * np.pi * np.arange(SPAN)[:, None] * np.arange(SPAN)[None, :] / SPAN
    cos, sin = np.cos(angle), np.sin(angle)
    forth = np.block([[cos, -sin], [sin, cos]])
    back = np.block([[cos, sin], [-sin, cos]])
    rows = np.arange(HALF * SUB)
    swap = np.zeros((HALF * SUB, HALF * SUB))
    swap[(rows % SUB) * HALF + rows // SUB, rows] = 1.0
    bf = lambda a: jnp.asarray(a.astype(np.float32)).astype(BF16)
    return dict(
        a_filter=bf(stage_a(natural)),
        a_value=bf(stage_a(stored)),
        a_back=bf(stage_a_back(stored)),
        twist=jnp.asarray(np.concatenate([np.cos(twist), -np.sin(twist)], 1).astype(np.float32)),
        forth=bf(forth),
        back=bf(back),
        swap=bf(swap),
        unswap=bf(swap.T),
    )


def dot(left, right):
    return jnp.dot(left, right, preferred_element_type=F32)


def stage_a_rows(swapped, a_table, twist, mid_ref):
    t_re = jnp.concatenate([twist[:, :SPAN]] * 2, 1)
    t_im = jnp.concatenate([twist[:, SPAN:]] * 2, 1)
    for c in range(SUB):
        block = swapped[c * HALF : (c + 1) * HALF, :]
        rows = jnp.concatenate([block[:, : 2 * SPAN], block[:, 2 * SPAN :]], 0)
        spec = dot(a_table, rows)
        re, im = spec[:BLOCKS], spec[BLOCKS:]
        out_re = (re * t_re - im * t_im).astype(BF16)
        out_im = (re * t_im + im * t_re).astype(BF16)
        for g in range(2):
            at = (g * SUB + c) * BLOCKS
            mid_ref[at : at + BLOCKS, :SPAN] = out_re[:, g * SPAN : (g + 1) * SPAN]
            mid_ref[at : at + BLOCKS, SPAN:] = out_im[:, g * SPAN : (g + 1) * SPAN]


CHUNK = 512


SLABS = 8


def filter_kernel(
    which, h_hbm, a_hbm, twist_hbm, forth_hbm, swap_hbm, out_ref,
    slab_ref, a_ref, twist_ref, forth_ref, swap_ref, gather_ref, mid_ref, slab_sem, table_sem,
):
    lane_block = pl.multiple_of((which[0] // 4) * SPAN, SPAN)
    piece = LENGTH // SLABS
    slabs = [
        pltpu.make_async_copy(
            h_hbm.at[pl.ds(k * piece, piece), pl.ds(lane_block, SPAN)],
            slab_ref.at[pl.ds(k * piece, piece), :],
            slab_sem.at[k],
        )
        for k in range(SLABS)
    ]
    pairs = [(a_hbm, a_ref), (twist_hbm, twist_ref), (forth_hbm, forth_ref), (swap_hbm, swap_ref)]
    loads = [pltpu.make_async_copy(s, d, table_sem.at[k]) for k, (s, d) in enumerate(pairs)]
    for copy in slabs + loads:
        copy.start()
    offset = (which[0] % 4) * GROUP
    rows = lax.broadcasted_iota(jnp.int32, (GROUP, SPAN), 0)
    lanes = lax.broadcasted_iota(jnp.int32, (GROUP, SPAN), 1)
    pick = jnp.where(lanes == rows + offset, 1.0, 0.0).astype(BF16)
    for block in range(BLOCKS):
        if block % (BLOCKS // SLABS) == 0:
            slabs[block // (BLOCKS // SLABS)].wait()
        half, a = divmod(block, HALF)
        turned = lax.dot_general(
            pick, slab_ref[block * SPAN : (block + 1) * SPAN, :], (((1,), (1,)), ((), ())), preferred_element_type=F32
        ).astype(BF16)
        for g in range(2):
            lane = (half * 2 + g) * SPAN
            gather_ref[a * SUB : (a + 1) * SUB, lane : lane + SPAN] = turned[g * SUB : (g + 1) * SUB]
    for copy in loads:
        copy.wait()
    swapped = dot(swap_ref[...], gather_ref[...]).astype(BF16)
    stage_a_rows(swapped, a_ref[...], twist_ref[...], mid_ref)
    for k in range(GROUP * BLOCKS // CHUNK):
        part = slice(k * CHUNK, (k + 1) * CHUNK)
        out_ref[part, :] = dot(mid_ref[part, :], forth_ref[...]).astype(out_ref.dtype)


def conv_kernel(
    starts, x_ref, spec_ref, a_ref, a_back_ref, twist_ref, forth_ref, back_ref, swap_ref, unswap_ref, w_hbm,
    out_ref, w_pair_ref, w_own_ref, mid_ref, turn_ref, sem,
):
    copies = weight_copies(starts[0], w_hbm, w_pair_ref, sem.at[0]) + weight_copies(starts[1], w_hbm, w_own_ref, sem.at[1])
    for copy in copies:
        copy.start()
    pieces = []
    for half in range(2):
        for g in range(2):
            piece = x_ref[:, g * SUB : (g + 1) * SUB, half * SPAN : (half + 1) * SPAN]
            pieces.append(piece.reshape(HALF * SUB, SPAN))
    swapped = dot(swap_ref[...], jnp.concatenate(pieces, 1)).astype(BF16)
    twist = twist_ref[...]
    stage_a_rows(swapped, a_ref[...], twist, mid_ref)
    t_re = jnp.concatenate([twist[:, :SPAN]] * (CHUNK // BLOCKS), 0)
    t_im = jnp.concatenate([twist[:, SPAN:]] * (CHUNK // BLOCKS), 0)
    for k in range(GROUP * BLOCKS // CHUNK):
        part = slice(k * CHUNK, (k + 1) * CHUNK)
        spec = dot(mid_ref[part, :], forth_ref[...])
        x_re, x_im = spec[:, :SPAN], spec[:, SPAN:]
        h = spec_ref[part, :].astype(F32)
        h_re, h_im = h[:, :SPAN], h[:, SPAN:]
        prod = jnp.concatenate([x_re * h_re - x_im * h_im, x_re * h_im + x_im * h_re], 1).astype(BF16)
        turn = dot(prod, back_ref[...])
        re, im = turn[:, :SPAN], turn[:, SPAN:]
        mid_ref[part, :SPAN] = (re * t_re + im * t_im).astype(BF16)
        mid_ref[part, SPAN:] = (im * t_re - re * t_im).astype(BF16)
    for c in range(SUB):
        sides = []
        for g in range(2):
            at = (g * SUB + c) * BLOCKS
            sides.append(
                jnp.concatenate([mid_ref[at : at + BLOCKS, :SPAN], mid_ref[at : at + BLOCKS, SPAN:]], 0)
            )
        y = dot(a_back_ref[...], jnp.concatenate(sides, 1)).astype(BF16)
        turn_ref[c * HALF : (c + 1) * HALF, : 2 * SPAN] = y[:HALF]
        turn_ref[c * HALF : (c + 1) * HALF, 2 * SPAN :] = y[HALF:]
    result = dot(unswap_ref[...], turn_ref[...]).astype(BF16)
    for half in range(2):
        for g in range(2):
            lane = (half * 2 + g) * SPAN
            out_ref[:, g * SUB : (g + 1) * SUB, half * SPAN : (half + 1) * SPAN] = result[:, lane : lane + SPAN].reshape(
                HALF, SUB, SPAN
            )
    for copy in copies:
        copy.wait()


def cost(flops, moved):
    return pl.CostEstimate(flops=flops, transcendentals=0, bytes_accessed=moved)


def in_hbm(*arrays):
    return tuple(pltpu.with_memory_space_constraint(a, pltpu.HBM) for a in arrays)


def filter_spectrum(which, long_filter, t):
    return pl.pallas_call(
        filter_kernel,
        out_shape=jax.ShapeDtypeStruct((GROUP * BLOCKS, 2 * SPAN), BF16),
        in_specs=[pl.BlockSpec(memory_space=pltpu.SMEM)] + [pl.BlockSpec(memory_space=pltpu.HBM)] * 5,
        out_specs=pl.BlockSpec(memory_space=pltpu.VMEM),
        scratch_shapes=[
            pltpu.VMEM((LENGTH, SPAN), BF16),
            pltpu.VMEM((2 * BLOCKS, BLOCKS), BF16),
            pltpu.VMEM((BLOCKS, 2 * SPAN), F32),
            pltpu.VMEM((2 * SPAN, 2 * SPAN), BF16),
            pltpu.VMEM((HALF * SUB, HALF * SUB), BF16),
            pltpu.VMEM((HALF * SUB, 4 * SPAN), BF16),
            pltpu.VMEM((GROUP * BLOCKS, 2 * SPAN), BF16),
            pltpu.SemaphoreType.DMA((SLABS,)),
            pltpu.SemaphoreType.DMA((4,)),
        ],
        compiler_params=pltpu.CompilerParams(vmem_limit_bytes=32 << 20),
        name="filter_spectrum",
    )(which, *in_hbm(long_filter, t["a_filter"], t["twist"], t["forth"], t["swap"]))


def convolve(starts, x, spec, w, t):
    inner, cols = w.shape[0], w.shape[1] // 8
    vmem = pl.BlockSpec(memory_space=pltpu.VMEM)
    return pl.pallas_call(
        conv_kernel,
        out_shape=(
            jax.ShapeDtypeStruct((HALF, GROUP, 2 * SPAN), BF16),
            jax.ShapeDtypeStruct((inner, cols), BF16),
            jax.ShapeDtypeStruct((inner, cols), BF16),
        ),
        in_specs=[pl.BlockSpec(memory_space=pltpu.SMEM)] + [vmem] * 9 + [pl.BlockSpec(memory_space=pltpu.HBM)],
        out_specs=(vmem, vmem, vmem),
        scratch_shapes=[
            pltpu.VMEM((GROUP * BLOCKS, 2 * SPAN), BF16),
            pltpu.VMEM((HALF * SUB, 4 * SPAN), BF16),
            pltpu.SemaphoreType.DMA((2, PARTS)),
        ],
        compiler_params=pltpu.CompilerParams(vmem_limit_bytes=32 << 20),
        name="convolve",
    )(
        starts, x, spec, t["a_value"], t["a_back"], t["twist"], t["forth"], t["back"], t["swap"], t["unswap"], *in_hbm(w)
    )


TURN = 4


def turn_kernel(v_hbm, out_hbm, in_ref, turned_ref, in_sem, out_sem):
    width = v_hbm.shape[1] // TURN
    loads = [
        pltpu.make_async_copy(v_hbm.at[:, pl.ds(k * width, width)], in_ref.at[k], in_sem.at[k]) for k in range(TURN)
    ]
    stores = [
        pltpu.make_async_copy(turned_ref.at[k], out_hbm.at[pl.ds(k * width, width), :], out_sem.at[k])
        for k in range(TURN)
    ]
    for load in loads:
        load.start()
    for k in range(TURN):
        loads[k].wait()
        turned_ref[k] = jnp.transpose(in_ref[k], (1, 0))
        stores[k].start()
    for store in stores:
        store.wait()


def turn(v):
    tokens, width = v.shape
    hbm = pl.BlockSpec(memory_space=pltpu.HBM)
    return pl.pallas_call(
        turn_kernel,
        out_shape=jax.ShapeDtypeStruct((width, tokens), BF16),
        in_specs=[hbm],
        out_specs=hbm,
        scratch_shapes=[
            pltpu.VMEM((TURN, tokens, width // TURN), BF16),
            pltpu.VMEM((TURN, width // TURN, tokens), BF16),
            pltpu.SemaphoreType.DMA((TURN,)),
            pltpu.SemaphoreType.DMA((TURN,)),
        ],
        compiler_params=pltpu.CompilerParams(vmem_limit_bytes=16 << 20),
        name="turn",
    )(*in_hbm(v))


PARTS = 4


def weight_copies(start, w_hbm, w_ref, sem):
    inner, cols = w_ref.shape
    rows = inner // PARTS
    start = pl.multiple_of(start, cols)
    return [
        pltpu.make_async_copy(
            w_hbm.at[pl.ds(k * rows, rows), pl.ds(start, cols)], w_ref.at[pl.ds(k * rows, rows), :], sem.at[k]
        )
        for k in range(PARTS)
    ]


def product(mix_ref, w_ref, copies):
    rows = w_ref.shape[0] // PARTS
    total = None
    for k in range(PARTS):
        copies[k].wait()
        part = dot(mix_ref[:, k * rows : (k + 1) * rows], w_ref[k * rows : (k + 1) * rows, :])
        total = part if total is None else total + part
    return total


def gate_kernel(y_ref, gate_ref, w_ref, mix_ref, out_ref):
    turned = jnp.transpose(y_ref[...], (1, 0))
    mix = (gate_ref[...].astype(F32) * turned.astype(F32)).astype(BF16)
    mix_ref[...] = mix
    out_ref[...] = dot(mix, w_ref[...]).astype(BF16)


def gate_project(y, gate, w):
    tokens, cols = gate.shape[0], w.shape[1]
    return pl.pallas_call(
        gate_kernel,
        out_shape=(jax.ShapeDtypeStruct(gate.shape, BF16), jax.ShapeDtypeStruct((tokens, cols), BF16)),
        compiler_params=pltpu.CompilerParams(vmem_limit_bytes=32 << 20),
        name="gate_project",
    )(y, gate, w)


def resident_kernel(mix_ref, w_ref, out_ref):
    out_ref[...] = dot(mix_ref[...], w_ref[...])


def project_resident(mix, w):
    return pl.pallas_call(
        resident_kernel,
        out_shape=jax.ShapeDtypeStruct((mix.shape[0], w.shape[1]), F32),
        compiler_params=pltpu.CompilerParams(vmem_limit_bytes=32 << 20),
        cost_estimate=cost(2 * mix.shape[0] * w.shape[0] * w.shape[1], 0),
        name="project_resident",
    )(mix, w)


def project(starts, cols, mix, w, pieces):
    tokens, inner = mix.shape[0], w.shape[0]
    rows = tokens // pieces
    vmem = pl.BlockSpec(memory_space=pltpu.VMEM)

    def kernel(starts, mix_ref, w_hbm, *refs):
        piece_refs, (own_ref, w_ref, sem) = refs[:pieces], refs[pieces:]
        copies = [weight_copies(starts[j], w_hbm, w_ref.at[j], sem.at[j]) for j in range(2)]
        for copy in copies[0] + copies[1]:
            copy.start()
        pair = product(mix_ref, w_ref.at[0], copies[0]).astype(BF16)
        for k in range(pieces):
            piece_refs[k][...] = pair[k * rows : (k + 1) * rows]
        own_ref[...] = product(mix_ref, w_ref.at[1], copies[1])

    out = pl.pallas_call(
        kernel,
        out_shape=(jax.ShapeDtypeStruct((rows, cols), BF16),) * pieces + (jax.ShapeDtypeStruct((tokens, cols), F32),),
        in_specs=[pl.BlockSpec(memory_space=pltpu.SMEM), vmem, pl.BlockSpec(memory_space=pltpu.HBM)],
        out_specs=(vmem,) * (pieces + 1),
        scratch_shapes=[pltpu.VMEM((2, inner, cols), BF16), pltpu.SemaphoreType.DMA((2, PARTS))],
        compiler_params=pltpu.CompilerParams(vmem_limit_bytes=32 << 20),
        cost_estimate=cost(4 * tokens * inner * cols, 4 * inner * cols),
        name="project",
    )(starts, mix, *in_hbm(w))
    return out[:pieces], out[pieces]


def finish(home, near, far_a, far_b):
    tokens, cols = home.shape
    rows = tokens // len(near)

    def kernel(home_ref, *refs):
        near_refs, (far_a_ref, far_b_ref, out_hbm, sum_ref, sem) = refs[: len(near)], refs[len(near) :]
        copies = []
        for k, near_ref in enumerate(near_refs):
            part = slice(k * rows, (k + 1) * rows)
            far = jnp.concatenate([far_a_ref[part, :], far_b_ref[part, :]], 1)
            total = home_ref[part, :] + near_ref[...].astype(F32) + far.astype(F32)
            sum_ref[part, :] = total.astype(BF16)
            copy = pltpu.make_async_copy(
                sum_ref.at[pl.ds(k * rows, rows), :], out_hbm.at[pl.ds(k * rows, rows), :], sem.at[k]
            )
            copy.start()
            copies.append(copy)
        for copy in copies:
            copy.wait()

    return pl.pallas_call(
        kernel,
        out_shape=jax.ShapeDtypeStruct(home.shape, BF16),
        in_specs=[pl.BlockSpec(memory_space=pltpu.VMEM)] * (3 + len(near)),
        out_specs=pl.BlockSpec(memory_space=pltpu.HBM),
        scratch_shapes=[pltpu.VMEM(home.shape, BF16), pltpu.SemaphoreType.DMA((len(near),))],
        compiler_params=pltpu.CompilerParams(vmem_limit_bytes=16 << 20),
        name="finish",
    )(home, *near, far_a, far_b)


CORE_PAIR = [(0, 1), (1, 0), (2, 3), (3, 2)]
PIECES_B = 4
PIECES_HOME = 2
CHIP_PAIR = [(0, 2), (2, 0), (1, 3), (3, 1)]


def per_device(query_gate, gated_value, long_filter, out_weight):
    t = tables()
    me = lax.axis_index("ctx")
    mine = lax.axis_index("ch")
    tokens, width = gated_value.shape
    turned = turn(gated_value).reshape(HALF, GROUP, tokens)
    x = lax.all_to_all(turned, "ctx", 0, 0, tiled=True)
    spec = filter_spectrum(me.reshape(1), long_filter, t)
    cols = out_weight.shape[1] // 4
    half = cols // 2
    first = jnp.stack([mine ^ 3, mine ^ 2]).astype(jnp.int32) * cols
    home = jnp.stack([mine ^ 1, mine]).astype(jnp.int32) * cols
    second = first + half
    y, w_pair, w_own = convolve(first, x, spec, out_weight, t)
    y = lax.all_to_all(y, "ctx", 0, 0, tiled=True).reshape(width, tokens)
    mix, pair_a = gate_project(y, query_gate, w_pair)
    in_a = lax.ppermute(pair_a, "ch", CORE_PAIR)
    own_a = project_resident(mix, w_own)
    sum_a = (own_a + in_a.astype(F32)).astype(BF16)
    mix, sum_a = lax.optimization_barrier((mix, sum_a))
    far_a = lax.ppermute(sum_a, "ch", CHIP_PAIR)
    pair_b, own_b = project(second, half, mix, out_weight, PIECES_B)
    in_b = [lax.ppermute(piece, "ch", CORE_PAIR) for piece in pair_b]
    sum_b = (own_b + jnp.concatenate(in_b, 0).astype(F32)).astype(BF16)
    mix, sum_b = lax.optimization_barrier((mix, sum_b))
    far_b = lax.ppermute(sum_b, "ch", CHIP_PAIR)
    mix, far_a = lax.optimization_barrier((mix, far_a))
    home_pair, home_own = project(home, cols, mix, out_weight, PIECES_HOME)
    near = [lax.ppermute(piece, "ch", CORE_PAIR) for piece in home_pair]
    return finish(home_own, near, far_a, far_b)


def solution(mesh):
    placed = (P("ctx", "ch"), P("ctx", "ch"), P(None, "ch"), P("ch", None))
    return jax.shard_map(
        per_device, mesh=mesh, in_specs=placed, out_specs=P("ctx", "ch"), check_vma=False
    )
```

```python
import functools

import jax
import jax.numpy as jnp
import numpy as np
from jax import lax
from jax.experimental import pallas as pl
from jax.experimental.pallas import tpu as pltpu
from jax.sharding import PartitionSpec as P

SPAN = 128
BLOCKS = 64
HALF = BLOCKS // 2
LENGTH = SPAN * BLOCKS
GROUP = 32
SUB = 16
F32 = jnp.float32
BF16 = jnp.bfloat16


def tables():
    first = np.arange(BLOCKS)[:, None] + 0.25
    natural = np.arange(BLOCKS)[None, :]
    stored = np.concatenate([np.arange(HALF), BLOCKS - 1 - np.arange(HALF)])[None, :]

    def stage_a(order):
        angle = 2 * np.pi * first * order / BLOCKS
        return np.concatenate([np.cos(angle), -np.sin(angle)], 0)

    def stage_a_back(order):
        angle = (2 * np.pi * first * order / BLOCKS).T
        return np.concatenate([np.cos(angle), -np.sin(angle)], 1) / LENGTH

    twist = 2 * np.pi * first * np.arange(SPAN)[None, :] / LENGTH
    angle = 2 * np.pi * np.arange(SPAN)[:, None] * np.arange(SPAN)[None, :] / SPAN
    cos, sin = np.cos(angle), np.sin(angle)
    forth = np.block([[cos, -sin], [sin, cos]])
    rows = np.arange(SUB * SUB)
    swap = np.zeros((SUB * SUB, SUB * SUB))
    swap[(rows % SUB) * SUB + rows // SUB, rows] = 1.0
    bf = lambda a: jnp.asarray(a.astype(np.float32)).astype(BF16)
    return dict(
        a_filter=bf(stage_a(natural)),
        a_value=bf(stage_a(stored)),
        a_back=bf(stage_a_back(stored)),
        twist=jnp.asarray(np.concatenate([np.cos(twist), -np.sin(twist)], 1).astype(np.float32)),
        forth=bf(forth),
        swap=bf(swap),
    )


def dot(left, right):
    return jnp.dot(left, right, preferred_element_type=F32)


def lane_of(half, high, g):
    return ((half * 2 + high) * 2 + g) * SPAN


def stage_a_rows(swapped, a_table, twist, mid_ref):
    t_re = jnp.concatenate([twist[:, :SPAN]] * 2, 1)
    t_im = jnp.concatenate([twist[:, SPAN:]] * 2, 1)
    for c in range(SUB):
        block = swapped[c * SUB : (c + 1) * SUB, :]
        rows = jnp.concatenate([block[:, k * 2 * SPAN : (k + 1) * 2 * SPAN] for k in range(4)], 0)
        spec = dot(a_table, rows)
        re, im = spec[:BLOCKS], spec[BLOCKS:]
        out_re = (re * t_re - im * t_im).astype(BF16)
        out_im = (re * t_im + im * t_re).astype(BF16)
        for g in range(2):
            at = (g * SUB + c) * BLOCKS
            mid_ref[at : at + BLOCKS, :SPAN] = out_re[:, g * SPAN : (g + 1) * SPAN]
            mid_ref[at : at + BLOCKS, SPAN:] = out_im[:, g * SPAN : (g + 1) * SPAN]


CHUNK = 512


SLABS = 8


HALF_PARTS = 2


def half_copies(side, chunk, w_hbm, w_ref, sem):
    inner, cols = w_ref.shape
    rows = inner // HALF_PARTS
    start = pl.multiple_of(chunk * cols, cols)
    return [
        pltpu.make_async_copy(
            w_hbm.at[pl.ds(side * inner + k * rows, rows), pl.ds(start, cols)],
            w_ref.at[pl.ds(k * rows, rows), :],
            sem.at[k],
        )
        for k in range(HALF_PARTS)
    ]


def filter_kernel(
    which, h_hbm, w_hbm, a_hbm, twist_hbm, forth_hbm, swap_hbm, out_ref, w_ref,
    slab_ref, a_ref, twist_ref, forth_ref, swap_ref, gather_ref, mid_ref, slab_sem, w_sem, table_sem,
):
    lane_block = pl.multiple_of((which[0] // 4) * SPAN, SPAN)
    piece = LENGTH // SLABS
    slabs = [
        pltpu.make_async_copy(
            h_hbm.at[pl.ds(k * piece, piece), pl.ds(lane_block, SPAN)],
            slab_ref.at[pl.ds(k * piece, piece), :],
            slab_sem.at[k],
        )
        for k in range(SLABS)
    ]
    pairs = [(a_hbm, a_ref), (twist_hbm, twist_ref), (forth_hbm, forth_ref), (swap_hbm, swap_ref)]
    loads = [pltpu.make_async_copy(s, d, table_sem.at[k]) for k, (s, d) in enumerate(pairs)]
    weights = half_copies(0, which[1], w_hbm, w_ref, w_sem)
    for copy in slabs + loads + weights:
        copy.start()
    offset = (which[0] % 4) * GROUP
    rows = lax.broadcasted_iota(jnp.int32, (GROUP, SPAN), 0)
    lanes = lax.broadcasted_iota(jnp.int32, (GROUP, SPAN), 1)
    pick = jnp.where(lanes == rows + offset, 1.0, 0.0).astype(BF16)
    for block in range(BLOCKS):
        if block % (BLOCKS // SLABS) == 0:
            slabs[block // (BLOCKS // SLABS)].wait()
        half, high, a = block // HALF, block // SUB % 2, block % SUB
        turned = lax.dot_general(
            pick, slab_ref[block * SPAN : (block + 1) * SPAN, :], (((1,), (1,)), ((), ())), preferred_element_type=F32
        ).astype(BF16)
        for g in range(2):
            lane = lane_of(half, high, g)
            gather_ref[a * SUB : (a + 1) * SUB, lane : lane + SPAN] = turned[g * SUB : (g + 1) * SUB]
    for copy in loads:
        copy.wait()
    swapped = dot(swap_ref[...], gather_ref[...]).astype(BF16)
    stage_a_rows(swapped, a_ref[...], twist_ref[...], mid_ref)
    for k in range(GROUP * BLOCKS // CHUNK):
        part = slice(k * CHUNK, (k + 1) * CHUNK)
        out_ref[part, :] = dot(mid_ref[part, :], forth_ref[...]).astype(out_ref.dtype)
    for copy in weights:
        copy.wait()


def conv_kernel(
    chunks, x_ref, spec_ref, a_ref, a_back_ref, twist_ref, forth_ref, swap_ref, w_hbm,
    out_ref, w_ref, mid_ref, turn_ref, sem,
):
    copies = half_copies(1, chunks[0], w_hbm, w_ref, sem)
    for copy in copies:
        copy.start()
    pieces = []
    for half in range(2):
        for high in range(2):
            for g in range(2):
                piece = x_ref[
                    high * SUB : (high + 1) * SUB, g * SUB : (g + 1) * SUB, half * SPAN : (half + 1) * SPAN
                ]
                pieces.append(piece.reshape(SUB * SUB, SPAN))
    swapped = dot(swap_ref[...], jnp.concatenate(pieces, 1)).astype(BF16)
    twist = twist_ref[...]
    stage_a_rows(swapped, a_ref[...], twist, mid_ref)
    t_re = jnp.concatenate([twist[:, :SPAN]] * (CHUNK // BLOCKS), 0)
    t_im = jnp.concatenate([twist[:, SPAN:]] * (CHUNK // BLOCKS), 0)
    for k in range(GROUP * BLOCKS // CHUNK):
        part = slice(k * CHUNK, (k + 1) * CHUNK)
        spec = dot(mid_ref[part, :], forth_ref[...])
        x_re, x_im = spec[:, :SPAN], spec[:, SPAN:]
        h = spec_ref[part, :].astype(F32)
        h_re, h_im = h[:, :SPAN], h[:, SPAN:]
        prod = jnp.concatenate([x_re * h_re - x_im * h_im, x_re * h_im + x_im * h_re], 1).astype(BF16)
        turn = lax.dot_general(prod, forth_ref[...], (((1,), (1,)), ((), ())), preferred_element_type=F32)
        re, im = turn[:, :SPAN], turn[:, SPAN:]
        mid_ref[part, :SPAN] = (re * t_re + im * t_im).astype(BF16)
        mid_ref[part, SPAN:] = (im * t_re - re * t_im).astype(BF16)
    for c in range(SUB):
        sides = []
        for g in range(2):
            at = (g * SUB + c) * BLOCKS
            sides.append(
                jnp.concatenate([mid_ref[at : at + BLOCKS, :SPAN], mid_ref[at : at + BLOCKS, SPAN:]], 0)
            )
        y = dot(a_back_ref[...], jnp.concatenate(sides, 1)).astype(BF16)
        for k in range(4):
            turn_ref[c * SUB : (c + 1) * SUB, k * 2 * SPAN : (k + 1) * 2 * SPAN] = y[k * SUB : (k + 1) * SUB]
    result = dot(swap_ref[...], turn_ref[...]).astype(BF16)
    for half in range(2):
        for high in range(2):
            for g in range(2):
                lane = lane_of(half, high, g)
                out_ref[
                    high * SUB : (high + 1) * SUB, g * SUB : (g + 1) * SUB, half * SPAN : (half + 1) * SPAN
                ] = result[:, lane : lane + SPAN].reshape(SUB, SUB, SPAN)
    for copy in copies:
        copy.wait()


def in_hbm(*arrays):
    return tuple(pltpu.with_memory_space_constraint(a, pltpu.HBM) for a in arrays)


def filter_spectrum(which, long_filter, weight, t):
    half_chunk = (weight.shape[0] // 2, weight.shape[1] // 4)
    vmem = pl.BlockSpec(memory_space=pltpu.VMEM)
    return pl.pallas_call(
        filter_kernel,
        out_shape=(
            jax.ShapeDtypeStruct((GROUP * BLOCKS, 2 * SPAN), BF16),
            jax.ShapeDtypeStruct(half_chunk, BF16),
        ),
        in_specs=[pl.BlockSpec(memory_space=pltpu.SMEM)] + [pl.BlockSpec(memory_space=pltpu.HBM)] * 6,
        out_specs=(vmem, vmem),
        scratch_shapes=[
            pltpu.VMEM((LENGTH, SPAN), BF16),
            pltpu.VMEM((2 * BLOCKS, BLOCKS), BF16),
            pltpu.VMEM((BLOCKS, 2 * SPAN), F32),
            pltpu.VMEM((2 * SPAN, 2 * SPAN), BF16),
            pltpu.VMEM((SUB * SUB, SUB * SUB), BF16),
            pltpu.VMEM((SUB * SUB, 8 * SPAN), BF16),
            pltpu.VMEM((GROUP * BLOCKS, 2 * SPAN), BF16),
            pltpu.SemaphoreType.DMA((SLABS,)),
            pltpu.SemaphoreType.DMA((HALF_PARTS,)),
            pltpu.SemaphoreType.DMA((4,)),
        ],
        compiler_params=pltpu.CompilerParams(vmem_limit_bytes=32 << 20),
        name="filter_spectrum",
    )(which, *in_hbm(long_filter, weight, t["a_filter"], t["twist"], t["forth"], t["swap"]))


def convolve(chunks, x, spec, w, t):
    vmem = pl.BlockSpec(memory_space=pltpu.VMEM)
    return pl.pallas_call(
        conv_kernel,
        out_shape=(
            jax.ShapeDtypeStruct((HALF, GROUP, 2 * SPAN), BF16),
            jax.ShapeDtypeStruct((w.shape[0] // 2, w.shape[1] // 4), BF16),
        ),
        in_specs=[pl.BlockSpec(memory_space=pltpu.SMEM)] + [vmem] * 7 + [pl.BlockSpec(memory_space=pltpu.HBM)],
        out_specs=(vmem, vmem),
        scratch_shapes=[
            pltpu.VMEM((GROUP * BLOCKS, 2 * SPAN), BF16),
            pltpu.VMEM((SUB * SUB, 8 * SPAN), BF16),
            pltpu.SemaphoreType.DMA((HALF_PARTS,)),
        ],
        compiler_params=pltpu.CompilerParams(vmem_limit_bytes=32 << 20),
        name="convolve",
    )(
        chunks, x, spec, t["a_value"], t["a_back"], t["twist"], t["forth"], t["swap"], *in_hbm(w)
    )


def turn_kernel(v_hbm, out_ref, in_ref, sem):
    width = v_hbm.shape[1] // 4
    copies = [
        pltpu.make_async_copy(v_hbm.at[:, pl.ds(k * width, width)], in_ref.at[k], sem.at[k]) for k in range(4)
    ]
    for copy in copies:
        copy.start()
    for k in range(4):
        copies[k].wait()
        out_ref[k * width : (k + 1) * width, :] = jnp.transpose(in_ref[k], (1, 0))


def turn(v):
    tokens, width = v.shape
    return pl.pallas_call(
        turn_kernel,
        out_shape=pltpu.VMEM((width, tokens), BF16),
        in_specs=[pl.BlockSpec(memory_space=pltpu.HBM)],
        out_specs=pl.BlockSpec(memory_space=pltpu.VMEM),
        scratch_shapes=[pltpu.VMEM((4, tokens, width // 4), BF16), pltpu.SemaphoreType.DMA((4,))],
        compiler_params=pltpu.CompilerParams(vmem_limit_bytes=16 << 20),
        name="turn",
    )(*in_hbm(v))


PARTS = 4


def weight_copies(chunk, w_hbm, w_ref, sem):
    inner, cols = w_ref.shape
    rows = inner // PARTS
    start = pl.multiple_of(chunk * cols, cols)
    return [
        pltpu.make_async_copy(
            w_hbm.at[pl.ds(k * rows, rows), pl.ds(start, cols)], w_ref.at[pl.ds(k * rows, rows), :], sem.at[k]
        )
        for k in range(PARTS)
    ]


def product(mix_ref, w_ref, copies):
    rows = w_ref.shape[0] // PARTS
    total = None
    for k in range(PARTS):
        copies[k].wait()
        part = dot(mix_ref[:, k * rows : (k + 1) * rows], w_ref[k * rows : (k + 1) * rows, :])
        total = part if total is None else total + part
    return total


def gate_kernel(y_ref, gate_ref, w_top_ref, w_low_ref, mix_ref, out_ref):
    turned = jnp.transpose(y_ref[...], (1, 0))
    mix = (gate_ref[...].astype(F32) * turned.astype(F32)).astype(BF16)
    mix_ref[...] = mix
    rows = w_top_ref.shape[0]
    out_ref[...] = (dot(mix[:, :rows], w_top_ref[...]) + dot(mix[:, rows:], w_low_ref[...])).astype(BF16)


def gate_project(y, gate, w_top, w_low):
    tokens, cols = gate.shape[0], w_top.shape[1]
    return pl.pallas_call(
        gate_kernel,
        out_shape=(jax.ShapeDtypeStruct(gate.shape, BF16), jax.ShapeDtypeStruct((tokens, cols), BF16)),
        compiler_params=pltpu.CompilerParams(vmem_limit_bytes=32 << 20),
        name="gate_project",
    )(y, gate, w_top, w_low)


def project(chunks, mix, w, dtypes):
    tokens, inner, cols = mix.shape[0], w.shape[0], w.shape[1] // 4
    count = len(dtypes)
    vmem = pl.BlockSpec(memory_space=pltpu.VMEM)

    def kernel(chunks, mix_ref, w_hbm, *refs):
        out_refs, (w_ref, sem) = refs[:count], refs[count:]
        copies = [weight_copies(chunks[j], w_hbm, w_ref.at[j], sem.at[j]) for j in range(count)]
        for copy in sum(copies, []):
            copy.start()
        for j in range(count):
            out_refs[j][...] = product(mix_ref, w_ref.at[j], copies[j]).astype(dtypes[j])

    return pl.pallas_call(
        kernel,
        out_shape=tuple(jax.ShapeDtypeStruct((tokens, cols), d) for d in dtypes),
        in_specs=[pl.BlockSpec(memory_space=pltpu.SMEM), vmem, pl.BlockSpec(memory_space=pltpu.HBM)],
        out_specs=(vmem,) * count,
        scratch_shapes=[pltpu.VMEM((count, inner, cols), BF16), pltpu.SemaphoreType.DMA((count, PARTS))],
        compiler_params=pltpu.CompilerParams(vmem_limit_bytes=32 << 20),
        name="project",
    )(chunks, mix, *in_hbm(w))


CORE_PAIR = [(0, 1), (1, 0), (2, 3), (3, 2)]
CHIP_PAIR = [(0, 2), (2, 0), (1, 3), (3, 1)]


def per_device(query_gate, gated_value, long_filter, out_weight):
    t = tables()
    me = lax.axis_index("ctx")
    mine = lax.axis_index("ch")
    tokens, width = gated_value.shape
    turned = turn(gated_value).reshape(HALF, GROUP, tokens)
    x = lax.all_to_all(turned, "ctx", 0, 0, tiled=True)
    order = jnp.arange(3, -1, -1, dtype=jnp.int32) ^ mine
    which = jnp.stack([me, mine ^ 3]).astype(jnp.int32)
    spec, w_top = filter_spectrum(which, long_filter, out_weight, t)
    y, w_low = convolve(order[:1], x, spec, out_weight, t)
    y = lax.all_to_all(y, "ctx", 0, 0, tiled=True).reshape(width, tokens)
    mix, away_pair = gate_project(y, query_gate, w_top, w_low)
    away_in = lax.ppermute(away_pair, "ch", CORE_PAIR)
    (away_own,) = project(order[1:2], mix, out_weight, (F32,))
    away_sum = (away_own + away_in.astype(F32)).astype(BF16)
    mix, away_sum = lax.optimization_barrier((mix, away_sum))
    far = lax.ppermute(away_sum, "ch", CHIP_PAIR)
    home_pair, home_own = project(order[2:], mix, out_weight, (BF16, F32))
    near = lax.ppermute(home_pair, "ch", CORE_PAIR)
    return (home_own + near.astype(F32) + far.astype(F32)).astype(BF16)


def solution(mesh):
    placed = (P("ctx", "ch"), P("ctx", "ch"), P(None, "ch"), P("ch", None))
    return jax.shard_map(
        per_device, mesh=mesh, in_specs=placed, out_specs=P("ctx", "ch"), check_vma=False
    )
```

```python
import functools

import jax
import jax.numpy as jnp
import numpy as np
from jax import lax
from jax.experimental import pallas as pl
from jax.experimental.pallas import tpu as pltpu
from jax.sharding import PartitionSpec as P

SPAN = 128
BLOCKS = 64
HALF = BLOCKS // 2
LENGTH = SPAN * BLOCKS
GROUP = 32
SUB = 16
F32 = jnp.float32
BF16 = jnp.bfloat16


def tables():
    first = np.arange(BLOCKS)[:, None] + 0.25
    natural = np.arange(BLOCKS)[None, :]
    stored = np.concatenate([np.arange(HALF), BLOCKS - 1 - np.arange(HALF)])[None, :]

    def stage_a(order):
        angle = 2 * np.pi * first * order / BLOCKS
        return np.concatenate([np.cos(angle), -np.sin(angle)], 0)

    def stage_a_back(order):
        angle = (2 * np.pi * first * order / BLOCKS).T
        return np.concatenate([np.cos(angle), -np.sin(angle)], 1) / LENGTH

    twist = 2 * np.pi * first * np.arange(SPAN)[None, :] / LENGTH
    angle = 2 * np.pi * np.arange(SPAN)[:, None] * np.arange(SPAN)[None, :] / SPAN
    cos, sin = np.cos(angle), np.sin(angle)
    forth = np.block([[cos, -sin], [sin, cos]])
    rows = np.arange(SUB * SUB)
    swap = np.zeros((SUB * SUB, SUB * SUB))
    swap[(rows % SUB) * SUB + rows // SUB, rows] = 1.0
    bf = lambda a: jnp.asarray(a.astype(np.float32)).astype(BF16)
    return dict(
        a_filter=bf(stage_a(natural)),
        a_value=bf(stage_a(stored)),
        a_back=bf(stage_a_back(stored)),
        twist=jnp.asarray(np.concatenate([np.cos(twist), -np.sin(twist)], 1).astype(np.float32)),
        forth=bf(forth),
        swap=bf(swap),
    )


def dot(left, right):
    return jnp.dot(left, right, preferred_element_type=F32)


def lane_of(half, high, g):
    return ((half * 2 + high) * 2 + g) * SPAN


def stage_a_rows(swapped, a_table, twist, mid_ref):
    t_re = jnp.concatenate([twist[:, :SPAN]] * 2, 1)
    t_im = jnp.concatenate([twist[:, SPAN:]] * 2, 1)
    for c in range(SUB):
        block = swapped[c * SUB : (c + 1) * SUB, :]
        rows = jnp.concatenate([block[:, k * 2 * SPAN : (k + 1) * 2 * SPAN] for k in range(4)], 0)
        spec = dot(a_table, rows)
        re, im = spec[:BLOCKS], spec[BLOCKS:]
        out_re = (re * t_re - im * t_im).astype(BF16)
        out_im = (re * t_im + im * t_re).astype(BF16)
        for g in range(2):
            at = (g * SUB + c) * BLOCKS
            mid_ref[at : at + BLOCKS, :SPAN] = out_re[:, g * SPAN : (g + 1) * SPAN]
            mid_ref[at : at + BLOCKS, SPAN:] = out_im[:, g * SPAN : (g + 1) * SPAN]


CHUNK = 512


SLABS = 8


QUARTERS = 4
EARLY = 3


def quarter_copies(first, count, chunk, w_hbm, w_ref, sem):
    rows, cols = w_ref.shape[0] // count, w_ref.shape[1]
    start = pl.multiple_of(chunk * cols, cols)
    return [
        pltpu.make_async_copy(
            w_hbm.at[pl.ds((first + k) * rows, rows), pl.ds(start, cols)],
            w_ref.at[pl.ds(k * rows, rows), :],
            sem.at[k],
        )
        for k in range(count)
    ]


def filter_kernel(
    which, h_hbm, w_hbm, a_hbm, twist_hbm, forth_hbm, swap_hbm, out_ref, w_ref,
    slab_ref, a_ref, twist_ref, forth_ref, swap_ref, gather_ref, mid_ref, slab_sem, w_sem, table_sem,
):
    lane_block = pl.multiple_of((which[0] // 4) * SPAN, SPAN)
    piece = LENGTH // SLABS
    slabs = [
        pltpu.make_async_copy(
            h_hbm.at[pl.ds(k * piece, piece), pl.ds(lane_block, SPAN)],
            slab_ref.at[pl.ds(k * piece, piece), :],
            slab_sem.at[k],
        )
        for k in range(SLABS)
    ]
    pairs = [(a_hbm, a_ref), (twist_hbm, twist_ref), (forth_hbm, forth_ref), (swap_hbm, swap_ref)]
    loads = [pltpu.make_async_copy(s, d, table_sem.at[k]) for k, (s, d) in enumerate(pairs)]
    weights = quarter_copies(0, EARLY, which[1], w_hbm, w_ref, w_sem)
    for copy in slabs + loads + weights:
        copy.start()
    offset = (which[0] % 4) * GROUP
    rows = lax.broadcasted_iota(jnp.int32, (GROUP, SPAN), 0)
    lanes = lax.broadcasted_iota(jnp.int32, (GROUP, SPAN), 1)
    pick = jnp.where(lanes == rows + offset, 1.0, 0.0).astype(BF16)
    for block in range(BLOCKS):
        if block % (BLOCKS // SLABS) == 0:
            slabs[block // (BLOCKS // SLABS)].wait()
        half, high, a = block // HALF, block // SUB % 2, block % SUB
        turned = lax.dot_general(
            pick, slab_ref[block * SPAN : (block + 1) * SPAN, :], (((1,), (1,)), ((), ())), preferred_element_type=F32
        ).astype(BF16)
        for g in range(2):
            lane = lane_of(half, high, g)
            gather_ref[a * SUB : (a + 1) * SUB, lane : lane + SPAN] = turned[g * SUB : (g + 1) * SUB]
    for copy in loads:
        copy.wait()
    swapped = dot(swap_ref[...], gather_ref[...]).astype(BF16)
    stage_a_rows(swapped, a_ref[...], twist_ref[...], mid_ref)
    for k in range(GROUP * BLOCKS // CHUNK):
        part = slice(k * CHUNK, (k + 1) * CHUNK)
        out_ref[part, :] = dot(mid_ref[part, :], forth_ref[...]).astype(out_ref.dtype)
    for copy in weights:
        copy.wait()


def conv_kernel(
    chunks, x_ref, spec_ref, a_ref, a_back_ref, twist_ref, forth_ref, swap_ref, w_hbm,
    out_ref, w_ref, mid_ref, turn_ref, sem,
):
    copies = quarter_copies(EARLY, QUARTERS - EARLY, chunks[0], w_hbm, w_ref, sem)
    for copy in copies:
        copy.start()
    pieces = []
    for half in range(2):
        for high in range(2):
            for g in range(2):
                piece = x_ref[
                    high * SUB : (high + 1) * SUB, g * SUB : (g + 1) * SUB, half * SPAN : (half + 1) * SPAN
                ]
                pieces.append(piece.reshape(SUB * SUB, SPAN))
    swapped = dot(swap_ref[...], jnp.concatenate(pieces, 1)).astype(BF16)
    twist = twist_ref[...]
    stage_a_rows(swapped, a_ref[...], twist, mid_ref)
    t_re = jnp.concatenate([twist[:, :SPAN]] * (CHUNK // BLOCKS), 0)
    t_im = jnp.concatenate([twist[:, SPAN:]] * (CHUNK // BLOCKS), 0)
    for k in range(GROUP * BLOCKS // CHUNK):
        part = slice(k * CHUNK, (k + 1) * CHUNK)
        spec = dot(mid_ref[part, :], forth_ref[...])
        x_re, x_im = spec[:, :SPAN], spec[:, SPAN:]
        h = spec_ref[part, :].astype(F32)
        h_re, h_im = h[:, :SPAN], h[:, SPAN:]
        prod = jnp.concatenate([x_re * h_re - x_im * h_im, x_re * h_im + x_im * h_re], 1).astype(BF16)
        turn = lax.dot_general(prod, forth_ref[...], (((1,), (1,)), ((), ())), preferred_element_type=F32)
        re, im = turn[:, :SPAN], turn[:, SPAN:]
        mid_ref[part, :SPAN] = (re * t_re + im * t_im).astype(BF16)
        mid_ref[part, SPAN:] = (im * t_re - re * t_im).astype(BF16)
    for copy in copies:
        copy.wait()
    for c in range(SUB):
        sides = []
        for g in range(2):
            at = (g * SUB + c) * BLOCKS
            sides.append(
                jnp.concatenate([mid_ref[at : at + BLOCKS, :SPAN], mid_ref[at : at + BLOCKS, SPAN:]], 0)
            )
        y = dot(a_back_ref[...], jnp.concatenate(sides, 1)).astype(BF16)
        for k in range(4):
            turn_ref[c * SUB : (c + 1) * SUB, k * 2 * SPAN : (k + 1) * 2 * SPAN] = y[k * SUB : (k + 1) * SUB]
    result = dot(swap_ref[...], turn_ref[...]).astype(BF16)
    for half in range(2):
        for high in range(2):
            for g in range(2):
                lane = lane_of(half, high, g)
                out_ref[
                    high * SUB : (high + 1) * SUB, g * SUB : (g + 1) * SUB, half * SPAN : (half + 1) * SPAN
                ] = result[:, lane : lane + SPAN].reshape(SUB, SUB, SPAN)


def in_hbm(*arrays):
    return tuple(pltpu.with_memory_space_constraint(a, pltpu.HBM) for a in arrays)


def filter_spectrum(which, long_filter, weight, t):
    early_chunk = (weight.shape[0] // QUARTERS * EARLY, weight.shape[1] // 4)
    vmem = pl.BlockSpec(memory_space=pltpu.VMEM)
    return pl.pallas_call(
        filter_kernel,
        out_shape=(
            jax.ShapeDtypeStruct((GROUP * BLOCKS, 2 * SPAN), BF16),
            jax.ShapeDtypeStruct(early_chunk, BF16),
        ),
        in_specs=[pl.BlockSpec(memory_space=pltpu.SMEM)] + [pl.BlockSpec(memory_space=pltpu.HBM)] * 6,
        out_specs=(vmem, vmem),
        scratch_shapes=[
            pltpu.VMEM((LENGTH, SPAN), BF16),
            pltpu.VMEM((2 * BLOCKS, BLOCKS), BF16),
            pltpu.VMEM((BLOCKS, 2 * SPAN), F32),
            pltpu.VMEM((2 * SPAN, 2 * SPAN), BF16),
            pltpu.VMEM((SUB * SUB, SUB * SUB), BF16),
            pltpu.VMEM((SUB * SUB, 8 * SPAN), BF16),
            pltpu.VMEM((GROUP * BLOCKS, 2 * SPAN), BF16),
            pltpu.SemaphoreType.DMA((SLABS,)),
            pltpu.SemaphoreType.DMA((EARLY,)),
            pltpu.SemaphoreType.DMA((4,)),
        ],
        compiler_params=pltpu.CompilerParams(vmem_limit_bytes=32 << 20),
        name="filter_spectrum",
    )(which, *in_hbm(long_filter, weight, t["a_filter"], t["twist"], t["forth"], t["swap"]))


def convolve(chunks, x, spec, w, t):
    vmem = pl.BlockSpec(memory_space=pltpu.VMEM)
    return pl.pallas_call(
        conv_kernel,
        out_shape=(
            jax.ShapeDtypeStruct((HALF, GROUP, 2 * SPAN), BF16),
            jax.ShapeDtypeStruct((w.shape[0] // QUARTERS * (QUARTERS - EARLY), w.shape[1] // 4), BF16),
        ),
        in_specs=[pl.BlockSpec(memory_space=pltpu.SMEM)] + [vmem] * 7 + [pl.BlockSpec(memory_space=pltpu.HBM)],
        out_specs=(vmem, vmem),
        scratch_shapes=[
            pltpu.VMEM((GROUP * BLOCKS, 2 * SPAN), BF16),
            pltpu.VMEM((SUB * SUB, 8 * SPAN), BF16),
            pltpu.SemaphoreType.DMA((QUARTERS - EARLY,)),
        ],
        compiler_params=pltpu.CompilerParams(vmem_limit_bytes=32 << 20),
        name="convolve",
    )(
        chunks, x, spec, t["a_value"], t["a_back"], t["twist"], t["forth"], t["swap"], *in_hbm(w)
    )


def turn_kernel(v_hbm, out_ref, in_ref, sem):
    width = v_hbm.shape[1] // 4
    copies = [
        pltpu.make_async_copy(v_hbm.at[:, pl.ds(k * width, width)], in_ref.at[k], sem.at[k]) for k in range(4)
    ]
    for copy in copies:
        copy.start()
    for k in range(4):
        copies[k].wait()
        out_ref[k * width : (k + 1) * width, :] = jnp.transpose(in_ref[k], (1, 0))


def turn(v):
    tokens, width = v.shape
    return pl.pallas_call(
        turn_kernel,
        out_shape=pltpu.VMEM((width, tokens), BF16),
        in_specs=[pl.BlockSpec(memory_space=pltpu.HBM)],
        out_specs=pl.BlockSpec(memory_space=pltpu.VMEM),
        scratch_shapes=[pltpu.VMEM((4, tokens, width // 4), BF16), pltpu.SemaphoreType.DMA((4,))],
        compiler_params=pltpu.CompilerParams(vmem_limit_bytes=16 << 20),
        name="turn",
    )(*in_hbm(v))


PARTS = 4


def weight_copies(chunk, w_hbm, w_ref, sem):
    inner, cols = w_ref.shape
    rows = inner // PARTS
    start = pl.multiple_of(chunk * cols, cols)
    return [
        pltpu.make_async_copy(
            w_hbm.at[pl.ds(k * rows, rows), pl.ds(start, cols)], w_ref.at[pl.ds(k * rows, rows), :], sem.at[k]
        )
        for k in range(PARTS)
    ]


def product(mix_ref, w_ref, copies):
    rows = w_ref.shape[0] // PARTS
    total = None
    for k in range(PARTS):
        copies[k].wait()
        part = dot(mix_ref[:, k * rows : (k + 1) * rows], w_ref[k * rows : (k + 1) * rows, :])
        total = part if total is None else total + part
    return total


def gate_kernel(y_ref, gate_ref, w_top_ref, w_low_ref, mix_ref, out_ref):
    turned = jnp.transpose(y_ref[...], (1, 0))
    mix = (gate_ref[...].astype(F32) * turned.astype(F32)).astype(BF16)
    mix_ref[...] = mix
    rows = w_top_ref.shape[0]
    out_ref[...] = (dot(mix[:, :rows], w_top_ref[...]) + dot(mix[:, rows:], w_low_ref[...])).astype(BF16)


def gate_project(y, gate, w_top, w_low):
    tokens, cols = gate.shape[0], w_top.shape[1]
    return pl.pallas_call(
        gate_kernel,
        out_shape=(jax.ShapeDtypeStruct(gate.shape, BF16), jax.ShapeDtypeStruct((tokens, cols), BF16)),
        compiler_params=pltpu.CompilerParams(vmem_limit_bytes=32 << 20),
        name="gate_project",
    )(y, gate, w_top, w_low)


def project(chunks, mix, w, dtypes):
    tokens, inner, cols = mix.shape[0], w.shape[0], w.shape[1] // 4
    count = len(dtypes)
    vmem = pl.BlockSpec(memory_space=pltpu.VMEM)

    def kernel(chunks, mix_ref, w_hbm, *refs):
        out_refs, (w_ref, sem) = refs[:count], refs[count:]
        copies = [weight_copies(chunks[j], w_hbm, w_ref.at[j], sem.at[j]) for j in range(count)]
        for copy in sum(copies, []):
            copy.start()
        for j in range(count):
            out_refs[j][...] = product(mix_ref, w_ref.at[j], copies[j]).astype(dtypes[j])

    return pl.pallas_call(
        kernel,
        out_shape=tuple(jax.ShapeDtypeStruct((tokens, cols), d) for d in dtypes),
        in_specs=[pl.BlockSpec(memory_space=pltpu.SMEM), vmem, pl.BlockSpec(memory_space=pltpu.HBM)],
        out_specs=(vmem,) * count,
        scratch_shapes=[pltpu.VMEM((count, inner, cols), BF16), pltpu.SemaphoreType.DMA((count, PARTS))],
        compiler_params=pltpu.CompilerParams(vmem_limit_bytes=32 << 20),
        name="project",
    )(chunks, mix, *in_hbm(w))


CORE_PAIR = [(0, 1), (1, 0), (2, 3), (3, 2)]
CHIP_PAIR = [(0, 2), (2, 0), (1, 3), (3, 1)]


def per_device(query_gate, gated_value, long_filter, out_weight):
    t = tables()
    me = lax.axis_index("ctx")
    mine = lax.axis_index("ch")
    tokens, width = gated_value.shape
    turned = turn(gated_value).reshape(HALF, GROUP, tokens)
    x = lax.all_to_all(turned, "ctx", 0, 0, tiled=True)
    order = jnp.arange(3, -1, -1, dtype=jnp.int32) ^ mine
    which = jnp.stack([me, mine ^ 3]).astype(jnp.int32)
    spec, w_top = filter_spectrum(which, long_filter, out_weight, t)
    y, w_low = convolve(order[:1], x, spec, out_weight, t)
    y = lax.all_to_all(y, "ctx", 0, 0, tiled=True).reshape(width, tokens)
    mix, away_pair = gate_project(y, query_gate, w_top, w_low)
    away_in = lax.ppermute(away_pair, "ch", CORE_PAIR)
    (away_own,) = project(order[1:2], mix, out_weight, (F32,))
    away_sum = (away_own + away_in.astype(F32)).astype(BF16)
    mix, away_sum = lax.optimization_barrier((mix, away_sum))
    far = lax.ppermute(away_sum, "ch", CHIP_PAIR)
    home_pair, home_own = project(order[2:], mix, out_weight, (BF16, F32))
    near = lax.ppermute(home_pair, "ch", CORE_PAIR)
    return (home_own + near.astype(F32) + far.astype(F32)).astype(BF16)


def solution(mesh):
    placed = (P("ctx", "ch"), P("ctx", "ch"), P(None, "ch"), P("ch", None))
    return jax.shard_map(
        per_device, mesh=mesh, in_specs=placed, out_specs=P("ctx", "ch"), check_vma=False
    )
```

```python
import functools

import jax
import jax.numpy as jnp
import numpy as np
from jax import lax
from jax.experimental import pallas as pl
from jax.experimental.pallas import tpu as pltpu
from jax.sharding import PartitionSpec as P

SPAN = 128
BLOCKS = 64
HALF = BLOCKS // 2
LENGTH = SPAN * BLOCKS
GROUP = 32
SUB = 16
F32 = jnp.float32
BF16 = jnp.bfloat16


def tables():
    first = np.arange(BLOCKS)[:, None] + 0.25
    natural = np.arange(BLOCKS)[None, :]
    stored = np.concatenate([np.arange(HALF), BLOCKS - 1 - np.arange(HALF)])[None, :]

    def stage_a(order):
        angle = 2 * np.pi * first * order / BLOCKS
        return np.concatenate([np.cos(angle), -np.sin(angle)], 0)

    def stage_a_back(order):
        angle = (2 * np.pi * first * order / BLOCKS).T
        return np.concatenate([np.cos(angle), -np.sin(angle)], 1) / LENGTH

    twist = 2 * np.pi * first * np.arange(SPAN)[None, :] / LENGTH
    angle = 2 * np.pi * np.arange(SPAN)[:, None] * np.arange(SPAN)[None, :] / SPAN
    cos, sin = np.cos(angle), np.sin(angle)
    forth = np.block([[cos, -sin], [sin, cos]])
    back = np.block([[cos, sin], [-sin, cos]])
    rows = np.arange(HALF * SUB)
    swap = np.zeros((HALF * SUB, HALF * SUB))
    swap[(rows % SUB) * HALF + rows // SUB, rows] = 1.0
    bf = lambda a: jnp.asarray(a.astype(np.float32)).astype(BF16)
    return dict(
        a_filter=bf(stage_a(natural)),
        a_value=bf(stage_a(stored)),
        a_back=bf(stage_a_back(stored)),
        twist=jnp.asarray(np.concatenate([np.cos(twist), -np.sin(twist)], 1).astype(np.float32)),
        forth=bf(forth),
        back=bf(back),
        swap=bf(swap),
        unswap=bf(swap.T),
    )


def dot(left, right):
    return jnp.dot(left, right, preferred_element_type=F32)


def stage_a_rows(swapped, a_table, twist, mid_ref):
    t_re = jnp.concatenate([twist[:, :SPAN]] * 2, 1)
    t_im = jnp.concatenate([twist[:, SPAN:]] * 2, 1)
    for c in range(SUB):
        block = swapped[c * HALF : (c + 1) * HALF, :]
        rows = jnp.concatenate([block[:, : 2 * SPAN], block[:, 2 * SPAN :]], 0)
        spec = dot(a_table, rows)
        re, im = spec[:BLOCKS], spec[BLOCKS:]
        out_re = (re * t_re - im * t_im).astype(BF16)
        out_im = (re * t_im + im * t_re).astype(BF16)
        for g in range(2):
            at = (g * SUB + c) * BLOCKS
            mid_ref[at : at + BLOCKS, :SPAN] = out_re[:, g * SPAN : (g + 1) * SPAN]
            mid_ref[at : at + BLOCKS, SPAN:] = out_im[:, g * SPAN : (g + 1) * SPAN]


CHUNK = 512


SLABS = 8


def filter_kernel(
    which, h_hbm, a_hbm, twist_hbm, forth_hbm, swap_hbm, out_ref,
    slab_ref, a_ref, twist_ref, forth_ref, swap_ref, gather_ref, mid_ref, slab_sem, table_sem,
):
    lane_block = pl.multiple_of((which[0] // 4) * SPAN, SPAN)
    piece = LENGTH // SLABS
    slabs = [
        pltpu.make_async_copy(
            h_hbm.at[pl.ds(k * piece, piece), pl.ds(lane_block, SPAN)],
            slab_ref.at[pl.ds(k * piece, piece), :],
            slab_sem.at[k],
        )
        for k in range(SLABS)
    ]
    pairs = [(a_hbm, a_ref), (twist_hbm, twist_ref), (forth_hbm, forth_ref), (swap_hbm, swap_ref)]
    loads = [pltpu.make_async_copy(s, d, table_sem.at[k]) for k, (s, d) in enumerate(pairs)]
    for copy in slabs + loads:
        copy.start()
    offset = (which[0] % 4) * GROUP
    rows = lax.broadcasted_iota(jnp.int32, (GROUP, SPAN), 0)
    lanes = lax.broadcasted_iota(jnp.int32, (GROUP, SPAN), 1)
    pick = jnp.where(lanes == rows + offset, 1.0, 0.0).astype(BF16)
    for block in range(BLOCKS):
        if block % (BLOCKS // SLABS) == 0:
            slabs[block // (BLOCKS // SLABS)].wait()
        half, a = divmod(block, HALF)
        turned = lax.dot_general(
            pick, slab_ref[block * SPAN : (block + 1) * SPAN, :], (((1,), (1,)), ((), ())), preferred_element_type=F32
        ).astype(BF16)
        for g in range(2):
            lane = (half * 2 + g) * SPAN
            gather_ref[a * SUB : (a + 1) * SUB, lane : lane + SPAN] = turned[g * SUB : (g + 1) * SUB]
    for copy in loads:
        copy.wait()
    swapped = dot(swap_ref[...], gather_ref[...]).astype(BF16)
    stage_a_rows(swapped, a_ref[...], twist_ref[...], mid_ref)
    for k in range(GROUP * BLOCKS // CHUNK):
        part = slice(k * CHUNK, (k + 1) * CHUNK)
        out_ref[part, :] = dot(mid_ref[part, :], forth_ref[...]).astype(out_ref.dtype)


def conv_kernel(
    chunks, x_ref, spec_ref, a_ref, a_back_ref, twist_ref, forth_ref, back_ref, swap_ref, unswap_ref, w_hbm,
    out_ref, w_ref, mid_ref, turn_ref, sem,
):
    copies = weight_copies(chunks[0], w_hbm, w_ref, sem)
    for copy in copies:
        copy.start()
    pieces = []
    for half in range(2):
        for g in range(2):
            piece = x_ref[:, g * SUB : (g + 1) * SUB, half * SPAN : (half + 1) * SPAN]
            pieces.append(piece.reshape(HALF * SUB, SPAN))
    swapped = dot(swap_ref[...], jnp.concatenate(pieces, 1)).astype(BF16)
    twist = twist_ref[...]
    stage_a_rows(swapped, a_ref[...], twist, mid_ref)
    t_re = jnp.concatenate([twist[:, :SPAN]] * (CHUNK // BLOCKS), 0)
    t_im = jnp.concatenate([twist[:, SPAN:]] * (CHUNK // BLOCKS), 0)
    for k in range(GROUP * BLOCKS // CHUNK):
        part = slice(k * CHUNK, (k + 1) * CHUNK)
        spec = dot(mid_ref[part, :], forth_ref[...])
        x_re, x_im = spec[:, :SPAN], spec[:, SPAN:]
        h = spec_ref[part, :].astype(F32)
        h_re, h_im = h[:, :SPAN], h[:, SPAN:]
        prod = jnp.concatenate([x_re * h_re - x_im * h_im, x_re * h_im + x_im * h_re], 1).astype(BF16)
        turn = dot(prod, back_ref[...])
        re, im = turn[:, :SPAN], turn[:, SPAN:]
        mid_ref[part, :SPAN] = (re * t_re + im * t_im).astype(BF16)
        mid_ref[part, SPAN:] = (im * t_re - re * t_im).astype(BF16)
    for c in range(SUB):
        sides = []
        for g in range(2):
            at = (g * SUB + c) * BLOCKS
            sides.append(
                jnp.concatenate([mid_ref[at : at + BLOCKS, :SPAN], mid_ref[at : at + BLOCKS, SPAN:]], 0)
            )
        y = dot(a_back_ref[...], jnp.concatenate(sides, 1)).astype(BF16)
        turn_ref[c * HALF : (c + 1) * HALF, : 2 * SPAN] = y[:HALF]
        turn_ref[c * HALF : (c + 1) * HALF, 2 * SPAN :] = y[HALF:]
    result = dot(unswap_ref[...], turn_ref[...]).astype(BF16)
    for half in range(2):
        for g in range(2):
            lane = (half * 2 + g) * SPAN
            out_ref[:, g * SUB : (g + 1) * SUB, half * SPAN : (half + 1) * SPAN] = result[:, lane : lane + SPAN].reshape(
                HALF, SUB, SPAN
            )
    for copy in copies:
        copy.wait()


def in_hbm(*arrays):
    return tuple(pltpu.with_memory_space_constraint(a, pltpu.HBM) for a in arrays)


def filter_spectrum(which, long_filter, t):
    return pl.pallas_call(
        filter_kernel,
        out_shape=jax.ShapeDtypeStruct((GROUP * BLOCKS, 2 * SPAN), BF16),
        in_specs=[pl.BlockSpec(memory_space=pltpu.SMEM)] + [pl.BlockSpec(memory_space=pltpu.HBM)] * 5,
        out_specs=pl.BlockSpec(memory_space=pltpu.VMEM),
        scratch_shapes=[
            pltpu.VMEM((LENGTH, SPAN), BF16),
            pltpu.VMEM((2 * BLOCKS, BLOCKS), BF16),
            pltpu.VMEM((BLOCKS, 2 * SPAN), F32),
            pltpu.VMEM((2 * SPAN, 2 * SPAN), BF16),
            pltpu.VMEM((HALF * SUB, HALF * SUB), BF16),
            pltpu.VMEM((HALF * SUB, 4 * SPAN), BF16),
            pltpu.VMEM((GROUP * BLOCKS, 2 * SPAN), BF16),
            pltpu.SemaphoreType.DMA((SLABS,)),
            pltpu.SemaphoreType.DMA((4,)),
        ],
        compiler_params=pltpu.CompilerParams(vmem_limit_bytes=32 << 20),
        name="filter_spectrum",
    )(which, *in_hbm(long_filter, t["a_filter"], t["twist"], t["forth"], t["swap"]))


def convolve(chunks, x, spec, w, t):
    inner, cols = w.shape[0], w.shape[1] // 4
    vmem = pl.BlockSpec(memory_space=pltpu.VMEM)
    return pl.pallas_call(
        conv_kernel,
        out_shape=(pltpu.VMEM((HALF, GROUP, 2 * SPAN), BF16), pltpu.VMEM((inner, cols), BF16)),
        in_specs=[pl.BlockSpec(memory_space=pltpu.SMEM)] + [vmem] * 9 + [pl.BlockSpec(memory_space=pltpu.HBM)],
        out_specs=(vmem, vmem),
        scratch_shapes=[
            pltpu.VMEM((GROUP * BLOCKS, 2 * SPAN), BF16),
            pltpu.VMEM((HALF * SUB, 4 * SPAN), BF16),
            pltpu.SemaphoreType.DMA((PARTS,)),
        ],
        compiler_params=pltpu.CompilerParams(vmem_limit_bytes=32 << 20),
        name="convolve",
    )(
        chunks, x, spec, t["a_value"], t["a_back"], t["twist"], t["forth"], t["back"], t["swap"], t["unswap"], *in_hbm(w)
    )


def turn_kernel(v_hbm, out_ref, in_ref, sem):
    width = v_hbm.shape[1] // 4
    copies = [
        pltpu.make_async_copy(v_hbm.at[:, pl.ds(k * width, width)], in_ref.at[k], sem.at[k]) for k in range(4)
    ]
    for copy in copies:
        copy.start()
    for k in range(4):
        copies[k].wait()
        out_ref[k * width : (k + 1) * width, :] = jnp.transpose(in_ref[k], (1, 0))


def turn(v):
    tokens, width = v.shape
    return pl.pallas_call(
        turn_kernel,
        out_shape=pltpu.VMEM((width, tokens), BF16),
        in_specs=[pl.BlockSpec(memory_space=pltpu.HBM)],
        out_specs=pl.BlockSpec(memory_space=pltpu.VMEM),
        scratch_shapes=[pltpu.VMEM((4, tokens, width // 4), BF16), pltpu.SemaphoreType.DMA((4,))],
        compiler_params=pltpu.CompilerParams(vmem_limit_bytes=16 << 20),
        name="turn",
    )(*in_hbm(v))


PARTS = 4


def weight_copies(chunk, w_hbm, w_ref, sem):
    inner, cols = w_ref.shape
    rows = inner // PARTS
    start = pl.multiple_of(chunk * cols, cols)
    return [
        pltpu.make_async_copy(
            w_hbm.at[pl.ds(k * rows, rows), pl.ds(start, cols)], w_ref.at[pl.ds(k * rows, rows), :], sem.at[k]
        )
        for k in range(PARTS)
    ]


def product(mix_ref, w_ref, copies):
    rows = w_ref.shape[0] // PARTS
    total = None
    for k in range(PARTS):
        copies[k].wait()
        part = dot(mix_ref[:, k * rows : (k + 1) * rows], w_ref[k * rows : (k + 1) * rows, :])
        total = part if total is None else total + part
    return total


def gate_kernel(y_ref, gate_ref, w_ref, mix_ref, out_ref):
    turned = jnp.transpose(y_ref[...], (1, 0))
    mix = (gate_ref[...].astype(F32) * turned.astype(F32)).astype(BF16)
    mix_ref[...] = mix
    out_ref[...] = dot(mix, w_ref[...]).astype(BF16)


def gate_project(y, gate, w):
    tokens, cols = gate.shape[0], w.shape[1]
    return pl.pallas_call(
        gate_kernel,
        out_shape=(jax.ShapeDtypeStruct(gate.shape, BF16), jax.ShapeDtypeStruct((tokens, cols), BF16)),
        compiler_params=pltpu.CompilerParams(vmem_limit_bytes=32 << 20),
        name="gate_project",
    )(y, gate, w)


def project(chunks, mix, w, targets):
    tokens, inner, cols = mix.shape[0], w.shape[0], w.shape[1] // 4
    count = 1 + max(j for j, _, _ in targets)
    pieces = [(j, dtype, k * tokens // n, tokens // n) for j, dtype, n in targets for k in range(n)]
    vmem = pl.BlockSpec(memory_space=pltpu.VMEM)

    def kernel(chunks, mix_ref, w_hbm, *refs):
        out_refs, (w_ref, sem) = refs[: len(pieces)], refs[len(pieces) :]
        copies = [weight_copies(chunks[j], w_hbm, w_ref.at[j], sem.at[j]) for j in range(count)]
        for copy in sum(copies, []):
            copy.start()
        for j in range(count):
            out = product(mix_ref, w_ref.at[j], copies[j])
            for (position, dtype, start, rows), out_ref in zip(pieces, out_refs):
                if position == j:
                    out_ref[...] = out[start : start + rows].astype(dtype)

    return pl.pallas_call(
        kernel,
        out_shape=tuple(jax.ShapeDtypeStruct((rows, cols), dtype) for _, dtype, _, rows in pieces),
        in_specs=[pl.BlockSpec(memory_space=pltpu.SMEM), vmem, pl.BlockSpec(memory_space=pltpu.HBM)],
        out_specs=(vmem,) * len(pieces),
        scratch_shapes=[pltpu.VMEM((count, inner, cols), BF16), pltpu.SemaphoreType.DMA((count, PARTS))],
        compiler_params=pltpu.CompilerParams(vmem_limit_bytes=32 << 20),
        name="project",
    )(chunks, mix, *in_hbm(w))


CORE_PAIR = [(0, 1), (1, 0), (2, 3), (3, 2)]
CHIP_PAIR = [(0, 2), (2, 0), (1, 3), (3, 1)]


def per_device(query_gate, gated_value, long_filter, out_weight):
    t = tables()
    me = lax.axis_index("ctx")
    mine = lax.axis_index("ch")
    tokens, width = gated_value.shape
    turned = turn(gated_value).reshape(HALF, GROUP, tokens)
    x = lax.all_to_all(turned, "ctx", 0, 0, tiled=True)
    spec = filter_spectrum(me.reshape(1), long_filter, t)
    y, w_first = convolve((mine ^ 3).reshape(1), x, spec, out_weight, t)
    y = lax.all_to_all(y, "ctx", 0, 0, tiled=True).reshape(width, tokens)
    mix, away_pair = gate_project(y, query_gate, w_first)
    away_in = lax.ppermute(away_pair, "ch", CORE_PAIR)
    (away_own,) = project((mine ^ 2).reshape(1), mix, out_weight, ((0, F32, 1),))
    away_sum = (away_own + away_in.astype(F32)).astype(BF16)
    mix, away_sum = lax.optimization_barrier((mix, away_sum))
    far = lax.ppermute(away_sum, "ch", CHIP_PAIR)
    *home_pair, home_own = project(jnp.stack([mine ^ 1, mine]), mix, out_weight, ((0, BF16, 2), (1, F32, 1)))
    near = jnp.concatenate([lax.ppermute(piece, "ch", CORE_PAIR) for piece in home_pair])
    return (home_own + near.astype(F32) + far.astype(F32)).astype(BF16)


def solution(mesh):
    placed = (P("ctx", "ch"), P("ctx", "ch"), P(None, "ch"), P("ch", None))
    return jax.shard_map(
        per_device, mesh=mesh, in_specs=placed, out_specs=P("ctx", "ch"), check_vma=False
    )
```

```python
import functools

import jax
import jax.numpy as jnp
import numpy as np
from jax import lax
from jax.experimental import pallas as pl
from jax.experimental.pallas import tpu as pltpu
from jax.sharding import PartitionSpec as P

SPAN = 128
BLOCKS = 64
HALF = BLOCKS // 2
LENGTH = SPAN * BLOCKS
GROUP = 32
SUB = 16
F32 = jnp.float32
BF16 = jnp.bfloat16


def tables():
    first = np.arange(BLOCKS)[:, None] + 0.25
    natural = np.arange(BLOCKS)[None, :]
    stored = np.concatenate([np.arange(HALF), BLOCKS - 1 - np.arange(HALF)])[None, :]

    def stage_a(order):
        angle = 2 * np.pi * first * order / BLOCKS
        return np.concatenate([np.cos(angle), -np.sin(angle)], 0)

    def stage_a_back(order):
        angle = (2 * np.pi * first * order / BLOCKS).T
        return np.concatenate([np.cos(angle), -np.sin(angle)], 1) / LENGTH

    twist = 2 * np.pi * first * np.arange(SPAN)[None, :] / LENGTH
    angle = 2 * np.pi * np.arange(SPAN)[:, None] * np.arange(SPAN)[None, :] / SPAN
    cos, sin = np.cos(angle), np.sin(angle)
    forth = np.block([[cos, -sin], [sin, cos]])
    back = np.block([[cos, sin], [-sin, cos]])
    rows = np.arange(HALF * SUB)
    swap = np.zeros((HALF * SUB, HALF * SUB))
    swap[(rows % SUB) * HALF + rows // SUB, rows] = 1.0
    bf = lambda a: jnp.asarray(a.astype(np.float32)).astype(BF16)
    return dict(
        a_filter=bf(stage_a(natural)),
        a_value=bf(stage_a(stored)),
        a_back=bf(stage_a_back(stored)),
        twist=jnp.asarray(np.concatenate([np.cos(twist), -np.sin(twist)], 1).astype(np.float32)),
        forth=bf(forth),
        back=bf(back),
        swap=bf(swap),
        unswap=bf(swap.T),
    )


def dot(left, right):
    return jnp.dot(left, right, preferred_element_type=F32)


def stage_a_rows(swapped, a_table, twist, mid_ref):
    t_re = jnp.concatenate([twist[:, :SPAN]] * 2, 1)
    t_im = jnp.concatenate([twist[:, SPAN:]] * 2, 1)
    for c in range(SUB):
        block = swapped[c * HALF : (c + 1) * HALF, :]
        rows = jnp.concatenate([block[:, : 2 * SPAN], block[:, 2 * SPAN :]], 0)
        spec = dot(a_table, rows)
        re, im = spec[:BLOCKS], spec[BLOCKS:]
        out_re = (re * t_re - im * t_im).astype(BF16)
        out_im = (re * t_im + im * t_re).astype(BF16)
        for g in range(2):
            at = (g * SUB + c) * BLOCKS
            mid_ref[at : at + BLOCKS, :SPAN] = out_re[:, g * SPAN : (g + 1) * SPAN]
            mid_ref[at : at + BLOCKS, SPAN:] = out_im[:, g * SPAN : (g + 1) * SPAN]


CHUNK = 512


SLABS = 8


def filter_kernel(
    which, h_hbm, a_hbm, twist_hbm, forth_hbm, swap_hbm, out_ref,
    slab_ref, a_ref, twist_ref, forth_ref, swap_ref, gather_ref, mid_ref, slab_sem, table_sem,
):
    lane_block = pl.multiple_of((which[0] // 4) * SPAN, SPAN)
    piece = LENGTH // SLABS
    slabs = [
        pltpu.make_async_copy(
            h_hbm.at[pl.ds(k * piece, piece), pl.ds(lane_block, SPAN)],
            slab_ref.at[pl.ds(k * piece, piece), :],
            slab_sem.at[k],
        )
        for k in range(SLABS)
    ]
    pairs = [(a_hbm, a_ref), (twist_hbm, twist_ref), (forth_hbm, forth_ref), (swap_hbm, swap_ref)]
    loads = [pltpu.make_async_copy(s, d, table_sem.at[k]) for k, (s, d) in enumerate(pairs)]
    for copy in slabs + loads:
        copy.start()
    offset = (which[0] % 4) * GROUP
    rows = lax.broadcasted_iota(jnp.int32, (GROUP, SPAN), 0)
    lanes = lax.broadcasted_iota(jnp.int32, (GROUP, SPAN), 1)
    pick = jnp.where(lanes == rows + offset, 1.0, 0.0).astype(BF16)
    for block in range(BLOCKS):
        if block % (BLOCKS // SLABS) == 0:
            slabs[block // (BLOCKS // SLABS)].wait()
        half, a = divmod(block, HALF)
        turned = lax.dot_general(
            pick, slab_ref[block * SPAN : (block + 1) * SPAN, :], (((1,), (1,)), ((), ())), preferred_element_type=F32
        ).astype(BF16)
        for g in range(2):
            lane = (half * 2 + g) * SPAN
            gather_ref[a * SUB : (a + 1) * SUB, lane : lane + SPAN] = turned[g * SUB : (g + 1) * SUB]
    for copy in loads:
        copy.wait()
    swapped = dot(swap_ref[...], gather_ref[...]).astype(BF16)
    stage_a_rows(swapped, a_ref[...], twist_ref[...], mid_ref)
    for k in range(GROUP * BLOCKS // CHUNK):
        part = slice(k * CHUNK, (k + 1) * CHUNK)
        out_ref[part, :] = dot(mid_ref[part, :], forth_ref[...]).astype(out_ref.dtype)


def conv_kernel(
    chunks, x_ref, spec_ref, a_ref, a_back_ref, twist_ref, forth_ref, back_ref, swap_ref, unswap_ref, w_hbm,
    out_ref, w_ref, mid_ref, turn_ref, sem,
):
    rows, cols = w_ref.shape[0] // PARTS, w_ref.shape[1]
    start = pl.multiple_of(chunks[0] * cols, cols)

    def weight_copy(k):
        part = pl.ds(pl.multiple_of(k * rows, rows), rows)
        return pltpu.make_async_copy(w_hbm.at[part, pl.ds(start, cols)], w_ref.at[part, :], sem.at[k])

    def begin(k, carry):
        weight_copy(k).start()
        return carry

    lax.fori_loop(0, PARTS, begin, 0)
    copies = [weight_copy(k) for k in range(PARTS)]
    pieces = []
    for half in range(2):
        for g in range(2):
            piece = x_ref[:, g * SUB : (g + 1) * SUB, half * SPAN : (half + 1) * SPAN]
            pieces.append(piece.reshape(HALF * SUB, SPAN))
    swapped = dot(swap_ref[...], jnp.concatenate(pieces, 1)).astype(BF16)
    twist = twist_ref[...]
    stage_a_rows(swapped, a_ref[...], twist, mid_ref)
    t_re = jnp.concatenate([twist[:, :SPAN]] * (CHUNK // BLOCKS), 0)
    t_im = jnp.concatenate([twist[:, SPAN:]] * (CHUNK // BLOCKS), 0)
    for k in range(GROUP * BLOCKS // CHUNK):
        part = slice(k * CHUNK, (k + 1) * CHUNK)
        spec = dot(mid_ref[part, :], forth_ref[...])
        x_re, x_im = spec[:, :SPAN], spec[:, SPAN:]
        h = spec_ref[part, :].astype(F32)
        h_re, h_im = h[:, :SPAN], h[:, SPAN:]
        prod = jnp.concatenate([x_re * h_re - x_im * h_im, x_re * h_im + x_im * h_re], 1).astype(BF16)
        turn = dot(prod, back_ref[...])
        re, im = turn[:, :SPAN], turn[:, SPAN:]
        mid_ref[part, :SPAN] = (re * t_re + im * t_im).astype(BF16)
        mid_ref[part, SPAN:] = (im * t_re - re * t_im).astype(BF16)
    for c in range(SUB):
        sides = []
        for g in range(2):
            at = (g * SUB + c) * BLOCKS
            sides.append(
                jnp.concatenate([mid_ref[at : at + BLOCKS, :SPAN], mid_ref[at : at + BLOCKS, SPAN:]], 0)
            )
        y = dot(a_back_ref[...], jnp.concatenate(sides, 1)).astype(BF16)
        turn_ref[c * HALF : (c + 1) * HALF, : 2 * SPAN] = y[:HALF]
        turn_ref[c * HALF : (c + 1) * HALF, 2 * SPAN :] = y[HALF:]
    result = dot(unswap_ref[...], turn_ref[...]).astype(BF16)
    for half in range(2):
        for g in range(2):
            lane = (half * 2 + g) * SPAN
            out_ref[:, g * SUB : (g + 1) * SUB, half * SPAN : (half + 1) * SPAN] = result[:, lane : lane + SPAN].reshape(
                HALF, SUB, SPAN
            )
    for copy in copies:
        copy.wait()


def in_hbm(*arrays):
    return tuple(pltpu.with_memory_space_constraint(a, pltpu.HBM) for a in arrays)


def filter_spectrum(which, long_filter, t):
    return pl.pallas_call(
        filter_kernel,
        out_shape=jax.ShapeDtypeStruct((GROUP * BLOCKS, 2 * SPAN), BF16),
        in_specs=[pl.BlockSpec(memory_space=pltpu.SMEM)] + [pl.BlockSpec(memory_space=pltpu.HBM)] * 5,
        out_specs=pl.BlockSpec(memory_space=pltpu.VMEM),
        scratch_shapes=[
            pltpu.VMEM((LENGTH, SPAN), BF16),
            pltpu.VMEM((2 * BLOCKS, BLOCKS), BF16),
            pltpu.VMEM((BLOCKS, 2 * SPAN), F32),
            pltpu.VMEM((2 * SPAN, 2 * SPAN), BF16),
            pltpu.VMEM((HALF * SUB, HALF * SUB), BF16),
            pltpu.VMEM((HALF * SUB, 4 * SPAN), BF16),
            pltpu.VMEM((GROUP * BLOCKS, 2 * SPAN), BF16),
            pltpu.SemaphoreType.DMA((SLABS,)),
            pltpu.SemaphoreType.DMA((4,)),
        ],
        compiler_params=pltpu.CompilerParams(vmem_limit_bytes=32 << 20),
        name="filter_spectrum",
    )(which, *in_hbm(long_filter, t["a_filter"], t["twist"], t["forth"], t["swap"]))


def convolve(chunks, x, spec, w, t):
    inner, cols = w.shape[0], w.shape[1] // 4
    vmem = pl.BlockSpec(memory_space=pltpu.VMEM)
    return pl.pallas_call(
        conv_kernel,
        out_shape=(pltpu.VMEM((HALF, GROUP, 2 * SPAN), BF16), pltpu.VMEM((inner, cols), BF16)),
        in_specs=[pl.BlockSpec(memory_space=pltpu.SMEM)] + [vmem] * 9 + [pl.BlockSpec(memory_space=pltpu.HBM)],
        out_specs=(vmem, vmem),
        scratch_shapes=[
            pltpu.VMEM((GROUP * BLOCKS, 2 * SPAN), BF16),
            pltpu.VMEM((HALF * SUB, 4 * SPAN), BF16),
            pltpu.SemaphoreType.DMA((PARTS,)),
        ],
        compiler_params=pltpu.CompilerParams(vmem_limit_bytes=32 << 20),
        name="convolve",
    )(
        chunks, x, spec, t["a_value"], t["a_back"], t["twist"], t["forth"], t["back"], t["swap"], t["unswap"], *in_hbm(w)
    )


def turn_kernel(v_hbm, out_ref, in_ref, sem):
    width = v_hbm.shape[1] // 4
    copies = [
        pltpu.make_async_copy(v_hbm.at[:, pl.ds(k * width, width)], in_ref.at[k], sem.at[k]) for k in range(4)
    ]
    for copy in copies:
        copy.start()
    for k in range(4):
        copies[k].wait()
        out_ref[k * width : (k + 1) * width, :] = jnp.transpose(in_ref[k], (1, 0))


def turn(v):
    tokens, width = v.shape
    return pl.pallas_call(
        turn_kernel,
        out_shape=pltpu.VMEM((width, tokens), BF16),
        in_specs=[pl.BlockSpec(memory_space=pltpu.HBM)],
        out_specs=pl.BlockSpec(memory_space=pltpu.VMEM),
        scratch_shapes=[pltpu.VMEM((4, tokens, width // 4), BF16), pltpu.SemaphoreType.DMA((4,))],
        compiler_params=pltpu.CompilerParams(vmem_limit_bytes=16 << 20),
        name="turn",
    )(*in_hbm(v))


PARTS = 4


def weight_copies(chunk, w_hbm, w_ref, sem):
    inner, cols = w_ref.shape
    rows = inner // PARTS
    start = pl.multiple_of(chunk * cols, cols)
    return [
        pltpu.make_async_copy(
            w_hbm.at[pl.ds(k * rows, rows), pl.ds(start, cols)], w_ref.at[pl.ds(k * rows, rows), :], sem.at[k]
        )
        for k in range(PARTS)
    ]


def product(mix_ref, w_ref, copies):
    rows = w_ref.shape[0] // PARTS
    total = None
    for k in range(PARTS):
        copies[k].wait()
        part = dot(mix_ref[:, k * rows : (k + 1) * rows], w_ref[k * rows : (k + 1) * rows, :])
        total = part if total is None else total + part
    return total


def gate_kernel(y_ref, gate_ref, w_ref, mix_ref, out_ref):
    turned = jnp.transpose(y_ref[...], (1, 0))
    mix = (gate_ref[...].astype(F32) * turned.astype(F32)).astype(BF16)
    mix_ref[...] = mix
    out_ref[...] = dot(mix, w_ref[...]).astype(BF16)


def gate_project(y, gate, w):
    tokens, cols = gate.shape[0], w.shape[1]
    return pl.pallas_call(
        gate_kernel,
        out_shape=(jax.ShapeDtypeStruct(gate.shape, BF16), jax.ShapeDtypeStruct((tokens, cols), BF16)),
        compiler_params=pltpu.CompilerParams(vmem_limit_bytes=32 << 20),
        name="gate_project",
    )(y, gate, w)


def project(chunks, mix, w, targets):
    tokens, inner, cols = mix.shape[0], w.shape[0], w.shape[1] // 4
    count = 1 + max(j for j, _, _ in targets)
    pieces = [(j, dtype, k * tokens // n, tokens // n) for j, dtype, n in targets for k in range(n)]
    vmem = pl.BlockSpec(memory_space=pltpu.VMEM)

    def kernel(chunks, mix_ref, w_hbm, *refs):
        out_refs, (w_ref, sem) = refs[: len(pieces)], refs[len(pieces) :]
        copies = [weight_copies(chunks[j], w_hbm, w_ref.at[j], sem.at[j]) for j in range(count)]
        for copy in sum(copies, []):
            copy.start()
        for j in range(count):
            out = product(mix_ref, w_ref.at[j], copies[j])
            for (position, dtype, start, rows), out_ref in zip(pieces, out_refs):
                if position == j:
                    out_ref[...] = out[start : start + rows].astype(dtype)

    return pl.pallas_call(
        kernel,
        out_shape=tuple(jax.ShapeDtypeStruct((rows, cols), dtype) for _, dtype, _, rows in pieces),
        in_specs=[pl.BlockSpec(memory_space=pltpu.SMEM), vmem, pl.BlockSpec(memory_space=pltpu.HBM)],
        out_specs=(vmem,) * len(pieces),
        scratch_shapes=[pltpu.VMEM((count, inner, cols), BF16), pltpu.SemaphoreType.DMA((count, PARTS))],
        compiler_params=pltpu.CompilerParams(vmem_limit_bytes=32 << 20),
        name="project",
    )(chunks, mix, *in_hbm(w))


def finish(home, near, far):
    tokens, cols = home.shape
    rows = tokens // PARTS
    each = near[0].shape[0]

    def kernel(home_ref, *refs):
        near_refs, (far_ref, out_hbm, sum_ref, sem) = refs[: len(near)], refs[len(near) :]
        copies = []
        for k in range(PARTS):
            part = slice(k * rows, (k + 1) * rows)
            piece, first = divmod(k * rows, each)
            other = near_refs[piece][first : first + rows, :]
            total = home_ref[part, :] + other.astype(F32) + far_ref[part, :].astype(F32)
            sum_ref[part, :] = total.astype(BF16)
            copy = pltpu.make_async_copy(
                sum_ref.at[pl.ds(k * rows, rows), :], out_hbm.at[pl.ds(k * rows, rows), :], sem.at[k]
            )
            copy.start()
            copies.append(copy)
        for copy in copies:
            copy.wait()

    return pl.pallas_call(
        kernel,
        out_shape=jax.ShapeDtypeStruct(home.shape, BF16),
        in_specs=[pl.BlockSpec(memory_space=pltpu.VMEM)] * (2 + len(near)),
        out_specs=pl.BlockSpec(memory_space=pltpu.HBM),
        scratch_shapes=[pltpu.VMEM(home.shape, BF16), pltpu.SemaphoreType.DMA((PARTS,))],
        compiler_params=pltpu.CompilerParams(vmem_limit_bytes=16 << 20),
        name="finish",
    )(home, *near, far)


CORE_PAIR = [(0, 1), (1, 0), (2, 3), (3, 2)]
CHIP_PAIR = [(0, 2), (2, 0), (1, 3), (3, 1)]


def per_device(query_gate, gated_value, long_filter, out_weight):
    t = tables()
    me = lax.axis_index("ctx")
    mine = lax.axis_index("ch")
    tokens, width = gated_value.shape
    turned = turn(gated_value).reshape(HALF, GROUP, tokens)
    x = lax.all_to_all(turned, "ctx", 0, 0, tiled=True)
    spec = filter_spectrum(me.reshape(1), long_filter, t)
    y, w_first = convolve((mine ^ 3).reshape(1), x, spec, out_weight, t)
    y = lax.all_to_all(y, "ctx", 0, 0, tiled=True).reshape(width, tokens)
    mix, away_pair = gate_project(y, query_gate, w_first)
    away_in = lax.ppermute(away_pair, "ch", CORE_PAIR)
    (away_own,) = project((mine ^ 2).reshape(1), mix, out_weight, ((0, F32, 1),))
    away_sum = (away_own + away_in.astype(F32)).astype(BF16)
    mix, away_sum = lax.optimization_barrier((mix, away_sum))
    far = lax.ppermute(away_sum, "ch", CHIP_PAIR)
    *home_pair, home_own = project(jnp.stack([mine ^ 1, mine]), mix, out_weight, ((0, BF16, 2), (1, F32, 1)))
    near = [lax.ppermute(piece, "ch", CORE_PAIR) for piece in home_pair]
    return finish(home_own, near, far)


def solution(mesh):
    placed = (P("ctx", "ch"), P("ctx", "ch"), P(None, "ch"), P("ch", None))
    return jax.shard_map(
        per_device, mesh=mesh, in_specs=placed, out_specs=P("ctx", "ch"), check_vma=False
    )
```

```python
import functools

import jax
import jax.numpy as jnp
import ml_dtypes
import numpy as np
from jax import lax
from jax.experimental import pallas as pl
from jax.experimental.pallas import tpu as pltpu
from jax.sharding import PartitionSpec as P

SPAN = 128
BLOCKS = 64
HALF = BLOCKS // 2
LENGTH = SPAN * BLOCKS
GROUP = 32
SUB = 16
F32 = jnp.float32
BF16 = jnp.bfloat16


def tables():
    first = np.arange(BLOCKS)[:, None] + 0.25
    natural = np.arange(BLOCKS)[None, :]
    stored = np.concatenate([np.arange(HALF), BLOCKS - 1 - np.arange(HALF)])[None, :]

    def stage_a(order):
        angle = 2 * np.pi * first * order / BLOCKS
        return np.concatenate([np.cos(angle), -np.sin(angle)], 0)

    def stage_a_back(order):
        angle = (2 * np.pi * first * order / BLOCKS).T
        return np.concatenate([np.cos(angle), -np.sin(angle)], 1) / LENGTH

    twist = 2 * np.pi * first * np.arange(SPAN)[None, :] / LENGTH
    angle = 2 * np.pi * np.arange(SPAN)[:, None] * np.arange(SPAN)[None, :] / SPAN
    cos, sin = np.cos(angle), np.sin(angle)
    forth = np.block([[cos, -sin], [sin, cos]])
    back = np.block([[cos, sin], [-sin, cos]])
    rows = np.arange(SUB * SUB)
    swap = np.zeros((SUB * SUB, SUB * SUB))
    swap[(rows % SUB) * SUB + rows // SUB, rows] = 1.0
    bf = lambda a: a.astype(np.float32).astype(ml_dtypes.bfloat16)

    def two(a):
        high = bf(a)
        return high, bf(a - high.astype(np.float64))

    made = dict(
        a_filter=np.concatenate(two(stage_a(natural)), 1),
        a_value=bf(stage_a(stored)),
        a_back=bf(stage_a_back(stored)),
        twist=np.concatenate([np.cos(twist), -np.sin(twist)], 1).astype(np.float32),
        forth=bf(forth),
        forth_rest=two(forth)[1],
        back=bf(back),
        swap=bf(swap),
    )
    return {name: jnp.asarray(table) for name, table in made.items()}


def dot(left, right):
    return jnp.dot(left, right, preferred_element_type=F32)


def lane_of(half, high, g):
    return ((half * 2 + high) * 2 + g) * SPAN


def stage_a_rows(swapped, a_table, twist, mid_ref):
    t_re = jnp.concatenate([twist[:, :SPAN]] * 2, 1)
    t_im = jnp.concatenate([twist[:, SPAN:]] * 2, 1)
    for c in range(SUB):
        block = swapped[c * SUB : (c + 1) * SUB, :]
        rows = jnp.concatenate([block[:, k * 2 * SPAN : (k + 1) * 2 * SPAN] for k in range(4)], 0)
        if a_table.shape[1] > BLOCKS:
            rows = jnp.concatenate([rows, rows], 0)
        spec = dot(a_table, rows)
        re, im = spec[:BLOCKS], spec[BLOCKS:]
        out_re = (re * t_re - im * t_im).astype(BF16)
        out_im = (re * t_im + im * t_re).astype(BF16)
        for g in range(2):
            at = (g * SUB + c) * BLOCKS
            mid_ref[at : at + BLOCKS, :SPAN] = out_re[:, g * SPAN : (g + 1) * SPAN]
            mid_ref[at : at + BLOCKS, SPAN:] = out_im[:, g * SPAN : (g + 1) * SPAN]


CHUNK = 512


SLABS = 8


def filter_kernel(
    which, h_hbm, a_hbm, twist_hbm, forth_hbm, rest_hbm, swap_hbm, out_ref,
    slab_ref, a_ref, twist_ref, forth_ref, rest_ref, swap_ref, gather_ref, mid_ref, slab_sem, table_sem,
):
    lane_block = pl.multiple_of((which[0] // 4) * SPAN, SPAN)
    piece = LENGTH // SLABS
    slabs = [
        pltpu.make_async_copy(
            h_hbm.at[pl.ds(k * piece, piece), pl.ds(lane_block, SPAN)],
            slab_ref.at[pl.ds(k * piece, piece), :],
            slab_sem.at[k],
        )
        for k in range(SLABS)
    ]
    pairs = [(a_hbm, a_ref), (twist_hbm, twist_ref), (forth_hbm, forth_ref), (rest_hbm, rest_ref), (swap_hbm, swap_ref)]
    loads = [pltpu.make_async_copy(s, d, table_sem.at[k]) for k, (s, d) in enumerate(pairs)]
    for copy in slabs + loads:
        copy.start()
    offset = (which[0] % 4) * GROUP
    rows = lax.broadcasted_iota(jnp.int32, (GROUP, SPAN), 0)
    lanes = lax.broadcasted_iota(jnp.int32, (GROUP, SPAN), 1)
    pick = jnp.where(lanes == rows + offset, 1.0, 0.0).astype(BF16)
    for block in range(BLOCKS):
        if block % (BLOCKS // SLABS) == 0:
            slabs[block // (BLOCKS // SLABS)].wait()
        half, high, a = block // HALF, block // SUB % 2, block % SUB
        turned = lax.dot_general(
            pick, slab_ref[block * SPAN : (block + 1) * SPAN, :], (((1,), (1,)), ((), ())), preferred_element_type=F32
        ).astype(BF16)
        for g in range(2):
            lane = lane_of(half, high, g)
            gather_ref[a * SUB : (a + 1) * SUB, lane : lane + SPAN] = turned[g * SUB : (g + 1) * SUB]
    for copy in loads:
        copy.wait()
    swapped = dot(swap_ref[...], gather_ref[...]).astype(BF16)
    stage_a_rows(swapped, a_ref[...], twist_ref[...], mid_ref)
    for k in range(GROUP * BLOCKS // CHUNK):
        part = slice(k * CHUNK, (k + 1) * CHUNK)
        mid = mid_ref[part, :]
        out_ref[part, :] = (dot(mid, forth_ref[...]) + dot(mid, rest_ref[...])).astype(out_ref.dtype)


def conv_kernel(
    chunks, x_ref, spec_ref, a_ref, a_back_ref, twist_ref, forth_ref, back_ref, swap_ref, w_hbm,
    out_ref, w_ref, mid_ref, turn_ref, sem,
):
    rows, cols = w_ref.shape[0] // PARTS, w_ref.shape[1]
    start = pl.multiple_of(chunks[0] * cols, cols)

    def weight_copy(k):
        part = pl.ds(pl.multiple_of(k * rows, rows), rows)
        return pltpu.make_async_copy(w_hbm.at[part, pl.ds(start, cols)], w_ref.at[part, :], sem.at[k])

    def begin(k, carry):
        weight_copy(k).start()
        return carry

    lax.fori_loop(0, PARTS, begin, 0)
    copies = [weight_copy(k) for k in range(PARTS)]
    pieces = []
    for half in range(2):
        for high in range(2):
            for g in range(2):
                piece = x_ref[
                    high * SUB : (high + 1) * SUB, g * SUB : (g + 1) * SUB, half * SPAN : (half + 1) * SPAN
                ]
                pieces.append(piece.reshape(SUB * SUB, SPAN))
    swapped = dot(swap_ref[...], jnp.concatenate(pieces, 1)).astype(BF16)
    twist = twist_ref[...]
    stage_a_rows(swapped, a_ref[...], twist, mid_ref)
    t_re = jnp.concatenate([twist[:, :SPAN]] * (CHUNK // BLOCKS), 0)
    t_im = jnp.concatenate([twist[:, SPAN:]] * (CHUNK // BLOCKS), 0)
    for k in range(GROUP * BLOCKS // CHUNK):
        part = slice(k * CHUNK, (k + 1) * CHUNK)
        spec = dot(mid_ref[part, :], forth_ref[...])
        x_re, x_im = spec[:, :SPAN], spec[:, SPAN:]
        h = spec_ref[part, :].astype(F32)
        h_re, h_im = h[:, :SPAN], h[:, SPAN:]
        prod = jnp.concatenate([x_re * h_re - x_im * h_im, x_re * h_im + x_im * h_re], 1).astype(BF16)
        turn = dot(prod, back_ref[...])
        re, im = turn[:, :SPAN], turn[:, SPAN:]
        mid_ref[part, :SPAN] = (re * t_re + im * t_im).astype(BF16)
        mid_ref[part, SPAN:] = (im * t_re - re * t_im).astype(BF16)
    for c in range(SUB):
        sides = []
        for g in range(2):
            at = (g * SUB + c) * BLOCKS
            sides.append(
                jnp.concatenate([mid_ref[at : at + BLOCKS, :SPAN], mid_ref[at : at + BLOCKS, SPAN:]], 0)
            )
        y = dot(a_back_ref[...], jnp.concatenate(sides, 1)).astype(BF16)
        for k in range(4):
            turn_ref[c * SUB : (c + 1) * SUB, k * 2 * SPAN : (k + 1) * 2 * SPAN] = y[k * SUB : (k + 1) * SUB]
    result = dot(swap_ref[...], turn_ref[...]).astype(BF16)
    for half in range(2):
        for high in range(2):
            for g in range(2):
                lane = lane_of(half, high, g)
                out_ref[
                    high * SUB : (high + 1) * SUB, g * SUB : (g + 1) * SUB, half * SPAN : (half + 1) * SPAN
                ] = result[:, lane : lane + SPAN].reshape(SUB, SUB, SPAN)
    for copy in copies:
        copy.wait()


def in_hbm(*arrays):
    return tuple(pltpu.with_memory_space_constraint(a, pltpu.HBM) for a in arrays)


def filter_spectrum(which, long_filter, t):
    return pl.pallas_call(
        filter_kernel,
        out_shape=jax.ShapeDtypeStruct((GROUP * BLOCKS, 2 * SPAN), BF16),
        in_specs=[pl.BlockSpec(memory_space=pltpu.SMEM)] + [pl.BlockSpec(memory_space=pltpu.HBM)] * 6,
        out_specs=pl.BlockSpec(memory_space=pltpu.VMEM),
        scratch_shapes=[
            pltpu.VMEM((LENGTH, SPAN), BF16),
            pltpu.VMEM((2 * BLOCKS, 2 * BLOCKS), BF16),
            pltpu.VMEM((BLOCKS, 2 * SPAN), F32),
            pltpu.VMEM((2 * SPAN, 2 * SPAN), BF16),
            pltpu.VMEM((2 * SPAN, 2 * SPAN), BF16),
            pltpu.VMEM((SUB * SUB, SUB * SUB), BF16),
            pltpu.VMEM((SUB * SUB, 8 * SPAN), BF16),
            pltpu.VMEM((GROUP * BLOCKS, 2 * SPAN), BF16),
            pltpu.SemaphoreType.DMA((SLABS,)),
            pltpu.SemaphoreType.DMA((5,)),
        ],
        compiler_params=pltpu.CompilerParams(vmem_limit_bytes=32 << 20),
        name="filter_spectrum",
    )(which, *in_hbm(long_filter, t["a_filter"], t["twist"], t["forth"], t["forth_rest"], t["swap"]))


def convolve(chunks, x, spec, w, t):
    inner, cols = w.shape[0], w.shape[1] // 4
    vmem = pl.BlockSpec(memory_space=pltpu.VMEM)
    return pl.pallas_call(
        conv_kernel,
        out_shape=(pltpu.VMEM((HALF, GROUP, 2 * SPAN), BF16), pltpu.VMEM((inner, cols), BF16)),
        in_specs=[pl.BlockSpec(memory_space=pltpu.SMEM)] + [vmem] * 8 + [pl.BlockSpec(memory_space=pltpu.HBM)],
        out_specs=(vmem, vmem),
        scratch_shapes=[
            pltpu.VMEM((GROUP * BLOCKS, 2 * SPAN), BF16),
            pltpu.VMEM((SUB * SUB, 8 * SPAN), BF16),
            pltpu.SemaphoreType.DMA((PARTS,)),
        ],
        compiler_params=pltpu.CompilerParams(vmem_limit_bytes=32 << 20),
        name="convolve",
    )(
        chunks, x, spec, t["a_value"], t["a_back"], t["twist"], t["forth"], t["back"], t["swap"], *in_hbm(w)
    )


def turn_kernel(v_hbm, out_ref, in_ref, sem):
    width = v_hbm.shape[1] // 4
    copies = [
        pltpu.make_async_copy(v_hbm.at[:, pl.ds(k * width, width)], in_ref.at[k], sem.at[k]) for k in range(4)
    ]
    for copy in copies:
        copy.start()
    for k in range(4):
        copies[k].wait()
        out_ref[k * width : (k + 1) * width, :] = jnp.transpose(in_ref[k], (1, 0))


def turn(v):
    tokens, width = v.shape
    return pl.pallas_call(
        turn_kernel,
        out_shape=pltpu.VMEM((width, tokens), BF16),
        in_specs=[pl.BlockSpec(memory_space=pltpu.HBM)],
        out_specs=pl.BlockSpec(memory_space=pltpu.VMEM),
        scratch_shapes=[pltpu.VMEM((4, tokens, width // 4), BF16), pltpu.SemaphoreType.DMA((4,))],
        compiler_params=pltpu.CompilerParams(vmem_limit_bytes=16 << 20),
        name="turn",
    )(*in_hbm(v))


PARTS = 4


def weight_copies(chunk, w_hbm, w_ref, sem):
    inner, cols = w_ref.shape
    rows = inner // PARTS
    start = pl.multiple_of(chunk * cols, cols)
    return [
        pltpu.make_async_copy(
            w_hbm.at[pl.ds(k * rows, rows), pl.ds(start, cols)], w_ref.at[pl.ds(k * rows, rows), :], sem.at[k]
        )
        for k in range(PARTS)
    ]


def product(mix_ref, w_ref, copies):
    rows = w_ref.shape[0] // PARTS
    total = None
    for k in range(PARTS):
        copies[k].wait()
        part = dot(mix_ref[:, k * rows : (k + 1) * rows], w_ref[k * rows : (k + 1) * rows, :])
        total = part if total is None else total + part
    return total


def gate_kernel(y_ref, gate_ref, w_ref, mix_ref, out_ref):
    turned = jnp.transpose(y_ref[...], (1, 0))
    mix = (gate_ref[...].astype(F32) * turned.astype(F32)).astype(BF16)
    mix_ref[...] = mix
    out_ref[...] = dot(mix, w_ref[...]).astype(BF16)


def gate_project(y, gate, w):
    tokens, cols = gate.shape[0], w.shape[1]
    return pl.pallas_call(
        gate_kernel,
        out_shape=(jax.ShapeDtypeStruct(gate.shape, BF16), jax.ShapeDtypeStruct((tokens, cols), BF16)),
        compiler_params=pltpu.CompilerParams(vmem_limit_bytes=32 << 20),
        name="gate_project",
    )(y, gate, w)


def project(chunks, mix, w, targets):
    tokens, inner, cols = mix.shape[0], w.shape[0], w.shape[1] // 4
    count = 1 + max(j for j, _, _ in targets)
    pieces = [(j, dtype, k * tokens // n, tokens // n) for j, dtype, n in targets for k in range(n)]
    vmem = pl.BlockSpec(memory_space=pltpu.VMEM)

    def kernel(chunks, mix_ref, w_hbm, *refs):
        out_refs, (w_ref, sem) = refs[: len(pieces)], refs[len(pieces) :]
        copies = [weight_copies(chunks[j], w_hbm, w_ref.at[j], sem.at[j]) for j in range(count)]
        for copy in sum(copies, []):
            copy.start()
        for j in range(count):
            out = product(mix_ref, w_ref.at[j], copies[j])
            for (position, dtype, start, rows), out_ref in zip(pieces, out_refs):
                if position == j:
                    out_ref[...] = out[start : start + rows].astype(dtype)

    return pl.pallas_call(
        kernel,
        out_shape=tuple(jax.ShapeDtypeStruct((rows, cols), dtype) for _, dtype, _, rows in pieces),
        in_specs=[pl.BlockSpec(memory_space=pltpu.SMEM), vmem, pl.BlockSpec(memory_space=pltpu.HBM)],
        out_specs=(vmem,) * len(pieces),
        scratch_shapes=[pltpu.VMEM((count, inner, cols), BF16), pltpu.SemaphoreType.DMA((count, PARTS))],
        compiler_params=pltpu.CompilerParams(vmem_limit_bytes=32 << 20),
        name="project",
    )(chunks, mix, *in_hbm(w))


def finish(home, near, far):
    tokens, cols = home.shape
    rows = tokens // PARTS
    each = near[0].shape[0]

    def kernel(home_ref, *refs):
        near_refs, (far_ref, out_hbm, sum_ref, sem) = refs[: len(near)], refs[len(near) :]
        copies = []
        for k in range(PARTS):
            part = slice(k * rows, (k + 1) * rows)
            piece, first = divmod(k * rows, each)
            other = near_refs[piece][first : first + rows, :]
            total = home_ref[part, :] + other.astype(F32) + far_ref[part, :].astype(F32)
            sum_ref[part, :] = total.astype(BF16)
            copy = pltpu.make_async_copy(
                sum_ref.at[pl.ds(k * rows, rows), :], out_hbm.at[pl.ds(k * rows, rows), :], sem.at[k]
            )
            copy.start()
            copies.append(copy)
        for copy in copies:
            copy.wait()

    return pl.pallas_call(
        kernel,
        out_shape=jax.ShapeDtypeStruct(home.shape, BF16),
        in_specs=[pl.BlockSpec(memory_space=pltpu.VMEM)] * (2 + len(near)),
        out_specs=pl.BlockSpec(memory_space=pltpu.HBM),
        scratch_shapes=[pltpu.VMEM(home.shape, BF16), pltpu.SemaphoreType.DMA((PARTS,))],
        compiler_params=pltpu.CompilerParams(vmem_limit_bytes=16 << 20),
        name="finish",
    )(home, *near, far)


CORE_PAIR = [(0, 1), (1, 0), (2, 3), (3, 2)]
CHIP_PAIR = [(0, 2), (2, 0), (1, 3), (3, 1)]


def per_device(query_gate, gated_value, long_filter, out_weight):
    t = tables()
    me = lax.axis_index("ctx")
    mine = lax.axis_index("ch")
    tokens, width = gated_value.shape
    turned = turn(gated_value).reshape(HALF, GROUP, tokens)
    x = lax.all_to_all(turned, "ctx", 0, 0, tiled=True)
    spec = filter_spectrum(me.reshape(1), long_filter, t)
    y, w_first = convolve((mine ^ 3).reshape(1), x, spec, out_weight, t)
    y = lax.all_to_all(y, "ctx", 0, 0, tiled=True).reshape(width, tokens)
    mix, away_pair = gate_project(y, query_gate, w_first)
    away_in = lax.ppermute(away_pair, "ch", CORE_PAIR)
    (away_own,) = project((mine ^ 2).reshape(1), mix, out_weight, ((0, F32, 1),))
    away_sum = (away_own + away_in.astype(F32)).astype(BF16)
    mix, away_sum = lax.optimization_barrier((mix, away_sum))
    far = lax.ppermute(away_sum, "ch", CHIP_PAIR)
    *home_pair, home_own = project(jnp.stack([mine ^ 1, mine]), mix, out_weight, ((0, BF16, 2), (1, F32, 1)))
    near = [lax.ppermute(piece, "ch", CORE_PAIR) for piece in home_pair]
    return finish(home_own, near, far)


def solution(mesh):
    placed = (P("ctx", "ch"), P("ctx", "ch"), P(None, "ch"), P("ch", None))
    return jax.shard_map(
        per_device, mesh=mesh, in_specs=placed, out_specs=P("ctx", "ch"), check_vma=False
    )
```

```python
import functools

import jax
import jax.numpy as jnp
import ml_dtypes
import numpy as np
from jax import lax
from jax.experimental import pallas as pl
from jax.experimental.pallas import tpu as pltpu
from jax.sharding import PartitionSpec as P

SPAN = 128
BLOCKS = 64
HALF = BLOCKS // 2
LENGTH = SPAN * BLOCKS
GROUP = 32
SUB = 16
F32 = jnp.float32
BF16 = jnp.bfloat16


def tables():
    first = np.arange(BLOCKS)[:, None] + 0.25
    natural = np.arange(BLOCKS)[None, :]
    stored = np.concatenate([np.arange(HALF), BLOCKS - 1 - np.arange(HALF)])[None, :]

    def stage_a(order):
        angle = 2 * np.pi * first * order / BLOCKS
        return np.concatenate([np.cos(angle), -np.sin(angle)], 0)

    def stage_a_back(order):
        angle = (2 * np.pi * first * order / BLOCKS).T
        return np.concatenate([np.cos(angle), -np.sin(angle)], 1) / LENGTH

    twist = 2 * np.pi * first * np.arange(SPAN)[None, :] / LENGTH
    angle = 2 * np.pi * np.arange(SPAN)[:, None] * np.arange(SPAN)[None, :] / SPAN
    cos, sin = np.cos(angle), np.sin(angle)
    forth = np.block([[cos, -sin], [sin, cos]])
    back = np.block([[cos, sin], [-sin, cos]])
    rows = np.arange(SUB * SUB)
    swap = np.zeros((SUB * SUB, SUB * SUB))
    swap[(rows % SUB) * SUB + rows // SUB, rows] = 1.0
    bf = lambda a: a.astype(np.float32).astype(ml_dtypes.bfloat16)

    def two(a):
        high = bf(a)
        return high, bf(a - high.astype(np.float64))

    made = dict(
        a_filter=np.concatenate(two(stage_a(natural)), 1),
        a_value=bf(stage_a(stored)),
        a_back=bf(stage_a_back(stored)),
        twist=np.concatenate([np.cos(twist), -np.sin(twist)], 1).astype(np.float32),
        forth=bf(forth),
        forth_rest=two(forth)[1],
        back=bf(back),
        swap=bf(swap),
    )
    return {name: jnp.asarray(table) for name, table in made.items()}


def dot(left, right):
    return jnp.dot(left, right, preferred_element_type=F32)


def lane_of(half, high, g):
    return ((half * 2 + high) * 2 + g) * SPAN


def stage_a_rows(swapped, a_table, twist, mid_ref):
    t_re = jnp.concatenate([twist[:, :SPAN]] * 2, 1)
    t_im = jnp.concatenate([twist[:, SPAN:]] * 2, 1)
    for c in range(SUB):
        block = swapped[c * SUB : (c + 1) * SUB, :]
        rows = jnp.concatenate([block[:, k * 2 * SPAN : (k + 1) * 2 * SPAN] for k in range(4)], 0)
        if a_table.shape[1] > BLOCKS:
            rows = jnp.concatenate([rows, rows], 0)
        spec = dot(a_table, rows)
        re, im = spec[:BLOCKS], spec[BLOCKS:]
        out_re = (re * t_re - im * t_im).astype(BF16)
        out_im = (re * t_im + im * t_re).astype(BF16)
        for g in range(2):
            at = (g * SUB + c) * BLOCKS
            mid_ref[at : at + BLOCKS, :SPAN] = out_re[:, g * SPAN : (g + 1) * SPAN]
            mid_ref[at : at + BLOCKS, SPAN:] = out_im[:, g * SPAN : (g + 1) * SPAN]


CHUNK = 512


SLABS = 8


def filter_kernel(
    which, h_hbm, a_hbm, twist_hbm, forth_hbm, rest_hbm, swap_hbm, out_ref,
    slab_ref, a_ref, twist_ref, forth_ref, rest_ref, swap_ref, gather_ref, mid_ref, slab_sem, table_sem,
):
    lane_block = pl.multiple_of((which[0] // 4) * SPAN, SPAN)
    piece = LENGTH // SLABS
    slabs = [
        pltpu.make_async_copy(
            h_hbm.at[pl.ds(k * piece, piece), pl.ds(lane_block, SPAN)],
            slab_ref.at[pl.ds(k * piece, piece), :],
            slab_sem.at[k],
        )
        for k in range(SLABS)
    ]
    pairs = [(a_hbm, a_ref), (twist_hbm, twist_ref), (forth_hbm, forth_ref), (rest_hbm, rest_ref), (swap_hbm, swap_ref)]
    loads = [pltpu.make_async_copy(s, d, table_sem.at[k]) for k, (s, d) in enumerate(pairs)]
    for copy in slabs + loads:
        copy.start()
    offset = (which[0] % 4) * GROUP
    rows = lax.broadcasted_iota(jnp.int32, (GROUP, SPAN), 0)
    lanes = lax.broadcasted_iota(jnp.int32, (GROUP, SPAN), 1)
    pick = jnp.where(lanes == rows + offset, 1.0, 0.0).astype(BF16)
    for block in range(BLOCKS):
        if block % (BLOCKS // SLABS) == 0:
            slabs[block // (BLOCKS // SLABS)].wait()
        half, high, a = block // HALF, block // SUB % 2, block % SUB
        turned = lax.dot_general(
            pick, slab_ref[block * SPAN : (block + 1) * SPAN, :], (((1,), (1,)), ((), ())), preferred_element_type=F32
        ).astype(BF16)
        for g in range(2):
            lane = lane_of(half, high, g)
            gather_ref[a * SUB : (a + 1) * SUB, lane : lane + SPAN] = turned[g * SUB : (g + 1) * SUB]
    for copy in loads:
        copy.wait()
    swapped = dot(swap_ref[...], gather_ref[...]).astype(BF16)
    stage_a_rows(swapped, a_ref[...], twist_ref[...], mid_ref)
    for k in range(GROUP * BLOCKS // CHUNK):
        part = slice(k * CHUNK, (k + 1) * CHUNK)
        mid = mid_ref[part, :]
        out_ref[part, :] = (dot(mid, forth_ref[...]) + dot(mid, rest_ref[...])).astype(out_ref.dtype)


def conv_kernel(
    chunks, x_ref, spec_ref, a_ref, a_back_ref, twist_ref, forth_ref, back_ref, swap_ref, w_hbm,
    out_ref, w_ref, mid_ref, turn_ref, sem,
):
    rows, cols = w_ref.shape[0] // PARTS, w_ref.shape[1]
    start = pl.multiple_of(chunks[0] * cols, cols)

    def weight_copy(k):
        part = pl.ds(pl.multiple_of(k * rows, rows), rows)
        return pltpu.make_async_copy(w_hbm.at[part, pl.ds(start, cols)], w_ref.at[part, :], sem.at[k])

    def begin(k, carry):
        weight_copy(k).start()
        return carry

    lax.fori_loop(0, PARTS, begin, 0)
    copies = [weight_copy(k) for k in range(PARTS)]
    pieces = []
    for half in range(2):
        for high in range(2):
            for g in range(2):
                piece = x_ref[
                    high * SUB : (high + 1) * SUB, g * SUB : (g + 1) * SUB, half * SPAN : (half + 1) * SPAN
                ]
                pieces.append(piece.reshape(SUB * SUB, SPAN))
    swapped = dot(swap_ref[...], jnp.concatenate(pieces, 1)).astype(BF16)
    twist = twist_ref[...]
    stage_a_rows(swapped, a_ref[...], twist, mid_ref)
    t_re = jnp.concatenate([twist[:, :SPAN]] * (CHUNK // BLOCKS), 0)
    t_im = jnp.concatenate([twist[:, SPAN:]] * (CHUNK // BLOCKS), 0)
    for k in range(GROUP * BLOCKS // CHUNK):
        part = slice(k * CHUNK, (k + 1) * CHUNK)
        spec = dot(mid_ref[part, :], forth_ref[...])
        x_re, x_im = spec[:, :SPAN], spec[:, SPAN:]
        h = spec_ref[part, :].astype(F32)
        h_re, h_im = h[:, :SPAN], h[:, SPAN:]
        prod = jnp.concatenate([x_re * h_re - x_im * h_im, x_re * h_im + x_im * h_re], 1).astype(BF16)
        turn = dot(prod, back_ref[...])
        re, im = turn[:, :SPAN], turn[:, SPAN:]
        mid_ref[part, :SPAN] = (re * t_re + im * t_im).astype(BF16)
        mid_ref[part, SPAN:] = (im * t_re - re * t_im).astype(BF16)
    for c in range(SUB):
        sides = []
        for g in range(2):
            at = (g * SUB + c) * BLOCKS
            sides.append(
                jnp.concatenate([mid_ref[at : at + BLOCKS, :SPAN], mid_ref[at : at + BLOCKS, SPAN:]], 0)
            )
        y = dot(a_back_ref[...], jnp.concatenate(sides, 1)).astype(BF16)
        for k in range(4):
            turn_ref[c * SUB : (c + 1) * SUB, k * 2 * SPAN : (k + 1) * 2 * SPAN] = y[k * SUB : (k + 1) * SUB]
    result = dot(swap_ref[...], turn_ref[...]).astype(BF16)
    for half in range(2):
        for high in range(2):
            for g in range(2):
                lane = lane_of(half, high, g)
                out_ref[
                    high * SUB : (high + 1) * SUB, g * SUB : (g + 1) * SUB, half * SPAN : (half + 1) * SPAN
                ] = result[:, lane : lane + SPAN].reshape(SUB, SUB, SPAN)
    for copy in copies:
        copy.wait()


def in_hbm(*arrays):
    return tuple(pltpu.with_memory_space_constraint(a, pltpu.HBM) for a in arrays)


def filter_spectrum(which, long_filter, t):
    return pl.pallas_call(
        filter_kernel,
        out_shape=jax.ShapeDtypeStruct((GROUP * BLOCKS, 2 * SPAN), BF16),
        in_specs=[pl.BlockSpec(memory_space=pltpu.SMEM)] + [pl.BlockSpec(memory_space=pltpu.HBM)] * 6,
        out_specs=pl.BlockSpec(memory_space=pltpu.VMEM),
        scratch_shapes=[
            pltpu.VMEM((LENGTH, SPAN), BF16),
            pltpu.VMEM((2 * BLOCKS, 2 * BLOCKS), BF16),
            pltpu.VMEM((BLOCKS, 2 * SPAN), F32),
            pltpu.VMEM((2 * SPAN, 2 * SPAN), BF16),
            pltpu.VMEM((2 * SPAN, 2 * SPAN), BF16),
            pltpu.VMEM((SUB * SUB, SUB * SUB), BF16),
            pltpu.VMEM((SUB * SUB, 8 * SPAN), BF16),
            pltpu.VMEM((GROUP * BLOCKS, 2 * SPAN), BF16),
            pltpu.SemaphoreType.DMA((SLABS,)),
            pltpu.SemaphoreType.DMA((5,)),
        ],
        compiler_params=pltpu.CompilerParams(vmem_limit_bytes=32 << 20),
        name="filter_spectrum",
    )(which, *in_hbm(long_filter, t["a_filter"], t["twist"], t["forth"], t["forth_rest"], t["swap"]))


def convolve(chunks, x, spec, w, t):
    inner, cols = w.shape[0], w.shape[1] // 4
    vmem = pl.BlockSpec(memory_space=pltpu.VMEM)
    return pl.pallas_call(
        conv_kernel,
        out_shape=(pltpu.VMEM((HALF, GROUP, 2 * SPAN), BF16), pltpu.VMEM((inner, cols), BF16)),
        in_specs=[pl.BlockSpec(memory_space=pltpu.SMEM)] + [vmem] * 8 + [pl.BlockSpec(memory_space=pltpu.HBM)],
        out_specs=(vmem, vmem),
        scratch_shapes=[
            pltpu.VMEM((GROUP * BLOCKS, 2 * SPAN), BF16),
            pltpu.VMEM((SUB * SUB, 8 * SPAN), BF16),
            pltpu.SemaphoreType.DMA((PARTS,)),
        ],
        compiler_params=pltpu.CompilerParams(vmem_limit_bytes=32 << 20),
        name="convolve",
    )(
        chunks, x, spec, t["a_value"], t["a_back"], t["twist"], t["forth"], t["back"], t["swap"], *in_hbm(w)
    )


TURN = 2


def turn_kernel(v_hbm, out_hbm, in_ref, turned_ref, in_sem, out_sem):
    width = v_hbm.shape[1] // TURN
    loads = [
        pltpu.make_async_copy(v_hbm.at[:, pl.ds(k * width, width)], in_ref.at[k], in_sem.at[k]) for k in range(TURN)
    ]
    stores = [
        pltpu.make_async_copy(turned_ref.at[k], out_hbm.at[pl.ds(k * width, width), :], out_sem.at[k])
        for k in range(TURN)
    ]
    for load in loads:
        load.start()
    for k in range(TURN):
        loads[k].wait()
        turned_ref[k] = jnp.transpose(in_ref[k], (1, 0))
        stores[k].start()
    for store in stores:
        store.wait()


def turn(v):
    tokens, width = v.shape
    hbm = pl.BlockSpec(memory_space=pltpu.HBM)
    return pl.pallas_call(
        turn_kernel,
        out_shape=jax.ShapeDtypeStruct((width, tokens), BF16),
        in_specs=[hbm],
        out_specs=hbm,
        scratch_shapes=[
            pltpu.VMEM((TURN, tokens, width // TURN), BF16),
            pltpu.VMEM((TURN, width // TURN, tokens), BF16),
            pltpu.SemaphoreType.DMA((TURN,)),
            pltpu.SemaphoreType.DMA((TURN,)),
        ],
        compiler_params=pltpu.CompilerParams(vmem_limit_bytes=16 << 20),
        name="turn",
    )(*in_hbm(v))


PARTS = 4


def weight_copies(chunk, w_hbm, w_ref, sem):
    inner, cols = w_ref.shape
    rows = inner // PARTS
    start = pl.multiple_of(chunk * cols, cols)
    return [
        pltpu.make_async_copy(
            w_hbm.at[pl.ds(k * rows, rows), pl.ds(start, cols)], w_ref.at[pl.ds(k * rows, rows), :], sem.at[k]
        )
        for k in range(PARTS)
    ]


def product(mix_ref, w_ref, copies):
    rows = w_ref.shape[0] // PARTS
    total = None
    for k in range(PARTS):
        copies[k].wait()
        part = dot(mix_ref[:, k * rows : (k + 1) * rows], w_ref[k * rows : (k + 1) * rows, :])
        total = part if total is None else total + part
    return total


def gate_kernel(y_ref, gate_ref, w_ref, mix_ref, out_ref):
    turned = jnp.transpose(y_ref[...], (1, 0))
    mix = (gate_ref[...].astype(F32) * turned.astype(F32)).astype(BF16)
    mix_ref[...] = mix
    out_ref[...] = dot(mix, w_ref[...]).astype(BF16)


def gate_project(y, gate, w):
    tokens, cols = gate.shape[0], w.shape[1]
    return pl.pallas_call(
        gate_kernel,
        out_shape=(jax.ShapeDtypeStruct(gate.shape, BF16), jax.ShapeDtypeStruct((tokens, cols), BF16)),
        compiler_params=pltpu.CompilerParams(vmem_limit_bytes=32 << 20),
        name="gate_project",
    )(y, gate, w)


def project(chunks, mix, w, targets):
    tokens, inner, cols = mix.shape[0], w.shape[0], w.shape[1] // 4
    count = 1 + max(j for j, _, _ in targets)
    pieces = [(j, dtype, k * tokens // n, tokens // n) for j, dtype, n in targets for k in range(n)]
    vmem = pl.BlockSpec(memory_space=pltpu.VMEM)

    def kernel(chunks, mix_ref, w_hbm, *refs):
        out_refs, (w_ref, sem) = refs[: len(pieces)], refs[len(pieces) :]
        copies = [weight_copies(chunks[j], w_hbm, w_ref.at[j], sem.at[j]) for j in range(count)]
        for copy in sum(copies, []):
            copy.start()
        for j in range(count):
            out = product(mix_ref, w_ref.at[j], copies[j])
            for (position, dtype, start, rows), out_ref in zip(pieces, out_refs):
                if position == j:
                    out_ref[...] = out[start : start + rows].astype(dtype)

    return pl.pallas_call(
        kernel,
        out_shape=tuple(jax.ShapeDtypeStruct((rows, cols), dtype) for _, dtype, _, rows in pieces),
        in_specs=[pl.BlockSpec(memory_space=pltpu.SMEM), vmem, pl.BlockSpec(memory_space=pltpu.HBM)],
        out_specs=(vmem,) * len(pieces),
        scratch_shapes=[pltpu.VMEM((count, inner, cols), BF16), pltpu.SemaphoreType.DMA((count, PARTS))],
        compiler_params=pltpu.CompilerParams(vmem_limit_bytes=32 << 20),
        name="project",
    )(chunks, mix, *in_hbm(w))


def finish(home, near, far):
    tokens, cols = home.shape
    rows = tokens // PARTS
    each = near[0].shape[0]

    def kernel(home_ref, *refs):
        near_refs, (far_ref, out_hbm, sum_ref, sem) = refs[: len(near)], refs[len(near) :]
        copies = []
        for k in range(PARTS):
            part = slice(k * rows, (k + 1) * rows)
            piece, first = divmod(k * rows, each)
            other = near_refs[piece][first : first + rows, :]
            total = home_ref[part, :] + other.astype(F32) + far_ref[part, :].astype(F32)
            sum_ref[part, :] = total.astype(BF16)
            copy = pltpu.make_async_copy(
                sum_ref.at[pl.ds(k * rows, rows), :], out_hbm.at[pl.ds(k * rows, rows), :], sem.at[k]
            )
            copy.start()
            copies.append(copy)
        for copy in copies:
            copy.wait()

    return pl.pallas_call(
        kernel,
        out_shape=jax.ShapeDtypeStruct(home.shape, BF16),
        in_specs=[pl.BlockSpec(memory_space=pltpu.VMEM)] * (2 + len(near)),
        out_specs=pl.BlockSpec(memory_space=pltpu.HBM),
        scratch_shapes=[pltpu.VMEM(home.shape, BF16), pltpu.SemaphoreType.DMA((PARTS,))],
        compiler_params=pltpu.CompilerParams(vmem_limit_bytes=16 << 20),
        name="finish",
    )(home, *near, far)


CORE_PAIR = [(0, 1), (1, 0), (2, 3), (3, 2)]
CHIP_PAIR = [(0, 2), (2, 0), (1, 3), (3, 1)]


def per_device(query_gate, gated_value, long_filter, out_weight):
    t = tables()
    me = lax.axis_index("ctx")
    mine = lax.axis_index("ch")
    tokens, width = gated_value.shape
    turned = turn(gated_value).reshape(HALF, GROUP, tokens)
    x = lax.all_to_all(turned, "ctx", 0, 0, tiled=True)
    spec = filter_spectrum(me.reshape(1), long_filter, t)
    y, w_first = convolve((mine ^ 3).reshape(1), x, spec, out_weight, t)
    y = lax.all_to_all(y, "ctx", 0, 0, tiled=True).reshape(width, tokens)
    mix, away_pair = gate_project(y, query_gate, w_first)
    away_in = lax.ppermute(away_pair, "ch", CORE_PAIR)
    (away_own,) = project((mine ^ 2).reshape(1), mix, out_weight, ((0, F32, 1),))
    away_sum = (away_own + away_in.astype(F32)).astype(BF16)
    mix, away_sum = lax.optimization_barrier((mix, away_sum))
    far = lax.ppermute(away_sum, "ch", CHIP_PAIR)
    *home_pair, home_own = project(jnp.stack([mine ^ 1, mine]), mix, out_weight, ((0, BF16, 2), (1, F32, 1)))
    near = [lax.ppermute(piece, "ch", CORE_PAIR) for piece in home_pair]
    return finish(home_own, near, far)


def solution(mesh):
    placed = (P("ctx", "ch"), P("ctx", "ch"), P(None, "ch"), P("ch", None))
    return jax.shard_map(
        per_device, mesh=mesh, in_specs=placed, out_specs=P("ctx", "ch"), check_vma=False
    )
```

```python
import functools

import jax
import jax.numpy as jnp
import ml_dtypes
import numpy as np
from jax import lax
from jax.experimental import pallas as pl
from jax.experimental.pallas import tpu as pltpu
from jax.sharding import PartitionSpec as P

SPAN = 128
BLOCKS = 64
HALF = BLOCKS // 2
LENGTH = SPAN * BLOCKS
GROUP = 32
SUB = 16
F32 = jnp.float32
BF16 = jnp.bfloat16


def tables():
    first = np.arange(BLOCKS)[:, None] + 0.25
    natural = np.arange(BLOCKS)[None, :]
    stored = np.concatenate([np.arange(HALF), BLOCKS - 1 - np.arange(HALF)])[None, :]

    def stage_a(order):
        angle = 2 * np.pi * first * order / BLOCKS
        return np.concatenate([np.cos(angle), -np.sin(angle)], 0)

    def stage_a_back(order):
        angle = (2 * np.pi * first * order / BLOCKS).T
        return np.concatenate([np.cos(angle), -np.sin(angle)], 1) / LENGTH

    twist = 2 * np.pi * first * np.arange(SPAN)[None, :] / LENGTH
    angle = 2 * np.pi * np.arange(SPAN)[:, None] * np.arange(SPAN)[None, :] / SPAN
    cos, sin = np.cos(angle), np.sin(angle)
    forth = np.block([[cos, -sin], [sin, cos]])
    back = np.block([[cos, sin], [-sin, cos]])
    rows = np.arange(SUB * SUB)
    swap = np.zeros((SUB * SUB, SUB * SUB))
    swap[(rows % SUB) * SUB + rows // SUB, rows] = 1.0
    bf = lambda a: a.astype(np.float32).astype(ml_dtypes.bfloat16)

    def two(a):
        high = bf(a)
        return high, bf(a - high.astype(np.float64))

    made = dict(
        a_filter=np.concatenate(two(stage_a(natural)), 1),
        a_value=bf(stage_a(stored)),
        a_back=bf(stage_a_back(stored)),
        twist=np.concatenate([np.cos(twist), -np.sin(twist)], 1).astype(np.float32),
        forth=bf(forth),
        forth_rest=two(forth)[1],
        back=bf(back),
        swap=bf(swap),
    )
    return {name: jnp.asarray(table) for name, table in made.items()}


def dot(left, right):
    return jnp.dot(left, right, preferred_element_type=F32)


def lane_of(half, high, g):
    return ((half * 2 + high) * 2 + g) * SPAN


def stage_a_rows(swapped, a_table, twist, mid_ref):
    t_re = jnp.concatenate([twist[:, :SPAN]] * 2, 1)
    t_im = jnp.concatenate([twist[:, SPAN:]] * 2, 1)
    for c in range(SUB):
        block = swapped[c * SUB : (c + 1) * SUB, :]
        rows = jnp.concatenate([block[:, k * 2 * SPAN : (k + 1) * 2 * SPAN] for k in range(4)], 0)
        if a_table.shape[1] > BLOCKS:
            rows = jnp.concatenate([rows, rows], 0)
        spec = dot(a_table, rows)
        re, im = spec[:BLOCKS], spec[BLOCKS:]
        out_re = (re * t_re - im * t_im).astype(BF16)
        out_im = (re * t_im + im * t_re).astype(BF16)
        for g in range(2):
            at = (g * SUB + c) * BLOCKS
            mid_ref[at : at + BLOCKS, :SPAN] = out_re[:, g * SPAN : (g + 1) * SPAN]
            mid_ref[at : at + BLOCKS, SPAN:] = out_im[:, g * SPAN : (g + 1) * SPAN]


CHUNK = 512


SLABS = 8


def filter_kernel(
    which, h_hbm, a_hbm, twist_hbm, forth_hbm, rest_hbm, swap_hbm, out_ref,
    slab_ref, a_ref, twist_ref, forth_ref, rest_ref, swap_ref, gather_ref, mid_ref, slab_sem, table_sem,
):
    lane_block = pl.multiple_of((which[0] // 4) * SPAN, SPAN)
    piece = LENGTH // SLABS
    slabs = [
        pltpu.make_async_copy(
            h_hbm.at[pl.ds(k * piece, piece), pl.ds(lane_block, SPAN)],
            slab_ref.at[pl.ds(k * piece, piece), :],
            slab_sem.at[k],
        )
        for k in range(SLABS)
    ]
    pairs = [(a_hbm, a_ref), (twist_hbm, twist_ref), (forth_hbm, forth_ref), (rest_hbm, rest_ref), (swap_hbm, swap_ref)]
    loads = [pltpu.make_async_copy(s, d, table_sem.at[k]) for k, (s, d) in enumerate(pairs)]
    for copy in slabs + loads:
        copy.start()
    offset = (which[0] % 4) * GROUP
    rows = lax.broadcasted_iota(jnp.int32, (GROUP, SPAN), 0)
    lanes = lax.broadcasted_iota(jnp.int32, (GROUP, SPAN), 1)
    pick = jnp.where(lanes == rows + offset, 1.0, 0.0).astype(BF16)
    for block in range(BLOCKS):
        if block % (BLOCKS // SLABS) == 0:
            slabs[block // (BLOCKS // SLABS)].wait()
        half, high, a = block // HALF, block // SUB % 2, block % SUB
        turned = lax.dot_general(
            pick, slab_ref[block * SPAN : (block + 1) * SPAN, :], (((1,), (1,)), ((), ())), preferred_element_type=F32
        ).astype(BF16)
        for g in range(2):
            lane = lane_of(half, high, g)
            gather_ref[a * SUB : (a + 1) * SUB, lane : lane + SPAN] = turned[g * SUB : (g + 1) * SUB]
    for copy in loads:
        copy.wait()
    swapped = dot(swap_ref[...], gather_ref[...]).astype(BF16)
    stage_a_rows(swapped, a_ref[...], twist_ref[...], mid_ref)
    for k in range(GROUP * BLOCKS // CHUNK):
        part = slice(k * CHUNK, (k + 1) * CHUNK)
        mid = mid_ref[part, :]
        out_ref[part, :] = (dot(mid, forth_ref[...]) + dot(mid, rest_ref[...])).astype(out_ref.dtype)


def conv_kernel(
    chunks, x_ref, spec_ref, a_ref, a_back_ref, twist_ref, forth_ref, back_ref, swap_ref, w_hbm,
    out_ref, w_ref, mid_ref, turn_ref, sem,
):
    rows, cols = w_ref.shape[0] // PARTS, w_ref.shape[1]
    start = pl.multiple_of(chunks[0] * cols, cols)

    def weight_copy(k):
        part = pl.ds(pl.multiple_of(k * rows, rows), rows)
        return pltpu.make_async_copy(w_hbm.at[part, pl.ds(start, cols)], w_ref.at[part, :], sem.at[k])

    def begin(k, carry):
        weight_copy(k).start()
        return carry

    lax.fori_loop(0, PARTS, begin, 0)
    copies = [weight_copy(k) for k in range(PARTS)]
    pieces = []
    for half in range(2):
        for high in range(2):
            for g in range(2):
                piece = x_ref[
                    high * SUB : (high + 1) * SUB, g * SUB : (g + 1) * SUB, half * SPAN : (half + 1) * SPAN
                ]
                pieces.append(piece.reshape(SUB * SUB, SPAN))
    swapped = dot(swap_ref[...], jnp.concatenate(pieces, 1)).astype(BF16)
    twist = twist_ref[...]
    stage_a_rows(swapped, a_ref[...], twist, mid_ref)
    t_re = jnp.concatenate([twist[:, :SPAN]] * (CHUNK // BLOCKS), 0)
    t_im = jnp.concatenate([twist[:, SPAN:]] * (CHUNK // BLOCKS), 0)
    for k in range(GROUP * BLOCKS // CHUNK):
        part = slice(k * CHUNK, (k + 1) * CHUNK)
        spec = dot(mid_ref[part, :], forth_ref[...])
        x_re, x_im = spec[:, :SPAN], spec[:, SPAN:]
        h = spec_ref[part, :].astype(F32)
        h_re, h_im = h[:, :SPAN], h[:, SPAN:]
        prod = jnp.concatenate([x_re * h_re - x_im * h_im, x_re * h_im + x_im * h_re], 1).astype(BF16)
        turn = dot(prod, back_ref[...])
        re, im = turn[:, :SPAN], turn[:, SPAN:]
        mid_ref[part, :SPAN] = (re * t_re + im * t_im).astype(BF16)
        mid_ref[part, SPAN:] = (im * t_re - re * t_im).astype(BF16)
    for c in range(SUB):
        sides = []
        for g in range(2):
            at = (g * SUB + c) * BLOCKS
            sides.append(
                jnp.concatenate([mid_ref[at : at + BLOCKS, :SPAN], mid_ref[at : at + BLOCKS, SPAN:]], 0)
            )
        y = dot(a_back_ref[...], jnp.concatenate(sides, 1)).astype(BF16)
        for k in range(4):
            turn_ref[c * SUB : (c + 1) * SUB, k * 2 * SPAN : (k + 1) * 2 * SPAN] = y[k * SUB : (k + 1) * SUB]
    result = dot(swap_ref[...], turn_ref[...]).astype(BF16)
    for half in range(2):
        for high in range(2):
            for g in range(2):
                lane = lane_of(half, high, g)
                out_ref[
                    high * SUB : (high + 1) * SUB, g * SUB : (g + 1) * SUB, half * SPAN : (half + 1) * SPAN
                ] = result[:, lane : lane + SPAN].reshape(SUB, SUB, SPAN)
    for copy in copies:
        copy.wait()


def in_hbm(*arrays):
    return tuple(pltpu.with_memory_space_constraint(a, pltpu.HBM) for a in arrays)


def filter_spectrum(which, long_filter, t):
    return pl.pallas_call(
        filter_kernel,
        out_shape=jax.ShapeDtypeStruct((GROUP * BLOCKS, 2 * SPAN), BF16),
        in_specs=[pl.BlockSpec(memory_space=pltpu.SMEM)] + [pl.BlockSpec(memory_space=pltpu.HBM)] * 6,
        out_specs=pl.BlockSpec(memory_space=pltpu.VMEM),
        scratch_shapes=[
            pltpu.VMEM((LENGTH, SPAN), BF16),
            pltpu.VMEM((2 * BLOCKS, 2 * BLOCKS), BF16),
            pltpu.VMEM((BLOCKS, 2 * SPAN), F32),
            pltpu.VMEM((2 * SPAN, 2 * SPAN), BF16),
            pltpu.VMEM((2 * SPAN, 2 * SPAN), BF16),
            pltpu.VMEM((SUB * SUB, SUB * SUB), BF16),
            pltpu.VMEM((SUB * SUB, 8 * SPAN), BF16),
            pltpu.VMEM((GROUP * BLOCKS, 2 * SPAN), BF16),
            pltpu.SemaphoreType.DMA((SLABS,)),
            pltpu.SemaphoreType.DMA((5,)),
        ],
        compiler_params=pltpu.CompilerParams(vmem_limit_bytes=32 << 20),
        name="filter_spectrum",
    )(which, *in_hbm(long_filter, t["a_filter"], t["twist"], t["forth"], t["forth_rest"], t["swap"]))


def convolve(chunks, x, spec, w, t):
    inner, cols = w.shape[0], w.shape[1] // 4
    vmem = pl.BlockSpec(memory_space=pltpu.VMEM)
    return pl.pallas_call(
        conv_kernel,
        out_shape=(pltpu.VMEM((HALF, GROUP, 2 * SPAN), BF16), pltpu.VMEM((inner, cols), BF16)),
        in_specs=[pl.BlockSpec(memory_space=pltpu.SMEM)] + [vmem] * 8 + [pl.BlockSpec(memory_space=pltpu.HBM)],
        out_specs=(vmem, vmem),
        scratch_shapes=[
            pltpu.VMEM((GROUP * BLOCKS, 2 * SPAN), BF16),
            pltpu.VMEM((SUB * SUB, 8 * SPAN), BF16),
            pltpu.SemaphoreType.DMA((PARTS,)),
        ],
        compiler_params=pltpu.CompilerParams(vmem_limit_bytes=32 << 20),
        name="convolve",
    )(
        chunks, x, spec, t["a_value"], t["a_back"], t["twist"], t["forth"], t["back"], t["swap"], *in_hbm(w)
    )


TURN = 2


def turn_kernel(v_hbm, out_hbm, in_ref, turned_ref, in_sem, out_sem):
    width = v_hbm.shape[1] // TURN
    loads = [
        pltpu.make_async_copy(v_hbm.at[:, pl.ds(k * width, width)], in_ref.at[k], in_sem.at[k]) for k in range(TURN)
    ]
    stores = [
        pltpu.make_async_copy(turned_ref.at[k], out_hbm.at[pl.ds(k * width, width), :], out_sem.at[k])
        for k in range(TURN)
    ]
    for load in loads:
        load.start()
    for k in range(TURN):
        loads[k].wait()
        turned_ref[k] = jnp.transpose(in_ref[k], (1, 0))
        stores[k].start()
    for store in stores:
        store.wait()


def turn(v):
    tokens, width = v.shape
    hbm = pl.BlockSpec(memory_space=pltpu.HBM)
    return pl.pallas_call(
        turn_kernel,
        out_shape=jax.ShapeDtypeStruct((width, tokens), BF16),
        in_specs=[hbm],
        out_specs=hbm,
        scratch_shapes=[
            pltpu.VMEM((TURN, tokens, width // TURN), BF16),
            pltpu.VMEM((TURN, width // TURN, tokens), BF16),
            pltpu.SemaphoreType.DMA((TURN,)),
            pltpu.SemaphoreType.DMA((TURN,)),
        ],
        compiler_params=pltpu.CompilerParams(vmem_limit_bytes=16 << 20),
        name="turn",
    )(*in_hbm(v))


PARTS = 4


def weight_copies(chunk, w_hbm, w_ref, sem):
    inner, cols = w_ref.shape
    rows = inner // PARTS
    start = pl.multiple_of(chunk * cols, cols)
    return [
        pltpu.make_async_copy(
            w_hbm.at[pl.ds(k * rows, rows), pl.ds(start, cols)], w_ref.at[pl.ds(k * rows, rows), :], sem.at[k]
        )
        for k in range(PARTS)
    ]


def product(mix_ref, w_ref, copies):
    rows = w_ref.shape[0] // PARTS
    total = None
    for k in range(PARTS):
        copies[k].wait()
        part = dot(mix_ref[:, k * rows : (k + 1) * rows], w_ref[k * rows : (k + 1) * rows, :])
        total = part if total is None else total + part
    return total


def gate_kernel(y_ref, gate_ref, w_ref, mix_ref, out_ref):
    rows = w_ref.shape[0] // PARTS
    total = None
    for k in range(PARTS):
        part = slice(k * rows, (k + 1) * rows)
        turned = jnp.transpose(y_ref[part, :], (1, 0))
        mix = (gate_ref[:, part].astype(F32) * turned.astype(F32)).astype(BF16)
        mix_ref[:, part] = mix
        product = dot(mix, w_ref[part, :])
        total = product if total is None else total + product
    out_ref[...] = total.astype(BF16)


def gate_project(y, gate, w):
    tokens, cols = gate.shape[0], w.shape[1]
    return pl.pallas_call(
        gate_kernel,
        out_shape=(jax.ShapeDtypeStruct(gate.shape, BF16), jax.ShapeDtypeStruct((tokens, cols), BF16)),
        compiler_params=pltpu.CompilerParams(vmem_limit_bytes=32 << 20),
        name="gate_project",
    )(y, gate, w)


def project(chunks, mix, w, targets):
    tokens, inner, cols = mix.shape[0], w.shape[0], w.shape[1] // 4
    count = 1 + max(j for j, _, _ in targets)
    pieces = [(j, dtype, k * tokens // n, tokens // n) for j, dtype, n in targets for k in range(n)]
    vmem = pl.BlockSpec(memory_space=pltpu.VMEM)

    def kernel(chunks, mix_ref, w_hbm, *refs):
        out_refs, (w_ref, sem) = refs[: len(pieces)], refs[len(pieces) :]
        copies = [weight_copies(chunks[j], w_hbm, w_ref.at[j], sem.at[j]) for j in range(count)]
        for copy in sum(copies, []):
            copy.start()
        for j in range(count):
            out = product(mix_ref, w_ref.at[j], copies[j])
            for (position, dtype, start, rows), out_ref in zip(pieces, out_refs):
                if position == j:
                    out_ref[...] = out[start : start + rows].astype(dtype)

    return pl.pallas_call(
        kernel,
        out_shape=tuple(jax.ShapeDtypeStruct((rows, cols), dtype) for _, dtype, _, rows in pieces),
        in_specs=[pl.BlockSpec(memory_space=pltpu.SMEM), vmem, pl.BlockSpec(memory_space=pltpu.HBM)],
        out_specs=(vmem,) * len(pieces),
        scratch_shapes=[pltpu.VMEM((count, inner, cols), BF16), pltpu.SemaphoreType.DMA((count, PARTS))],
        compiler_params=pltpu.CompilerParams(vmem_limit_bytes=32 << 20),
        name="project",
    )(chunks, mix, *in_hbm(w))


def finish(home, near, far):
    tokens, cols = home.shape
    rows = tokens // PARTS
    each = near[0].shape[0]

    def kernel(home_ref, *refs):
        near_refs, (far_ref, out_hbm, sum_ref, sem) = refs[: len(near)], refs[len(near) :]
        copies = []
        for k in range(PARTS):
            part = slice(k * rows, (k + 1) * rows)
            piece, first = divmod(k * rows, each)
            other = near_refs[piece][first : first + rows, :]
            total = home_ref[part, :] + other.astype(F32) + far_ref[part, :].astype(F32)
            sum_ref[part, :] = total.astype(BF16)
            copy = pltpu.make_async_copy(
                sum_ref.at[pl.ds(k * rows, rows), :], out_hbm.at[pl.ds(k * rows, rows), :], sem.at[k]
            )
            copy.start()
            copies.append(copy)
        for copy in copies:
            copy.wait()

    return pl.pallas_call(
        kernel,
        out_shape=jax.ShapeDtypeStruct(home.shape, BF16),
        in_specs=[pl.BlockSpec(memory_space=pltpu.VMEM)] * (2 + len(near)),
        out_specs=pl.BlockSpec(memory_space=pltpu.HBM),
        scratch_shapes=[pltpu.VMEM(home.shape, BF16), pltpu.SemaphoreType.DMA((PARTS,))],
        compiler_params=pltpu.CompilerParams(vmem_limit_bytes=16 << 20),
        name="finish",
    )(home, *near, far)


CORE_PAIR = [(0, 1), (1, 0), (2, 3), (3, 2)]
CHIP_PAIR = [(0, 2), (2, 0), (1, 3), (3, 1)]


def per_device(query_gate, gated_value, long_filter, out_weight):
    t = tables()
    me = lax.axis_index("ctx")
    mine = lax.axis_index("ch")
    tokens, width = gated_value.shape
    turned = turn(gated_value).reshape(HALF, GROUP, tokens)
    x = lax.all_to_all(turned, "ctx", 0, 0, tiled=True)
    spec = filter_spectrum(me.reshape(1), long_filter, t)
    y, w_first = convolve((mine ^ 3).reshape(1), x, spec, out_weight, t)
    y = lax.all_to_all(y, "ctx", 0, 0, tiled=True).reshape(width, tokens)
    mix, away_pair = gate_project(y, query_gate, w_first)
    away_in = lax.ppermute(away_pair, "ch", CORE_PAIR)
    (away_own,) = project((mine ^ 2).reshape(1), mix, out_weight, ((0, F32, 1),))
    away_sum = (away_own + away_in.astype(F32)).astype(BF16)
    mix, away_sum = lax.optimization_barrier((mix, away_sum))
    far = lax.ppermute(away_sum, "ch", CHIP_PAIR)
    *home_pair, home_own = project(jnp.stack([mine ^ 1, mine]), mix, out_weight, ((0, BF16, 2), (1, F32, 1)))
    near = [lax.ppermute(piece, "ch", CORE_PAIR) for piece in home_pair]
    return finish(home_own, near, far)


def solution(mesh):
    placed = (P("ctx", "ch"), P("ctx", "ch"), P(None, "ch"), P("ch", None))
    return jax.shard_map(
        per_device, mesh=mesh, in_specs=placed, out_specs=P("ctx", "ch"), check_vma=False
    )
```

```python
import functools

import jax
import jax.numpy as jnp
import ml_dtypes
import numpy as np
from jax import lax
from jax.experimental import pallas as pl
from jax.experimental.pallas import tpu as pltpu
from jax.sharding import PartitionSpec as P

SPAN = 128
BLOCKS = 64
HALF = BLOCKS // 2
LENGTH = SPAN * BLOCKS
GROUP = 32
SUB = 16
F32 = jnp.float32
BF16 = jnp.bfloat16


def tables():
    first = np.arange(BLOCKS)[:, None] + 0.25
    natural = np.arange(BLOCKS)[None, :]
    stored = np.concatenate([np.arange(HALF), BLOCKS - 1 - np.arange(HALF)])[None, :]

    def stage_a(order):
        angle = 2 * np.pi * first * order / BLOCKS
        return np.concatenate([np.cos(angle), -np.sin(angle)], 0)

    def stage_a_back(order):
        angle = (2 * np.pi * first * order / BLOCKS).T
        return np.concatenate([np.cos(angle), -np.sin(angle)], 1) / LENGTH

    twist = 2 * np.pi * first * np.arange(SPAN)[None, :] / LENGTH
    angle = 2 * np.pi * np.arange(SPAN)[:, None] * np.arange(SPAN)[None, :] / SPAN
    cos, sin = np.cos(angle), np.sin(angle)
    forth = np.block([[cos, -sin], [sin, cos]])
    back = np.block([[cos, sin], [-sin, cos]])
    rows = np.arange(SUB * SUB)
    swap = np.zeros((SUB * SUB, SUB * SUB))
    swap[(rows % SUB) * SUB + rows // SUB, rows] = 1.0
    bf = lambda a: a.astype(np.float32).astype(ml_dtypes.bfloat16)

    def two(a):
        high = bf(a)
        return high, bf(a - high.astype(np.float64))

    made = dict(
        a_filter=np.concatenate(two(stage_a(natural)), 1),
        a_value=bf(stage_a(stored)),
        a_back=bf(stage_a_back(stored)),
        twist=np.concatenate([np.cos(twist), -np.sin(twist)], 1).astype(np.float32),
        forth=bf(forth),
        forth_rest=two(forth)[1],
        back=bf(back),
        swap=bf(swap),
    )
    return {name: jnp.asarray(table) for name, table in made.items()}


def dot(left, right):
    return jnp.dot(left, right, preferred_element_type=F32)


def lane_of(half, high, g):
    return ((half * 2 + high) * 2 + g) * SPAN


def stage_a_rows(swapped, a_table, twist, mid_ref):
    t_re = jnp.concatenate([twist[:, :SPAN]] * 2, 1)
    t_im = jnp.concatenate([twist[:, SPAN:]] * 2, 1)
    for c in range(SUB):
        block = swapped[c * SUB : (c + 1) * SUB, :]
        rows = jnp.concatenate([block[:, k * 2 * SPAN : (k + 1) * 2 * SPAN] for k in range(4)], 0)
        if a_table.shape[1] > BLOCKS:
            rows = jnp.concatenate([rows, rows], 0)
        spec = dot(a_table, rows)
        re, im = spec[:BLOCKS], spec[BLOCKS:]
        out_re = (re * t_re - im * t_im).astype(BF16)
        out_im = (re * t_im + im * t_re).astype(BF16)
        for g in range(2):
            at = (g * SUB + c) * BLOCKS
            mid_ref[at : at + BLOCKS, :SPAN] = out_re[:, g * SPAN : (g + 1) * SPAN]
            mid_ref[at : at + BLOCKS, SPAN:] = out_im[:, g * SPAN : (g + 1) * SPAN]


CHUNK = 512


SLABS = 8


def filter_kernel(
    which, h_hbm, a_hbm, twist_hbm, forth_hbm, rest_hbm, swap_hbm, out_ref,
    slab_ref, a_ref, twist_ref, forth_ref, rest_ref, swap_ref, gather_ref, mid_ref, slab_sem, table_sem,
):
    lane_block = pl.multiple_of((which[0] // 4) * SPAN, SPAN)
    piece = LENGTH // SLABS
    slabs = [
        pltpu.make_async_copy(
            h_hbm.at[pl.ds(k * piece, piece), pl.ds(lane_block, SPAN)],
            slab_ref.at[pl.ds(k * piece, piece), :],
            slab_sem.at[k],
        )
        for k in range(SLABS)
    ]
    pairs = [(a_hbm, a_ref), (twist_hbm, twist_ref), (forth_hbm, forth_ref), (rest_hbm, rest_ref), (swap_hbm, swap_ref)]
    loads = [pltpu.make_async_copy(s, d, table_sem.at[k]) for k, (s, d) in enumerate(pairs)]
    for copy in slabs + loads:
        copy.start()
    offset = (which[0] % 4) * GROUP
    rows = lax.broadcasted_iota(jnp.int32, (GROUP, SPAN), 0)
    lanes = lax.broadcasted_iota(jnp.int32, (GROUP, SPAN), 1)
    pick = jnp.where(lanes == rows + offset, 1.0, 0.0).astype(BF16)
    for block in range(BLOCKS):
        if block % (BLOCKS // SLABS) == 0:
            slabs[block // (BLOCKS // SLABS)].wait()
        half, high, a = block // HALF, block // SUB % 2, block % SUB
        turned = lax.dot_general(
            pick, slab_ref[block * SPAN : (block + 1) * SPAN, :], (((1,), (1,)), ((), ())), preferred_element_type=F32
        ).astype(BF16)
        for g in range(2):
            lane = lane_of(half, high, g)
            gather_ref[a * SUB : (a + 1) * SUB, lane : lane + SPAN] = turned[g * SUB : (g + 1) * SUB]
    for copy in loads:
        copy.wait()
    swapped = dot(swap_ref[...], gather_ref[...]).astype(BF16)
    stage_a_rows(swapped, a_ref[...], twist_ref[...], mid_ref)
    for k in range(GROUP * BLOCKS // CHUNK):
        part = slice(k * CHUNK, (k + 1) * CHUNK)
        mid = mid_ref[part, :]
        out_ref[part, :] = (dot(mid, forth_ref[...]) + dot(mid, rest_ref[...])).astype(out_ref.dtype)


def conv_kernel(
    chunks, x_ref, spec_ref, a_ref, a_back_ref, twist_ref, forth_ref, back_ref, swap_ref, w_hbm,
    out_ref, w_ref, mid_ref, turn_ref, sem,
):
    rows, cols = w_ref.shape[0] // PARTS, w_ref.shape[1]
    start = pl.multiple_of(chunks[0] * cols, cols)

    def weight_copy(k):
        part = pl.ds(pl.multiple_of(k * rows, rows), rows)
        return pltpu.make_async_copy(w_hbm.at[part, pl.ds(start, cols)], w_ref.at[part, :], sem.at[k])

    def begin(k, carry):
        weight_copy(k).start()
        return carry

    lax.fori_loop(0, PARTS, begin, 0)
    copies = [weight_copy(k) for k in range(PARTS)]
    pieces = []
    for half in range(2):
        for high in range(2):
            for g in range(2):
                piece = x_ref[
                    high * SUB : (high + 1) * SUB, g * SUB : (g + 1) * SUB, half * SPAN : (half + 1) * SPAN
                ]
                pieces.append(piece.reshape(SUB * SUB, SPAN))
    swapped = dot(swap_ref[...], jnp.concatenate(pieces, 1)).astype(BF16)
    twist = twist_ref[...]
    stage_a_rows(swapped, a_ref[...], twist, mid_ref)
    t_re = jnp.concatenate([twist[:, :SPAN]] * (CHUNK // BLOCKS), 0)
    t_im = jnp.concatenate([twist[:, SPAN:]] * (CHUNK // BLOCKS), 0)
    for k in range(GROUP * BLOCKS // CHUNK):
        part = slice(k * CHUNK, (k + 1) * CHUNK)
        spec = dot(mid_ref[part, :], forth_ref[...])
        x_re, x_im = spec[:, :SPAN], spec[:, SPAN:]
        h = spec_ref[part, :].astype(F32)
        h_re, h_im = h[:, :SPAN], h[:, SPAN:]
        prod = jnp.concatenate([x_re * h_re - x_im * h_im, x_re * h_im + x_im * h_re], 1).astype(BF16)
        turn = dot(prod, back_ref[...])
        re, im = turn[:, :SPAN], turn[:, SPAN:]
        mid_ref[part, :SPAN] = (re * t_re + im * t_im).astype(BF16)
        mid_ref[part, SPAN:] = (im * t_re - re * t_im).astype(BF16)
    for c in range(SUB):
        sides = []
        for g in range(2):
            at = (g * SUB + c) * BLOCKS
            sides.append(
                jnp.concatenate([mid_ref[at : at + BLOCKS, :SPAN], mid_ref[at : at + BLOCKS, SPAN:]], 0)
            )
        y = dot(a_back_ref[...], jnp.concatenate(sides, 1)).astype(BF16)
        for k in range(4):
            turn_ref[c * SUB : (c + 1) * SUB, k * 2 * SPAN : (k + 1) * 2 * SPAN] = y[k * SUB : (k + 1) * SUB]
    result = dot(swap_ref[...], turn_ref[...]).astype(BF16)
    for half in range(2):
        for high in range(2):
            for g in range(2):
                lane = lane_of(half, high, g)
                out_ref[
                    high * SUB : (high + 1) * SUB, g * SUB : (g + 1) * SUB, half * SPAN : (half + 1) * SPAN
                ] = result[:, lane : lane + SPAN].reshape(SUB, SUB, SPAN)
    for copy in copies:
        copy.wait()


def in_hbm(*arrays):
    return tuple(pltpu.with_memory_space_constraint(a, pltpu.HBM) for a in arrays)


def filter_spectrum(which, long_filter, t):
    return pl.pallas_call(
        filter_kernel,
        out_shape=jax.ShapeDtypeStruct((GROUP * BLOCKS, 2 * SPAN), BF16),
        in_specs=[pl.BlockSpec(memory_space=pltpu.SMEM)] + [pl.BlockSpec(memory_space=pltpu.HBM)] * 6,
        out_specs=pl.BlockSpec(memory_space=pltpu.VMEM),
        scratch_shapes=[
            pltpu.VMEM((LENGTH, SPAN), BF16),
            pltpu.VMEM((2 * BLOCKS, 2 * BLOCKS), BF16),
            pltpu.VMEM((BLOCKS, 2 * SPAN), F32),
            pltpu.VMEM((2 * SPAN, 2 * SPAN), BF16),
            pltpu.VMEM((2 * SPAN, 2 * SPAN), BF16),
            pltpu.VMEM((SUB * SUB, SUB * SUB), BF16),
            pltpu.VMEM((SUB * SUB, 8 * SPAN), BF16),
            pltpu.VMEM((GROUP * BLOCKS, 2 * SPAN), BF16),
            pltpu.SemaphoreType.DMA((SLABS,)),
            pltpu.SemaphoreType.DMA((5,)),
        ],
        compiler_params=pltpu.CompilerParams(vmem_limit_bytes=32 << 20),
        name="filter_spectrum",
    )(which, *in_hbm(long_filter, t["a_filter"], t["twist"], t["forth"], t["forth_rest"], t["swap"]))


def convolve(chunks, x, spec, w, t):
    inner, cols = w.shape[0], w.shape[1] // 4
    vmem = pl.BlockSpec(memory_space=pltpu.VMEM)
    return pl.pallas_call(
        conv_kernel,
        out_shape=(pltpu.VMEM((HALF, GROUP, 2 * SPAN), BF16), pltpu.VMEM((inner, cols), BF16)),
        in_specs=[pl.BlockSpec(memory_space=pltpu.SMEM)] + [vmem] * 8 + [pl.BlockSpec(memory_space=pltpu.HBM)],
        out_specs=(vmem, vmem),
        scratch_shapes=[
            pltpu.VMEM((GROUP * BLOCKS, 2 * SPAN), BF16),
            pltpu.VMEM((SUB * SUB, 8 * SPAN), BF16),
            pltpu.SemaphoreType.DMA((PARTS,)),
        ],
        compiler_params=pltpu.CompilerParams(vmem_limit_bytes=32 << 20),
        name="convolve",
    )(
        chunks, x, spec, t["a_value"], t["a_back"], t["twist"], t["forth"], t["back"], t["swap"], *in_hbm(w)
    )


TURN = 2


def turn_kernel(v_hbm, out_hbm, in_ref, turned_ref, in_sem, out_sem):
    width = v_hbm.shape[1] // TURN
    loads = [
        pltpu.make_async_copy(v_hbm.at[:, pl.ds(k * width, width)], in_ref.at[k], in_sem.at[k]) for k in range(TURN)
    ]
    stores = [
        pltpu.make_async_copy(turned_ref.at[k], out_hbm.at[pl.ds(k * width, width), :], out_sem.at[k])
        for k in range(TURN)
    ]
    for load in loads:
        load.start()
    for k in range(TURN):
        loads[k].wait()
        turned_ref[k] = jnp.transpose(in_ref[k], (1, 0))
        stores[k].start()
    for store in stores:
        store.wait()


def turn(v):
    tokens, width = v.shape
    hbm = pl.BlockSpec(memory_space=pltpu.HBM)
    return pl.pallas_call(
        turn_kernel,
        out_shape=jax.ShapeDtypeStruct((width, tokens), BF16),
        in_specs=[hbm],
        out_specs=hbm,
        scratch_shapes=[
            pltpu.VMEM((TURN, tokens, width // TURN), BF16),
            pltpu.VMEM((TURN, width // TURN, tokens), BF16),
            pltpu.SemaphoreType.DMA((TURN,)),
            pltpu.SemaphoreType.DMA((TURN,)),
        ],
        compiler_params=pltpu.CompilerParams(vmem_limit_bytes=16 << 20),
        name="turn",
    )(*in_hbm(v))


PARTS = 4


def weight_copies(chunk, w_hbm, w_ref, sem):
    inner, cols = w_ref.shape
    rows = inner // PARTS
    start = pl.multiple_of(chunk * cols, cols)
    return [
        pltpu.make_async_copy(
            w_hbm.at[pl.ds(k * rows, rows), pl.ds(start, cols)], w_ref.at[pl.ds(k * rows, rows), :], sem.at[k]
        )
        for k in range(PARTS)
    ]


def product(mix_ref, w_ref, copies):
    rows = w_ref.shape[0] // PARTS
    total = None
    for k in range(PARTS):
        copies[k].wait()
        part = dot(mix_ref[:, k * rows : (k + 1) * rows], w_ref[k * rows : (k + 1) * rows, :])
        total = part if total is None else total + part
    return total


def gate_kernel(y_ref, gate_ref, w_ref, mix_ref, out_ref):
    rows = w_ref.shape[0] // PARTS
    total = None
    for k in range(PARTS):
        part = slice(k * rows, (k + 1) * rows)
        turned = jnp.transpose(y_ref[part, :], (1, 0))
        mix = (gate_ref[:, part].astype(F32) * turned.astype(F32)).astype(BF16)
        mix_ref[:, part] = mix
        product = dot(mix, w_ref[part, :])
        total = product if total is None else total + product
    out_ref[...] = total.astype(BF16)


def gate_project(y, gate, w):
    tokens, cols = gate.shape[0], w.shape[1]
    return pl.pallas_call(
        gate_kernel,
        out_shape=(jax.ShapeDtypeStruct(gate.shape, BF16), jax.ShapeDtypeStruct((tokens, cols), BF16)),
        compiler_params=pltpu.CompilerParams(vmem_limit_bytes=32 << 20),
        name="gate_project",
    )(y, gate, w)


def project(chunks, mix, w, targets):
    tokens, inner, cols = mix.shape[0], w.shape[0], w.shape[1] // 4
    count = 1 + max(j for j, _, _ in targets)
    pieces = [(j, dtype, k * tokens // n, tokens // n) for j, dtype, n in targets for k in range(n)]
    vmem = pl.BlockSpec(memory_space=pltpu.VMEM)

    def kernel(chunks, mix_ref, w_hbm, *refs):
        out_refs, (w_ref, sem) = refs[: len(pieces)], refs[len(pieces) :]
        copies = [weight_copies(chunks[j], w_hbm, w_ref.at[j], sem.at[j]) for j in range(count)]
        for copy in sum(copies, []):
            copy.start()
        for j in range(count):
            out = product(mix_ref, w_ref.at[j], copies[j])
            for (position, dtype, start, rows), out_ref in zip(pieces, out_refs):
                if position == j:
                    out_ref[...] = out[start : start + rows].astype(dtype)

    return pl.pallas_call(
        kernel,
        out_shape=tuple(jax.ShapeDtypeStruct((rows, cols), dtype) for _, dtype, _, rows in pieces),
        in_specs=[pl.BlockSpec(memory_space=pltpu.SMEM), vmem, pl.BlockSpec(memory_space=pltpu.HBM)],
        out_specs=(vmem,) * len(pieces),
        scratch_shapes=[pltpu.VMEM((count, inner, cols), BF16), pltpu.SemaphoreType.DMA((count, PARTS))],
        compiler_params=pltpu.CompilerParams(vmem_limit_bytes=32 << 20),
        name="project",
    )(chunks, mix, *in_hbm(w))


OUT_PARTS = 8


def finish(home, near, far):
    tokens, cols = home.shape
    rows = tokens // OUT_PARTS
    each = near[0].shape[0]

    def kernel(home_ref, *refs):
        near_refs, (far_ref, out_hbm, sum_ref, sem) = refs[: len(near)], refs[len(near) :]
        copies = []
        for k in range(OUT_PARTS):
            part = slice(k * rows, (k + 1) * rows)
            piece, first = divmod(k * rows, each)
            other = near_refs[piece][first : first + rows, :]
            total = home_ref[part, :] + other.astype(F32) + far_ref[part, :].astype(F32)
            sum_ref[part, :] = total.astype(BF16)
            copy = pltpu.make_async_copy(
                sum_ref.at[pl.ds(k * rows, rows), :], out_hbm.at[pl.ds(k * rows, rows), :], sem.at[k]
            )
            copy.start()
            copies.append(copy)
        for copy in copies:
            copy.wait()

    return pl.pallas_call(
        kernel,
        out_shape=jax.ShapeDtypeStruct(home.shape, BF16),
        in_specs=[pl.BlockSpec(memory_space=pltpu.VMEM)] * (2 + len(near)),
        out_specs=pl.BlockSpec(memory_space=pltpu.HBM),
        scratch_shapes=[pltpu.VMEM(home.shape, BF16), pltpu.SemaphoreType.DMA((OUT_PARTS,))],
        compiler_params=pltpu.CompilerParams(vmem_limit_bytes=16 << 20),
        name="finish",
    )(home, *near, far)


CORE_PAIR = [(0, 1), (1, 0), (2, 3), (3, 2)]
CHIP_PAIR = [(0, 2), (2, 0), (1, 3), (3, 1)]


def per_device(query_gate, gated_value, long_filter, out_weight):
    t = tables()
    me = lax.axis_index("ctx")
    mine = lax.axis_index("ch")
    tokens, width = gated_value.shape
    turned = turn(gated_value).reshape(HALF, GROUP, tokens)
    x = lax.all_to_all(turned, "ctx", 0, 0, tiled=True)
    spec = filter_spectrum(me.reshape(1), long_filter, t)
    y, w_first = convolve((mine ^ 3).reshape(1), x, spec, out_weight, t)
    y = lax.all_to_all(y, "ctx", 0, 0, tiled=True).reshape(width, tokens)
    mix, away_pair = gate_project(y, query_gate, w_first)
    away_in = lax.ppermute(away_pair, "ch", CORE_PAIR)
    (away_own,) = project((mine ^ 2).reshape(1), mix, out_weight, ((0, F32, 1),))
    away_sum = (away_own + away_in.astype(F32)).astype(BF16)
    mix, away_sum = lax.optimization_barrier((mix, away_sum))
    far = lax.ppermute(away_sum, "ch", CHIP_PAIR)
    *home_pair, home_own = project(jnp.stack([mine ^ 1, mine]), mix, out_weight, ((0, BF16, 2), (1, F32, 1)))
    near = [lax.ppermute(piece, "ch", CORE_PAIR) for piece in home_pair]
    return finish(home_own, near, far)


def solution(mesh):
    placed = (P("ctx", "ch"), P("ctx", "ch"), P(None, "ch"), P("ch", None))
    return jax.shard_map(
        per_device, mesh=mesh, in_specs=placed, out_specs=P("ctx", "ch"), check_vma=False
    )
```
